32 devices in a mesh: section: 4 (over y, core), dp: 2 (over x), mp: 4 (over z).
Axes of the slice: x: 2, y: 2, z: 4, core: 2. Of those that a mesh axis runs over, the one named last changes fastest.
Arguments:
- rollouts: bfloat16 [8, 256, 8192], P(('section', 'dp'), None, 'mp'), may hold values from -6 to 6
- lengths: int32 [8], replicated, may hold values from 1 to 256, 512 in all
- norm_gain: float32 [4, 8192], P('section'), may hold values from 0.5 to 12, as said below
- w_query: bfloat16 [4, 8192, 4096], P('section', 'dp', 'mp'), may hold values from -0.0625 to 0.0625
- w_keyval: bfloat16 [4, 8192, 2048], P('section', 'dp'), may hold values from -0.0625 to 0.0625
- out_head: float32 [4, 4096], P('section', 'mp'), may hold values from -0.25 to 0.25
- res_head: float32 [4, 8192], P('section', 'mp'), may hold values from -0.0625 to 0.0625
Outputs:
- scores: float32 [4, 8, 256], P(None, ('section', 'dp'))
The draws below stay inside these ranges and needn't reach their ends.
Inputs may be any that keep to these rules, and one draw needn't show every extreme that they name: The lengths sum to 512; the largest equals 256. `norm_gain`: positive gains.
All inputs are finite; a program needn't handle non-finite values.
Results may differ from the reference program's by a relative error of at most 0.005.
The reference program's roundings to bfloat16 on the way (of `normed`, `query`, `keyval` and `probs`) count: a program that leaves them out, or rounds other values in their place, can miss the bound.
Values may be sent and summed in bfloat16 or wider, within the bound.
A program may use at most 192 MiB of HBM per device.

```python
import math
import jax
import jax.numpy as jnp
import numpy as np
from jax import lax

D = 8192
HD = 128
KV = 8
HEADS = 32
LMAX = 256
MODELS = 4
ROLLOUTS = 8
TOTAL = 512


def draw_norm_gain(key, part):
    gains = jnp.exp(jax.random.uniform(key, (MODELS, D), jnp.float32, jnp.log(0.5), jnp.log(2.0)))
    return gains.astype(jnp.float32)


def level_of(stream_key, extent, split, low, top_value):
    def one(dim, parts):
        heights = jax.random.uniform(jax.random.fold_in(jax.random.fold_in(stream_key, 6), dim), (parts,), jnp.float32, low / len(split), top_value / len(split))
        return jnp.repeat(jnp.exp(heights), extent[dim] // parts).reshape((-1,) + (1,) * (len(extent) - dim - 1))

    factor_of = one(*split[0])
    for cut in split[1:]:
        factor_of = factor_of * one(*cut)
    return factor_of


def profile(amount, total, limit, lean):
    portions = [(1 << 20) // math.isqrt(rank ** lean) + 1 for rank in range(2, amount + 1)]
    spare, counts = total - limit - (amount - 1), [1] * (amount - 1)
    while spare > 0:
        free = [i for i in range(amount - 1) if counts[i] < limit]
        pool, budget = sum([portions[i] for i in free]), spare
        for i in free:
            more = min(limit - counts[i], max(1, budget * portions[i] // pool), spare)
            counts[i] = counts[i] + more
            spare = spare - more
    return np.array([limit] + counts)


def ragged(own_key, amount, total, bound, slope):
    if amount == 2:
        one = jax.random.randint(own_key, (), max(1, total - bound), min(bound, total - 1) + 1)
        return jnp.stack([one, total - one])
    sizes = jnp.asarray(profile(amount, total, bound, slope), jnp.int32)
    twos = (amount - 1) // 2
    giver, taker = sizes[1:1 + 2 * twos:2], sizes[2:2 + 2 * twos:2]
    margin = jnp.minimum(giver - 1, bound - taker)
    shifted = jax.random.randint(jax.random.fold_in(own_key, 1), (twos,), 0, 1 << 20) % (margin + 1)
    sizes = sizes.at[1:1 + 2 * twos:2].set(giver - shifted).at[2:2 + 2 * twos:2].set(taker + shifted)
    return sizes[jax.random.permutation(jax.random.fold_in(own_key, 2), amount)]


def noise(stream_key, extent, deviation, most, cuts=(), kind=jnp.bfloat16):
    values = deviation * jax.random.normal(stream_key, extent, jnp.float32)
    if cuts:
        values = values * level_of(stream_key, extent, cuts, -0.22, 0.18)
    return jnp.clip(values, -most, most).astype(kind)


def setup_inputs(seed: int = 0) -> dict:
    streams_of = jax.random.split(jax.random.key(seed), 8)
    return {
        "rollouts": noise(streams_of[0], (ROLLOUTS, LMAX, D), 1.0, 6.0, ((0, 8), (2, 4))),
        "lengths": ragged(streams_of[1], ROLLOUTS, TOTAL, LMAX, 2).astype(jnp.int32),
        "norm_gain": draw_norm_gain(jax.random.fold_in(streams_of[7], 71), 0),
        "w_query": noise(streams_of[3], (MODELS, D, HEADS * HD), D ** -0.5, 0.0625, ((0, 4), (1, 2), (2, 4))),
        "w_keyval": noise(streams_of[4], (MODELS, D, 2 * KV * HD), D ** -0.5, 0.0625, ((0, 4), (1, 2))),
        "out_head": noise(streams_of[5], (MODELS, HEADS * HD), (HEADS * HD // 9) ** -0.5, 0.25, ((0, 4), (1, 4)), jnp.float32),
        "res_head": noise(streams_of[6], (MODELS, D), D ** -0.5, 0.0625, ((0, 4), (1, 4)), jnp.float32),
    }


EPS = 1e-05

def one_model(rollouts, lengths, gain, w_query, w_keyval, out_head, res_head):
    xf = rollouts.astype(jnp.float32)
    meansq = lax.optimization_barrier(jnp.mean(xf * xf, axis=-1, keepdims=True))
    normed = (xf * lax.rsqrt(meansq + EPS) * gain).astype(jnp.bfloat16)
    flat = normed.reshape(ROLLOUTS * LMAX, D)
    query = jnp.dot(flat, w_query, preferred_element_type=jnp.float32).astype(jnp.bfloat16)
    keyval = jnp.dot(flat, w_keyval, preferred_element_type=jnp.float32).astype(jnp.bfloat16)
    query = query.reshape(ROLLOUTS, LMAX, HEADS, HD)
    keyval = keyval.reshape(ROLLOUTS, LMAX, KV, 2, HD)
    position = jnp.arange(LMAX, dtype=jnp.int32)
    scale = 1.0 / math.sqrt(HD)

    def attend(items):
        query_r, keyval_r, length, inputs_r = items
        keys = jnp.repeat(keyval_r[:, :, 0, :], HEADS // KV, axis=1).astype(jnp.float32)
        values = jnp.repeat(keyval_r[:, :, 1, :], HEADS // KV, axis=1).astype(jnp.float32)
        logits = jnp.einsum('qhd,khd->hqk', query_r.astype(jnp.float32), keys) * scale
        allowed = (position[None, :] <= position[:, None]) & (position[None, :] < length)
        logits = jnp.where(allowed[None], logits, -jnp.inf)
        top = lax.optimization_barrier(jnp.max(logits, axis=-1, keepdims=True))
        expo = jnp.exp(logits - top)
        probs = (expo / lax.optimization_barrier(jnp.sum(expo, axis=-1, keepdims=True))).astype(jnp.bfloat16)
        attended = jnp.einsum('hqk,khd->qhd', probs.astype(jnp.float32), values)
        head_term = lax.optimization_barrier(jnp.sum(attended.reshape(LMAX, HEADS * HD) * out_head, axis=-1))
        res_term = lax.optimization_barrier(jnp.sum(inputs_r.astype(jnp.float32) * res_head, axis=-1))
        total = head_term + res_term
        return jnp.where(position < length, total, jnp.zeros_like(total))
    return lax.map(attend, (query, keyval, lengths, rollouts))

def reference(rollouts, lengths, norm_gain, w_query, w_keyval, out_head, res_head):
    results = []
    for model in range(MODELS):
        results.append(one_model(rollouts, lengths, norm_gain[model], w_query[model], w_keyval[model], out_head[model], res_head[model]))
    return jnp.stack(results, axis=0)
```

```python
import functools
import math

import jax
import jax.numpy as jnp
from jax import lax
from jax.experimental import pallas as pl
from jax.experimental.pallas import tpu as pltpu
from jax.sharding import PartitionSpec as P

HD = 128
KV = 8
HEADS = 32
GROUP = HEADS // KV
EPS = 1e-05
CHUNKS = 8
OWN = ("section", "dp")


def coords(index, row_count, cols):
    return (index // (row_count * cols), index // cols % row_count, index % cols)


def share_kernel(sections, row_count, cols, part_ref, out_ref, held, send_sem, recv_sem):
    count = sections * row_count * cols
    me = (lax.axis_index("section") * row_count + lax.axis_index("dp")) * cols
    me = me + lax.axis_index("mp")
    barrier = pltpu.get_barrier_semaphore()

    def peer(step):
        return coords((me + step) % count, row_count, cols)

    def greet(step, carry):
        pl.semaphore_signal(
            barrier, inc=1, device_id=peer(step), device_id_type=pl.DeviceIdType.MESH
        )
        return carry

    lax.fori_loop(1, count, greet, 0)
    pl.semaphore_wait(barrier, count - 1)

    def copy(step):
        return pltpu.make_async_remote_copy(
            src_ref=part_ref,
            dst_ref=held.at[me],
            send_sem=send_sem.at[step],
            recv_sem=recv_sem.at[step],
            device_id=peer(step),
            device_id_type=pl.DeviceIdType.MESH,
        )

    def send(step, carry):
        copy(step).start()
        return carry

    def finish(step, carry):
        copy(step).wait()
        return carry

    lax.fori_loop(1, count, send, 0)
    held[me] = part_ref[...]
    lax.fori_loop(1, count, finish, 0)
    for section in range(sections):
        begin = section * row_count * cols
        out_ref[section] = jnp.sum(held[begin : begin + row_count * cols], axis=0)


def share(partial, sections, row_count, cols):
    rows = partial.shape[0] // 128
    count = sections * row_count * cols
    return pl.pallas_call(
        functools.partial(share_kernel, sections, row_count, cols),
        out_shape=jax.ShapeDtypeStruct((sections, rows, 128), jnp.float32),
        in_specs=[pl.BlockSpec(memory_space=pltpu.VMEM)],
        out_specs=pl.BlockSpec(memory_space=pltpu.VMEM),
        scratch_shapes=[
            pltpu.VMEM((count, rows, 128), jnp.float32),
            pltpu.SemaphoreType.DMA((count,)),
            pltpu.SemaphoreType.DMA((count,)),
        ],
        compiler_params=pltpu.CompilerParams(collective_id=0, has_side_effects=True),
    )(partial.reshape(rows, 128)).reshape(sections, rows * 128)


def spread_kernel(
    sections, row_count, cols, placed_ref, out_ref, stat_ref, sib, comb, got, allm, *sems
):
    pair_send, pair_recv, swap_send, swap_recv, col_send, col_recv = sems[:6]
    half_send, half_recv, stat_send, stat_recv, fwd_send, fwd_recv, fst_send, fst_recv = sems[6:]
    pairs, parts = sections // 2, cols // row_count
    sec, row, col = (lax.axis_index(name) for name in ("section", "dp", "mp"))
    par, pair = sec % 2, sec // 2
    sibling = (2 * pair + 1 - par, row, col)
    count = pairs * row_count

    def target(step):
        return (pair + step // row_count) % pairs, (row + step % row_count) % row_count

    def source(step):
        far = (pair + pairs - step // row_count) % pairs
        return (2 * far + par) * row_count + (row + row_count - step % row_count) % row_count

    def plane(step):
        far, line = target(step)
        return (2 * far + par, line, col)

    def column(step):
        return (sec, row, (col + step) % cols)

    def copy(src, dst, send_sem, recv_sem, device):
        return pltpu.make_async_remote_copy(
            src_ref=src,
            dst_ref=dst,
            send_sem=send_sem,
            recv_sem=recv_sem,
            device_id=device,
            device_id_type=pl.DeviceIdType.MESH,
        )

    barrier = pltpu.get_barrier_semaphore()
    others = [sibling]
    others += [plane(step) for step in range(1, count)]
    others += [column(step) for step in range(1, cols)]
    for device in others:
        pl.semaphore_signal(
            barrier, inc=1, device_id=device, device_id_type=pl.DeviceIdType.MESH
        )
    pl.semaphore_wait(barrier, len(others))

    to_pair = [
        copy(
            placed_ref.at[far, 1 - par], sib.at[far], pair_send.at[far], pair_recv.at[far], sibling
        )
        for far in range(pairs)
    ]
    for one in to_pair:
        one.start()
    for far in range(pairs):
        to_pair[far].wait_recv()
        comb[far] = placed_ref[far, par] + sib[far]

    chunks = 4
    high = allm.shape[1] // chunks
    spans = [pl.ds(chunk * high, high) for chunk in range(chunks)]
    place = pair * row_count + row
    me = sec * row_count + row
    swaps = [[] for _ in spans]
    gathers = [[] for _ in spans]
    halves = [[] for _ in spans]
    stats = [[] for _ in spans]
    forwards = []

    for chunk, span in enumerate(spans):
        for step in range(1, count):
            far, line = target(step)
            slot = chunk * count + step
            swaps[chunk].append(
                copy(
                    comb.at[far, line, span], got.at[place, span],
                    swap_send.at[slot], swap_recv.at[slot], plane(step),
                )
            )
            swaps[chunk][-1].start()
    got[place] = comb[pair, row]

    for chunk, span in enumerate(spans):
        for one in swaps[chunk]:
            one.wait_recv()
        total = got[0, span]
        for index in range(1, count):
            total = total + got[index, span]
        allm[col, span] = total
        for step in range(1, cols):
            slot = chunk * cols + step
            gathers[chunk].append(
                copy(
                    allm.at[col, span], allm.at[col, span],
                    col_send.at[slot], col_recv.at[slot], column(step),
                )
            )
            gathers[chunk][-1].start()

    for chunk, span in enumerate(spans):
        for one in gathers[chunk]:
            one.wait_recv()
        for step in range(1, count):
            far, line = target(step)
            slot = chunk * count + step
            halves[chunk].append(
                copy(
                    allm.at[pl.ds(line * parts, parts), span], out_ref.at[me, :, span],
                    half_send.at[slot], half_recv.at[slot], plane(step),
                )
            )
            halves[chunk][-1].start()
        out_ref[me, :, span] = allm[pl.ds(row * parts, parts), span]
        slot = chunk * count
        forwards.append(
            copy(
                out_ref.at[me, :, span], out_ref.at[me, :, span],
                fwd_send.at[slot], fwd_recv.at[slot], sibling,
            )
        )
        forwards[-1].start()
        square = jnp.zeros((high, 1), jnp.float32)
        for index in range(cols):
            values = allm[index, span].astype(jnp.float32)
            square += jnp.sum(values * values, axis=1, keepdims=True)
        square = square / (cols * allm.shape[2])
        stat_ref[me, span] = jnp.broadcast_to(square, (high, 128))
        for step in range(1, count):
            slot = chunk * count + step
            stats[chunk].append(
                copy(
                    stat_ref.at[me, span], stat_ref.at[me, span],
                    stat_send.at[slot], stat_recv.at[slot], plane(step),
                )
            )
            stats[chunk][-1].start()
        slot = chunk * count
        forwards.append(
            copy(
                stat_ref.at[me, span], stat_ref.at[me, span],
                fst_send.at[slot], fst_recv.at[slot], sibling,
            )
        )
        forwards[-1].start()
    for chunk, span in enumerate(spans):
        for step in range(1, count):
            origin = source(step)
            slot = chunk * count + step
            halves[chunk][step - 1].wait_recv()
            forwards.append(
                copy(
                    out_ref.at[origin, :, span], out_ref.at[origin, :, span],
                    fwd_send.at[slot], fwd_recv.at[slot], sibling,
                )
            )
            forwards[-1].start()
            stats[chunk][step - 1].wait_recv()
            forwards.append(
                copy(
                    stat_ref.at[origin, span], stat_ref.at[origin, span],
                    fst_send.at[slot], fst_recv.at[slot], sibling,
                )
            )
            forwards[-1].start()
    for one in forwards:
        one.wait()
    for one in to_pair + sum(swaps + gathers + halves + stats, []):
        one.wait_send()


def spread(placed, sections, row_count, cols):
    owners = sections * row_count
    rows, width = placed.shape[0] // owners, placed.shape[1]
    pairs, count = sections // 2, sections // 2 * row_count
    parts = cols // row_count
    sizes = [pairs] * 2 + [4 * count] * 2 + [4 * cols] * 2 + [4 * count] * 8
    return pl.pallas_call(
        functools.partial(spread_kernel, sections, row_count, cols),
        out_shape=(
            jax.ShapeDtypeStruct((owners, parts, rows, width), jnp.bfloat16),
            jax.ShapeDtypeStruct((owners, rows, 128), jnp.float32),
        ),
        in_specs=[pl.BlockSpec(memory_space=pltpu.VMEM)],
        out_specs=(
            pl.BlockSpec(memory_space=pltpu.VMEM),
            pl.BlockSpec(memory_space=pltpu.VMEM),
        ),
        scratch_shapes=[
            pltpu.VMEM((pairs, row_count, rows, width), jnp.bfloat16),
            pltpu.VMEM((pairs, row_count, rows, width), jnp.bfloat16),
            pltpu.VMEM((count, rows, width), jnp.bfloat16),
            pltpu.VMEM((cols, rows, width), jnp.bfloat16),
        ]
        + [pltpu.SemaphoreType.DMA((size,)) for size in sizes],
        compiler_params=pltpu.CompilerParams(
            collective_id=1, has_side_effects=True, vmem_limit_bytes=40 * 1024 * 1024
        ),
    )(placed.reshape(pairs, 2, row_count, rows, width))


def score_kernel(
    cols, heads, kvs, half_ref, meansq_ref, gain_ref, wq_ref, wkv_ref, seg_col_ref, seg_row_ref,
    head_ref, res_ref, out_ref, normed, weights, mine, sent, got, bias, w_sem, send_sem, recv_sem
):
    owners, parts, rows, width = half_ref.shape
    tokens = owners * rows
    sec, row, col = (lax.axis_index(name) for name in ("section", "dp", "mp"))
    peer = (sec, 1 - row, col)
    chunk = 2 * HD
    queries = heads * HD // chunk
    count = kvs + queries
    kv_first = col * 2 * heads // GROUP

    barrier = pltpu.get_barrier_semaphore()
    pl.semaphore_signal(barrier, inc=1, device_id=peer, device_id_type=pl.DeviceIdType.MESH)

    loads = []
    for turn, line in enumerate((1 - row, row)):
        for index in range(count):
            if index < kvs:
                begin, ref = (kv_first + line * kvs + index) * chunk, wkv_ref
            else:
                begin, ref = line * heads * HD + (index - kvs) * chunk, wq_ref
            slot = turn * count + index
            columns = pl.ds(pl.multiple_of(begin, chunk), chunk)
            loads.append(
                pltpu.make_async_copy(ref.at[0, :, columns], weights.at[slot], w_sem.at[slot])
            )
            loads[-1].start()

    def norm(owner, carry):
        scale = lax.rsqrt(meansq_ref[owner][:, :1] + EPS)
        spot = pl.ds(pl.multiple_of(owner * rows, rows), rows)
        for part in range(parts):
            values = half_ref[owner, part].astype(jnp.float32)
            normed[spot, part * width : (part + 1) * width] = (
                values * scale * gain_ref[row * parts + part]
            ).astype(jnp.bfloat16)
        return carry

    lax.fori_loop(0, owners, norm, 0)
    pl.semaphore_wait(barrier, 1)

    copies = []
    for index in range(count):
        loads[index].wait()
        sent[index] = jnp.dot(normed[...], weights[index], preferred_element_type=jnp.float32)
        copies.append(
            pltpu.make_async_remote_copy(
                src_ref=sent.at[index],
                dst_ref=got.at[index],
                send_sem=send_sem.at[index],
                recv_sem=recv_sem.at[index],
                device_id=peer,
                device_id_type=pl.DeviceIdType.MESH,
            )
        )
        copies[-1].start()
    for index in range(count):
        loads[count + index].wait()
        mine[index] = jnp.dot(
            normed[...], weights[count + index], preferred_element_type=jnp.float32
        )

    inner = col - row * parts
    held = jnp.where((inner >= 0) & (inner < parts), 1.0, 0.0).astype(jnp.float32)
    inner = jnp.clip(inner, 0, parts - 1)

    def residual(owner, carry):
        values = half_ref[owner, inner].astype(jnp.float32) * res_ref[...]
        lanes = values[:, :128]
        for group in range(1, width // 128):
            lanes = lanes + values[:, group * 128 : (group + 1) * 128]
        out_ref[pl.ds(pl.multiple_of(owner * rows, rows), rows), :] = lanes * held
        return carry

    lax.fori_loop(0, owners, residual, 0)
    ahead = lax.broadcasted_iota(jnp.int32, (tokens, tokens), 0) >= lax.broadcasted_iota(
        jnp.int32, (tokens, tokens), 1
    )
    allowed = (seg_col_ref[...] == seg_row_ref[...]) & ahead
    bias[...] = jnp.where(allowed, 0.0, -jnp.inf)

    keyval = []
    for index in range(kvs):
        copies[index].wait_recv()
        keyval.append((mine[index] + got[index]).astype(jnp.bfloat16))
    step = 256
    for index in range(queries):
        copies[kvs + index].wait_recv()
        query = (mine[kvs + index] + got[kvs + index]).astype(jnp.bfloat16)
        for inside in range(chunk // HD):
            head = index * (chunk // HD) + inside
            pair = keyval[head * kvs // heads]
            head_cols = head_ref[row, :, head * HD : (head + 1) * HD]
            for begin in range(0, tokens, step):
                end = begin + step
                logits = lax.dot_general(
                    query[begin:end, inside * HD : (inside + 1) * HD],
                    pair[:end, :HD],
                    (((1,), (1,)), ((), ())),
                    preferred_element_type=jnp.float32,
                ) * (1.0 / math.sqrt(HD))
                logits = logits + bias[begin:end, :end]
                expo = jnp.exp(logits - jnp.max(logits, axis=1, keepdims=True))
                probs = (expo / jnp.sum(expo, axis=1, keepdims=True)).astype(jnp.bfloat16)
                attended = jnp.dot(probs, pair[:end, HD:], preferred_element_type=jnp.float32)
                out_ref[begin:end, :] += attended * head_cols
    for one in copies:
        one.wait_send()


def score(half, meansq, gain, w_query, w_keyval, segment, out_head, res_head, heads, kvs):
    owners, parts, rows, width = half.shape
    tokens, depth = owners * rows, parts * width
    count = kvs + heads // 2
    vmem = pl.BlockSpec(memory_space=pltpu.VMEM)
    anyw = pl.BlockSpec(memory_space=pl.ANY)
    cols = gain.shape[0]
    return pl.pallas_call(
        functools.partial(score_kernel, cols, heads, kvs),
        out_shape=jax.ShapeDtypeStruct((tokens, 128), jnp.float32),
        in_specs=[vmem, vmem, vmem, anyw, anyw, vmem, vmem, vmem, vmem],
        out_specs=vmem,
        scratch_shapes=[
            pltpu.VMEM((tokens, depth), jnp.bfloat16),
            pltpu.VMEM((2 * count, depth, 2 * HD), jnp.bfloat16),
            pltpu.VMEM((count, tokens, 2 * HD), jnp.float32),
            pltpu.VMEM((count, tokens, 2 * HD), jnp.float32),
            pltpu.VMEM((count, tokens, 2 * HD), jnp.float32),
            pltpu.VMEM((tokens, tokens), jnp.float32),
            pltpu.SemaphoreType.DMA((2 * count,)),
            pltpu.SemaphoreType.DMA((count,)),
            pltpu.SemaphoreType.DMA((count,)),
        ],
        compiler_params=pltpu.CompilerParams(
            collective_id=2, has_side_effects=True, vmem_limit_bytes=50 * 1024 * 1024
        ),
    )(
        half, meansq, gain, w_query, w_keyval, segment[:, None], segment[None, :],
        out_head.reshape(2, 1, heads * HD), res_head,
    )


def fused_kernel(
    chunks, lengths_ref, x_any, gain_ref, wq_ref, wkv_ref, head_ref, res_ref, out_ref,
    x_ref, placed, sib, comb, yb, own, xb, full, normed, weights, sent, got, mine, keys, values,
    acc, scale, stat, stats, part, held, x_sem, w_sem, sib_send, sib_recv, y_send, y_recv,
    x_send, x_recv, z_send, z_recv, fy_send, fy_recv, fs_send, fs_recv, p_send, p_recv,
    stat_send, stat_recv, held_send, held_recv,
):
    sections, row_count, cols = 4, 2, 4
    count = sections * row_count * cols
    tokens, width = acc.shape[0], x_ref.shape[1]
    high = tokens // chunks
    rows = high // sections
    rolls = lengths_ref.shape[0]
    chunk = 2 * HD
    parts = weights.shape[0] // 2
    sec, row, col = (lax.axis_index(name) for name in ("section", "dp", "mp"))
    core, side = sec % 2, sec // 2
    me = (sec * row_count + row) * cols + col
    rank = jnp.where(row == 0, col, 3 - col)
    sibling = (2 * side + 1 - core, row, col)
    across = 2 * (1 - side) + core
    over_y = (across, row, col)
    over_x = (sec, 1 - row, col)

    def line(target):
        return (sec, row, jnp.where(row == 0, target, 3 - target))

    def half(origin):
        return jnp.where(row == 0, origin, 1 - origin)

    def copy(src, dst, send_sem, recv_sem, device):
        return pltpu.make_async_remote_copy(
            src_ref=src,
            dst_ref=dst,
            send_sem=send_sem,
            recv_sem=recv_sem,
            device_id=device,
            device_id_type=pl.DeviceIdType.MESH,
        )

    load = pltpu.make_async_copy(x_any, x_ref, x_sem)
    load.start()
    kv_first = col * 2
    loads = []
    for turn, where in enumerate((1 - row, row)):
        for index in range(parts):
            if index == 0:
                begin, ref = (kv_first + where) * chunk, wkv_ref
            else:
                begin, ref = where * GROUP * HD + (index - 1) * chunk, wq_ref
            slot = turn * parts + index
            columns = pl.ds(pl.multiple_of(begin, chunk), chunk)
            loads.append(
                pltpu.make_async_copy(ref.at[0, :, columns], weights.at[slot], w_sem.at[slot])
            )
            loads[-1].start()

    barrier = pltpu.get_barrier_semaphore()

    def peer(step):
        return coords((me + step) % count, row_count, cols)

    def greet(step, carry):
        pl.semaphore_signal(
            barrier, inc=1, device_id=peer(step), device_id_type=pl.DeviceIdType.MESH
        )
        return carry

    lax.fori_loop(1, count, greet, 0)

    owner = sec * row_count + row
    my_off, my_len, total = 0, 0, 0
    offsets = []
    for index in range(rolls):
        length = lengths_ref[index]
        offsets.append(total)
        total = total + length
        my_off = my_off + jnp.where(index < owner, length, 0)
        my_len = my_len + jnp.where(index == owner, length, 0)

    load.wait()
    limit = x_ref.shape[0]

    def place(begin):
        slots = begin + lax.broadcasted_iota(jnp.int32, (high, limit), 0)
        spots = lax.broadcasted_iota(jnp.int32, (high, limit), 1)
        hit = (slots == my_off + spots) & (spots < my_len)
        rows_here = jnp.dot(
            jnp.where(hit, 1.0, 0.0).astype(jnp.bfloat16), x_ref[...],
            preferred_element_type=jnp.float32,
        )
        return rows_here.astype(jnp.bfloat16).reshape(2, 2, rows, width)

    placed[0] = place(0)
    pl.semaphore_wait(barrier, count - 1)

    to_sib, to_y, to_x = [], [], []
    for c in range(chunks):
        if c:
            placed[c] = place(c * high)
        to_sib.append(
            copy(placed.at[c, :, 1 - core], sib.at[c], sib_send.at[c], sib_recv.at[c], sibling)
        )
        to_sib[-1].start()
        if c:
            reduce_pair(c - 1, to_sib, to_y, placed, sib, comb, yb, y_send, y_recv, core, side, over_y, copy)
    reduce_pair(chunks - 1, to_sib, to_y, placed, sib, comb, yb, y_send, y_recv, core, side, over_y, copy)

    early = rank <= 1
    mine_half = col % 2

    def z_copy(c, origin, target, slot):
        ref = full.at[c, half(origin), sec]
        return copy(ref, ref, z_send.at[c, slot], z_recv.at[c, origin], line(target))

    def fy_copy(c, origin, group):
        ref = full.at[c, half(origin), group]
        return copy(ref, ref, fy_send.at[c, origin], fy_recv.at[c, origin], over_y)

    def fs_copy(c, which, group):
        ref = full.at[c, :, group]
        return copy(ref, ref, fs_send.at[c, which], fs_recv.at[c, which], sibling)

    def gather_own(c):
        to_y[c].wait_recv()
        own[c] = comb[c, side] + yb[c]
        to_x.append(copy(own.at[c], xb.at[c], x_send.at[c], x_recv.at[c], over_x))

        @pl.when(rank >= 2)
        def _():
            to_x[c].start()

    def land(c):
        @pl.when(early)
        def _():
            to_x[c].wait_recv()
            full[c, mine_half, sec] = own[c] + xb[c]

        @pl.when(rank == 0)
        def _():
            z_copy(c, 0, 1, 0).start()
            fy_copy(c, 0, sec).start()

        @pl.when(rank == 1)
        def _():
            z_copy(c, 1, 2, 0).start()
            z_copy(c, 1, 0, 1).start()
            fy_copy(c, 1, sec).start()

    def pass_on(c):
        for origin in (1, 0):
            @pl.when(rank != origin)
            def _():
                z_copy(c, origin, origin, 0).wait_recv()
                fy_copy(c, origin, sec).start()

            if origin == 0:
                @pl.when(rank == 1)
                def _():
                    z_copy(c, 0, 2, 2).start()

            @pl.when(rank == 2)
            def _():
                z_copy(c, origin, 3, origin).start()
        fs_copy(c, 0, sec).start()

    def to_both(c):
        for origin in (1, 0):
            fy_copy(c, origin, across).wait_recv()
        fs_copy(c, 1, across).start()

    gather_own(0)
    for c in range(1, chunks):
        gather_own(c)
        land(c - 1)

    blocks = tokens // 128
    lane_blocks = placed.shape[0] // blocks

    for block in range(blocks):
        seen = placed[block * lane_blocks : (block + 1) * lane_blocks].reshape(128, width)
        square = jnp.zeros((128, 128), jnp.float32)
        for group in range(width // 128):
            piece = seen[:, group * 128 : (group + 1) * 128].astype(jnp.float32)
            square = square + piece * piece
        stat[block : block + 1] = jnp.sum(jnp.transpose(square), axis=0, keepdims=True)

    def everyone(src, dst, send_sem, recv_sem):
        def one(step):
            return copy(src, dst.at[me], send_sem.at[step], recv_sem.at[step], peer(step))

        def send(step, carry):
            one(step).start()
            return carry

        def finish(step, carry):
            one(step).wait()
            return carry

        return (
            lambda: lax.fori_loop(1, count, send, 0),
            lambda: lax.fori_loop(1, count, finish, 0),
        )

    send_stats, finish_stats = everyone(stat, stats, stat_send, stat_recv)
    send_stats()
    stats[me] = stat[...]
    land(chunks - 1)

    keys[...] = jnp.zeros_like(keys)
    values[...] = jnp.zeros_like(values)

    def ready():
        finish_stats()
        mean = jnp.sum(stats[...], axis=0) / (cols * width)
        factor = lax.rsqrt(mean + EPS)
        for block in range(blocks):
            wide = jnp.broadcast_to(factor[block : block + 1], (128, 128))
            scale[block * 128 : (block + 1) * 128] = jnp.transpose(wide)

    def exchange(c):
        return copy(sent.at[c], got.at[c], p_send.at[c], p_recv.at[c], over_x)

    def project(c):
        for which, group in ((0, 2 * side + 1 - core), (1, 2 * (1 - side) + 1 - core)):
            fs_copy(c, which, group).wait_recv()
        here = slice(c * high, (c + 1) * high)
        factor = scale[here, :1]
        for part_index in range(2):
            piece = full[c, part_index].reshape(high, width).astype(jnp.float32)
            normed[:, part_index * width : (part_index + 1) * width] = (
                piece * factor * gain_ref[row * 2 + part_index]
            ).astype(jnp.bfloat16)
        for index in range(parts):
            if c == 0:
                loads[index].wait()
            sent[c, index] = jnp.dot(
                normed[...], weights[index], preferred_element_type=jnp.float32
            )
        exchange(c).start()
        for index in range(parts):
            if c == 0:
                loads[parts + index].wait()
            mine[c, index] = jnp.dot(
                normed[...], weights[parts + index], preferred_element_type=jnp.float32
            )

        acc[here] = jnp.zeros((high, 128), jnp.float32)

        @pl.when(early)
        def _():
            piece = full[c, mine_half].reshape(high, width).astype(jnp.float32) * res_ref[...]
            lanes = piece[:, :128]
            for group in range(1, width // 128):
                lanes = lanes + piece[:, group * 128 : (group + 1) * 128]
            acc[here] = lanes

    def attend(c):
        here = slice(c * high, (c + 1) * high)
        end = -(-(c + 1) * high // 128) * 128
        exchange(c).wait_recv()
        pair = (mine[c, 0] + got[c, 0]).astype(jnp.bfloat16)
        keys[here] = pair[:, :HD]
        values[here] = pair[:, HD:]
        heads = []
        for index in range(1, parts):
            both = (mine[c, index] + got[c, index]).astype(jnp.bfloat16)
            heads += [both[:, :HD], both[:, HD:]]
        query = jnp.concatenate(heads, axis=0)
        logits = lax.dot_general(
            query, keys[:end], (((1,), (1,)), ((), ())), preferred_element_type=jnp.float32
        ) * (1.0 / math.sqrt(HD))
        slots = c * high + lax.broadcasted_iota(jnp.int32, (high, end), 0)
        spots = lax.broadcasted_iota(jnp.int32, (high, end), 1)
        start = jnp.zeros((high, end), jnp.int32)
        for offset in offsets[1:]:
            start = jnp.where(slots >= offset, offset, start)
        allowed = (spots >= start) & (spots <= slots)
        bias = jnp.where(allowed, 0.0, -jnp.inf)
        logits = logits + jnp.concatenate([bias] * len(heads), axis=0)
        expo = jnp.exp(logits - jnp.max(logits, axis=1, keepdims=True))
        probs = (expo / jnp.sum(expo, axis=1, keepdims=True)).astype(jnp.bfloat16)
        attended = jnp.dot(probs, values[:end], preferred_element_type=jnp.float32)
        lanes = acc[here]
        for head in range(len(heads)):
            lanes = lanes + attended[head * high : (head + 1) * high] * head_ref[
                row, :, head * HD : (head + 1) * HD
            ]
        acc[here] = lanes

    steps = []
    for k in range(chunks + 5):
        if k < chunks:
            pass_on(k)
        if 0 <= k - 1 < chunks:
            to_both(k - 1)
        if k == 2:
            ready()
        if 0 <= k - 2 < chunks:
            project(k - 2)
        if 0 <= k - 4 < chunks:
            attend(k - 4)

    for block in range(blocks):
        lanes = acc[block * 128 : (block + 1) * 128]
        part[block : block + 1] = jnp.sum(jnp.transpose(lanes), axis=0, keepdims=True)
    send_part, finish_part = everyone(part, held, held_send, held_recv)
    send_part()
    held[me] = part[...]

    for c in range(chunks):
        to_sib[c].wait_send()
        to_y[c].wait_send()

        @pl.when(rank >= 2)
        def _():
            to_x[c].wait_send()

        for origin in range(2):
            fy_copy(c, origin, sec).wait_send()
        fs_copy(c, 0, sec).wait_send()
        fs_copy(c, 1, across).wait_send()
        exchange(c).wait_send()

        @pl.when(rank == 0)
        def _():
            z_copy(c, 0, 1, 0).wait_send()

        @pl.when(rank == 1)
        def _():
            z_copy(c, 1, 2, 0).wait_send()
            z_copy(c, 1, 0, 1).wait_send()
            z_copy(c, 0, 2, 2).wait_send()

        @pl.when(rank == 2)
        def _():
            z_copy(c, 1, 3, 1).wait_send()
            z_copy(c, 0, 3, 0).wait_send()

    finish_part()
    spots = lax.broadcasted_iota(jnp.int32, (128, limit), 1)
    totals = []
    for section in range(sections):
        begin = section * row_count * cols
        totals.append(jnp.sum(held[begin : begin + row_count * cols], axis=0))
    result = jnp.zeros((sections, limit), jnp.float32)
    for block in range(blocks):
        slots = block * 128 + lax.broadcasted_iota(jnp.int32, (128, limit), 0)
        hit = (slots == my_off + spots) & (spots < my_len)
        picked = jnp.concatenate([one[block : block + 1] for one in totals], axis=0)
        result = result + jnp.dot(
            picked, jnp.where(hit, 1.0, 0.0), preferred_element_type=jnp.float32,
            precision=lax.Precision.HIGHEST,
        )
    out_ref[...] = result


def reduce_pair(c, to_sib, to_y, placed, sib, comb, yb, y_send, y_recv, core, side, over_y, copy):
    to_sib[c].wait_recv()
    comb[c] = placed[c, :, core] + sib[c]
    to_y.append(copy(comb.at[c, 1 - side], yb.at[c], y_send.at[c], y_recv.at[c], over_y))
    to_y[-1].start()


def fused(rollouts, lengths, gain, w_query, w_keyval, out_head, res_head, chunks):
    limit, width = rollouts.shape[1:]
    depth = w_query.shape[1]
    tokens = lengths.shape[0] * limit // 4
    high = tokens // chunks
    rows = high // 4
    vmem = pl.BlockSpec(memory_space=pltpu.VMEM)
    anyw = pl.BlockSpec(memory_space=pl.ANY)
    smem = pl.BlockSpec(memory_space=pltpu.SMEM)
    bf16, f32, dma = jnp.bfloat16, jnp.float32, pltpu.SemaphoreType.DMA
    parts = 3
    sems = [(chunks,)] * 6 + [(chunks, 3)] + [(chunks, 2)] * 5 + [(chunks,)] * 2 + [(32,)] * 4
    out = pl.pallas_call(
        functools.partial(fused_kernel, chunks),
        out_shape=jax.ShapeDtypeStruct((4, limit), f32),
        in_specs=[smem, anyw, vmem, anyw, anyw, vmem, vmem],
        out_specs=vmem,
        scratch_shapes=[
            pltpu.VMEM((limit, width), bf16),
            pltpu.VMEM((chunks, 2, 2, rows, width), bf16),
            pltpu.VMEM((chunks, 2, rows, width), bf16),
            pltpu.VMEM((chunks, 2, rows, width), bf16),
            pltpu.VMEM((chunks, rows, width), bf16),
            pltpu.VMEM((chunks, rows, width), bf16),
            pltpu.VMEM((chunks, rows, width), bf16),
            pltpu.VMEM((chunks, 2, 4, rows, width), bf16),
            pltpu.VMEM((high, depth), bf16),
            pltpu.VMEM((2 * parts, depth, 2 * HD), bf16),
            pltpu.VMEM((chunks, parts, high, 2 * HD), f32),
            pltpu.VMEM((chunks, parts, high, 2 * HD), f32),
            pltpu.VMEM((chunks, parts, high, 2 * HD), f32),
            pltpu.VMEM((tokens, HD), bf16),
            pltpu.VMEM((tokens, HD), bf16),
            pltpu.VMEM((tokens, 128), f32),
            pltpu.VMEM((tokens, 128), f32),
            pltpu.VMEM((tokens // 128, 128), f32),
            pltpu.VMEM((32, tokens // 128, 128), f32),
            pltpu.VMEM((tokens // 128, 128), f32),
            pltpu.VMEM((32, tokens // 128, 128), f32),
            dma,
            dma((2 * parts,)),
        ]
        + [dma(size) for size in sems],
        compiler_params=pltpu.CompilerParams(
            collective_id=3, has_side_effects=True, vmem_limit_bytes=48 * 1024 * 1024
        ),
    )(
        lengths, rollouts.reshape(limit, width), gain, w_query, w_keyval,
        out_head.reshape(2, 1, GROUP * HD), res_head,
    )
    return out.reshape(4, 1, limit)


def plain(half, meansq, gains, w_query, w_keyval, segment, out_head, res_head):
    owners, _, rows, local_width = half.shape
    tokens = owners * rows
    row_count, cols = lax.axis_size("dp"), lax.axis_size("mp")
    my_row, my_col = lax.axis_index("dp"), lax.axis_index("mp")
    slots = jnp.arange(tokens, dtype=jnp.int32)
    scale_row = lax.rsqrt(meansq[:, None, :, :1] + EPS)
    parts = cols // row_count
    gain = lax.dynamic_slice_in_dim(gains, my_row * parts, parts, 0)
    normed = (half.astype(jnp.float32) * scale_row * gain[None]).astype(jnp.bfloat16)

    heads_here = w_query.shape[2] // HD
    kv_here = max(1, heads_here // GROUP)
    kv_first = my_col * heads_here // GROUP
    w_kv = lax.dynamic_slice_in_dim(w_keyval[0], kv_first * 2 * HD, kv_here * 2 * HD, 1)
    q_part, kv_part = 0.0, 0.0
    for part in range(parts):
        rows = normed[:, part].reshape(tokens, local_width)
        begin = part * local_width
        end = begin + local_width
        q_part += jnp.dot(rows, w_query[0, begin:end], preferred_element_type=jnp.float32)
        kv_part += jnp.dot(rows, w_kv[begin:end], preferred_element_type=jnp.float32)
    heads, kvs = heads_here, kv_here
    summed = lax.psum(jnp.concatenate([q_part, kv_part], axis=1), "dp")
    head_cols = out_head[0]
    weight = (my_row == 0).astype(jnp.float32)
    summed = summed.astype(jnp.bfloat16)
    query = summed[:, : heads * HD].reshape(tokens, kvs, heads // kvs, HD)
    keyval = summed[:, heads * HD :].reshape(tokens, kvs, 2, HD)
    logits = jnp.einsum(
        "qkgd,skd->kgqs", query, keyval[:, :, 0, :], preferred_element_type=jnp.float32
    ) * (1.0 / math.sqrt(HD))
    allowed = (segment[:, None] == segment[None, :]) & (slots[None, :] <= slots[:, None])
    logits = jnp.where(allowed, logits, -jnp.inf)
    expo = jnp.exp(logits - jnp.max(logits, axis=-1, keepdims=True))
    probs = (expo / jnp.sum(expo, axis=-1, keepdims=True)).astype(jnp.bfloat16)
    attended = jnp.einsum(
        "kgqs,skd->qkgd", probs, keyval[:, :, 1, :], preferred_element_type=jnp.float32
    ).reshape(tokens, heads * HD)
    inner = my_col - my_row * parts
    res_in = lax.dynamic_index_in_dim(half, jnp.clip(inner, 0, parts - 1), 1, keepdims=False)
    res_sum = jnp.sum(
        res_in.reshape(tokens, local_width).astype(jnp.float32) * res_head[0][None, :], axis=1
    )
    res_sum = jnp.where((inner >= 0) & (inner < parts), res_sum, 0.0)
    return weight * jnp.sum(attended * head_cols[None, :], axis=1) + res_sum


def body(rollouts, lengths, norm_gain, w_query, w_keyval, out_head, res_head):
    roll_count, max_len, local_width = rollouts.shape
    sections, row_count, cols = (lax.axis_size(name) for name in ("section", "dp", "mp"))
    if (sections, row_count, cols, roll_count) == (4, 2, 4, 1) and w_query.shape[2] == 8 * HD:
        gains = norm_gain[0].reshape(cols, 1, local_width)
        return fused(rollouts, lengths, gains, w_query, w_keyval, out_head, res_head, CHUNKS)
    owner = lax.axis_index(OWN)
    total_rolls = lengths.shape[0]
    tokens = total_rolls * max_len // 4

    ids = jnp.arange(total_rolls, dtype=jnp.int32)
    offsets = jnp.sum(jnp.where(ids[None, :] < ids[:, None], lengths[None, :], 0), axis=1)
    slots = jnp.arange(tokens, dtype=jnp.int32)
    segment = jnp.sum((slots[:, None] >= offsets[None, :]).astype(jnp.int32), axis=1)

    position = jnp.arange(max_len, dtype=jnp.int32)
    mine = owner * roll_count + jnp.arange(roll_count, dtype=jnp.int32)
    my_off = jnp.sum(jnp.where(ids[None, :] == mine[:, None], offsets[None, :], 0), axis=1)
    my_len = jnp.sum(jnp.where(ids[None, :] == mine[:, None], lengths[None, :], 0), axis=1)
    place = (
        (slots[:, None, None] == my_off[None, :, None] + position[None, None, :])
        & (position[None, None, :] < my_len[None, :, None])
    ).astype(jnp.bfloat16)
    placed = jnp.dot(
        place.reshape(tokens, roll_count * max_len),
        rollouts.reshape(roll_count * max_len, local_width),
        preferred_element_type=jnp.float32,
    ).astype(jnp.bfloat16)
    half, meansq = spread(placed, sections, row_count, cols)
    heads_here = w_query.shape[2] // HD
    gains = norm_gain[0].reshape(cols, 1, local_width)
    if row_count == 2 and heads_here % (2 * GROUP) == 0 and tokens % 256 == 0:
        lanes = score(
            half, meansq, gains, w_query, w_keyval, segment, out_head, res_head,
            heads_here // 2, heads_here // 2 // GROUP,
        )
        partial = jnp.sum(lanes, axis=1)
    else:
        partial = plain(
            half, meansq, gains, w_query, w_keyval, segment, out_head, res_head
        )
    home = share(partial, sections, row_count, cols)
    home = jnp.pad(home, ((0, 0), (0, max_len)))
    lines = []
    for local in range(roll_count):
        line = lax.dynamic_slice_in_dim(home, my_off[local], max_len, 1)
        lines.append(jnp.where(position[None, :] < my_len[local], line, 0.0))
    return jnp.stack(lines, axis=1)


def solution(mesh):
    in_specs = (
        P(("section", "dp"), None, "mp"),
        P(),
        P("section", None),
        P("section", "dp", "mp"),
        P("section", "dp", None),
        P("section", "mp"),
        P("section", "mp"),
    )
    out_specs = P(None, ("section", "dp"), None)
    return jax.shard_map(body, mesh=mesh, in_specs=in_specs, out_specs=out_specs, check_vma=False)
```

```python
import functools
import math

import jax
import jax.numpy as jnp
from jax import lax
from jax.experimental import pallas as pl
from jax.experimental.pallas import tpu as pltpu
from jax.sharding import PartitionSpec as P

HD = 128
KV = 8
HEADS = 32
GROUP = HEADS // KV
EPS = 1e-05
CHUNKS = 8
OWN = ("section", "dp")


def coords(index, row_count, cols):
    return (index // (row_count * cols), index // cols % row_count, index % cols)


def share_kernel(sections, row_count, cols, part_ref, out_ref, held, send_sem, recv_sem):
    count = sections * row_count * cols
    me = (lax.axis_index("section") * row_count + lax.axis_index("dp")) * cols
    me = me + lax.axis_index("mp")
    barrier = pltpu.get_barrier_semaphore()

    def peer(step):
        return coords((me + step) % count, row_count, cols)

    def greet(step, carry):
        pl.semaphore_signal(
            barrier, inc=1, device_id=peer(step), device_id_type=pl.DeviceIdType.MESH
        )
        return carry

    lax.fori_loop(1, count, greet, 0)
    pl.semaphore_wait(barrier, count - 1)

    def copy(step):
        return pltpu.make_async_remote_copy(
            src_ref=part_ref,
            dst_ref=held.at[me],
            send_sem=send_sem.at[step],
            recv_sem=recv_sem.at[step],
            device_id=peer(step),
            device_id_type=pl.DeviceIdType.MESH,
        )

    def send(step, carry):
        copy(step).start()
        return carry

    def finish(step, carry):
        copy(step).wait()
        return carry

    lax.fori_loop(1, count, send, 0)
    held[me] = part_ref[...]
    lax.fori_loop(1, count, finish, 0)
    for section in range(sections):
        begin = section * row_count * cols
        out_ref[section] = jnp.sum(held[begin : begin + row_count * cols], axis=0)


def share(partial, sections, row_count, cols):
    rows = partial.shape[0] // 128
    count = sections * row_count * cols
    return pl.pallas_call(
        functools.partial(share_kernel, sections, row_count, cols),
        out_shape=jax.ShapeDtypeStruct((sections, rows, 128), jnp.float32),
        in_specs=[pl.BlockSpec(memory_space=pltpu.VMEM)],
        out_specs=pl.BlockSpec(memory_space=pltpu.VMEM),
        scratch_shapes=[
            pltpu.VMEM((count, rows, 128), jnp.float32),
            pltpu.SemaphoreType.DMA((count,)),
            pltpu.SemaphoreType.DMA((count,)),
        ],
        compiler_params=pltpu.CompilerParams(collective_id=0, has_side_effects=True),
    )(partial.reshape(rows, 128)).reshape(sections, rows * 128)


def spread_kernel(
    sections, row_count, cols, placed_ref, out_ref, stat_ref, sib, comb, got, allm, *sems
):
    pair_send, pair_recv, swap_send, swap_recv, col_send, col_recv = sems[:6]
    half_send, half_recv, stat_send, stat_recv, fwd_send, fwd_recv, fst_send, fst_recv = sems[6:]
    pairs, parts = sections // 2, cols // row_count
    sec, row, col = (lax.axis_index(name) for name in ("section", "dp", "mp"))
    par, pair = sec % 2, sec // 2
    sibling = (2 * pair + 1 - par, row, col)
    count = pairs * row_count

    def target(step):
        return (pair + step // row_count) % pairs, (row + step % row_count) % row_count

    def source(step):
        far = (pair + pairs - step // row_count) % pairs
        return (2 * far + par) * row_count + (row + row_count - step % row_count) % row_count

    def plane(step):
        far, line = target(step)
        return (2 * far + par, line, col)

    def column(step):
        return (sec, row, (col + step) % cols)

    def copy(src, dst, send_sem, recv_sem, device):
        return pltpu.make_async_remote_copy(
            src_ref=src,
            dst_ref=dst,
            send_sem=send_sem,
            recv_sem=recv_sem,
            device_id=device,
            device_id_type=pl.DeviceIdType.MESH,
        )

    barrier = pltpu.get_barrier_semaphore()
    others = [sibling]
    others += [plane(step) for step in range(1, count)]
    others += [column(step) for step in range(1, cols)]
    for device in others:
        pl.semaphore_signal(
            barrier, inc=1, device_id=device, device_id_type=pl.DeviceIdType.MESH
        )
    pl.semaphore_wait(barrier, len(others))

    to_pair = [
        copy(
            placed_ref.at[far, 1 - par], sib.at[far], pair_send.at[far], pair_recv.at[far], sibling
        )
        for far in range(pairs)
    ]
    for one in to_pair:
        one.start()
    for far in range(pairs):
        to_pair[far].wait_recv()
        comb[far] = placed_ref[far, par] + sib[far]

    chunks = 4
    high = allm.shape[1] // chunks
    spans = [pl.ds(chunk * high, high) for chunk in range(chunks)]
    place = pair * row_count + row
    me = sec * row_count + row
    swaps = [[] for _ in spans]
    gathers = [[] for _ in spans]
    halves = [[] for _ in spans]
    stats = [[] for _ in spans]
    forwards = []

    for chunk, span in enumerate(spans):
        for step in range(1, count):
            far, line = target(step)
            slot = chunk * count + step
            swaps[chunk].append(
                copy(
                    comb.at[far, line, span], got.at[place, span],
                    swap_send.at[slot], swap_recv.at[slot], plane(step),
                )
            )
            swaps[chunk][-1].start()
    got[place] = comb[pair, row]

    for chunk, span in enumerate(spans):
        for one in swaps[chunk]:
            one.wait_recv()
        total = got[0, span]
        for index in range(1, count):
            total = total + got[index, span]
        allm[col, span] = total
        for step in range(1, cols):
            slot = chunk * cols + step
            gathers[chunk].append(
                copy(
                    allm.at[col, span], allm.at[col, span],
                    col_send.at[slot], col_recv.at[slot], column(step),
                )
            )
            gathers[chunk][-1].start()

    for chunk, span in enumerate(spans):
        for one in gathers[chunk]:
            one.wait_recv()
        for step in range(1, count):
            far, line = target(step)
            slot = chunk * count + step
            halves[chunk].append(
                copy(
                    allm.at[pl.ds(line * parts, parts), span], out_ref.at[me, :, span],
                    half_send.at[slot], half_recv.at[slot], plane(step),
                )
            )
            halves[chunk][-1].start()
        out_ref[me, :, span] = allm[pl.ds(row * parts, parts), span]
        slot = chunk * count
        forwards.append(
            copy(
                out_ref.at[me, :, span], out_ref.at[me, :, span],
                fwd_send.at[slot], fwd_recv.at[slot], sibling,
            )
        )
        forwards[-1].start()
        square = jnp.zeros((high, 1), jnp.float32)
        for index in range(cols):
            values = allm[index, span].astype(jnp.float32)
            square += jnp.sum(values * values, axis=1, keepdims=True)
        square = square / (cols * allm.shape[2])
        stat_ref[me, span] = jnp.broadcast_to(square, (high, 128))
        for step in range(1, count):
            slot = chunk * count + step
            stats[chunk].append(
                copy(
                    stat_ref.at[me, span], stat_ref.at[me, span],
                    stat_send.at[slot], stat_recv.at[slot], plane(step),
                )
            )
            stats[chunk][-1].start()
        slot = chunk * count
        forwards.append(
            copy(
                stat_ref.at[me, span], stat_ref.at[me, span],
                fst_send.at[slot], fst_recv.at[slot], sibling,
            )
        )
        forwards[-1].start()
    for chunk, span in enumerate(spans):
        for step in range(1, count):
            origin = source(step)
            slot = chunk * count + step
            halves[chunk][step - 1].wait_recv()
            forwards.append(
                copy(
                    out_ref.at[origin, :, span], out_ref.at[origin, :, span],
                    fwd_send.at[slot], fwd_recv.at[slot], sibling,
                )
            )
            forwards[-1].start()
            stats[chunk][step - 1].wait_recv()
            forwards.append(
                copy(
                    stat_ref.at[origin, span], stat_ref.at[origin, span],
                    fst_send.at[slot], fst_recv.at[slot], sibling,
                )
            )
            forwards[-1].start()
    for one in forwards:
        one.wait()
    for one in to_pair + sum(swaps + gathers + halves + stats, []):
        one.wait_send()


def spread(placed, sections, row_count, cols):
    owners = sections * row_count
    rows, width = placed.shape[0] // owners, placed.shape[1]
    pairs, count = sections // 2, sections // 2 * row_count
    parts = cols // row_count
    sizes = [pairs] * 2 + [4 * count] * 2 + [4 * cols] * 2 + [4 * count] * 8
    return pl.pallas_call(
        functools.partial(spread_kernel, sections, row_count, cols),
        out_shape=(
            jax.ShapeDtypeStruct((owners, parts, rows, width), jnp.bfloat16),
            jax.ShapeDtypeStruct((owners, rows, 128), jnp.float32),
        ),
        in_specs=[pl.BlockSpec(memory_space=pltpu.VMEM)],
        out_specs=(
            pl.BlockSpec(memory_space=pltpu.VMEM),
            pl.BlockSpec(memory_space=pltpu.VMEM),
        ),
        scratch_shapes=[
            pltpu.VMEM((pairs, row_count, rows, width), jnp.bfloat16),
            pltpu.VMEM((pairs, row_count, rows, width), jnp.bfloat16),
            pltpu.VMEM((count, rows, width), jnp.bfloat16),
            pltpu.VMEM((cols, rows, width), jnp.bfloat16),
        ]
        + [pltpu.SemaphoreType.DMA((size,)) for size in sizes],
        compiler_params=pltpu.CompilerParams(
            collective_id=1, has_side_effects=True, vmem_limit_bytes=40 * 1024 * 1024
        ),
    )(placed.reshape(pairs, 2, row_count, rows, width))


def score_kernel(
    cols, heads, kvs, half_ref, meansq_ref, gain_ref, wq_ref, wkv_ref, seg_col_ref, seg_row_ref,
    head_ref, res_ref, out_ref, normed, weights, mine, sent, got, bias, w_sem, send_sem, recv_sem
):
    owners, parts, rows, width = half_ref.shape
    tokens = owners * rows
    sec, row, col = (lax.axis_index(name) for name in ("section", "dp", "mp"))
    peer = (sec, 1 - row, col)
    chunk = 2 * HD
    queries = heads * HD // chunk
    count = kvs + queries
    kv_first = col * 2 * heads // GROUP

    barrier = pltpu.get_barrier_semaphore()
    pl.semaphore_signal(barrier, inc=1, device_id=peer, device_id_type=pl.DeviceIdType.MESH)

    loads = []
    for turn, line in enumerate((1 - row, row)):
        for index in range(count):
            if index < kvs:
                begin, ref = (kv_first + line * kvs + index) * chunk, wkv_ref
            else:
                begin, ref = line * heads * HD + (index - kvs) * chunk, wq_ref
            slot = turn * count + index
            columns = pl.ds(pl.multiple_of(begin, chunk), chunk)
            loads.append(
                pltpu.make_async_copy(ref.at[0, :, columns], weights.at[slot], w_sem.at[slot])
            )
            loads[-1].start()

    def norm(owner, carry):
        scale = lax.rsqrt(meansq_ref[owner][:, :1] + EPS)
        spot = pl.ds(pl.multiple_of(owner * rows, rows), rows)
        for part in range(parts):
            values = half_ref[owner, part].astype(jnp.float32)
            normed[spot, part * width : (part + 1) * width] = (
                values * scale * gain_ref[row * parts + part]
            ).astype(jnp.bfloat16)
        return carry

    lax.fori_loop(0, owners, norm, 0)
    pl.semaphore_wait(barrier, 1)

    copies = []
    for index in range(count):
        loads[index].wait()
        sent[index] = jnp.dot(normed[...], weights[index], preferred_element_type=jnp.float32)
        copies.append(
            pltpu.make_async_remote_copy(
                src_ref=sent.at[index],
                dst_ref=got.at[index],
                send_sem=send_sem.at[index],
                recv_sem=recv_sem.at[index],
                device_id=peer,
                device_id_type=pl.DeviceIdType.MESH,
            )
        )
        copies[-1].start()
    for index in range(count):
        loads[count + index].wait()
        mine[index] = jnp.dot(
            normed[...], weights[count + index], preferred_element_type=jnp.float32
        )

    inner = col - row * parts
    held = jnp.where((inner >= 0) & (inner < parts), 1.0, 0.0).astype(jnp.float32)
    inner = jnp.clip(inner, 0, parts - 1)

    def residual(owner, carry):
        values = half_ref[owner, inner].astype(jnp.float32) * res_ref[...]
        lanes = values[:, :128]
        for group in range(1, width // 128):
            lanes = lanes + values[:, group * 128 : (group + 1) * 128]
        out_ref[pl.ds(pl.multiple_of(owner * rows, rows), rows), :] = lanes * held
        return carry

    lax.fori_loop(0, owners, residual, 0)
    ahead = lax.broadcasted_iota(jnp.int32, (tokens, tokens), 0) >= lax.broadcasted_iota(
        jnp.int32, (tokens, tokens), 1
    )
    allowed = (seg_col_ref[...] == seg_row_ref[...]) & ahead
    bias[...] = jnp.where(allowed, 0.0, -jnp.inf)

    keyval = []
    for index in range(kvs):
        copies[index].wait_recv()
        keyval.append((mine[index] + got[index]).astype(jnp.bfloat16))
    step = 256
    for index in range(queries):
        copies[kvs + index].wait_recv()
        query = (mine[kvs + index] + got[kvs + index]).astype(jnp.bfloat16)
        for inside in range(chunk // HD):
            head = index * (chunk // HD) + inside
            pair = keyval[head * kvs // heads]
            head_cols = head_ref[row, :, head * HD : (head + 1) * HD]
            for begin in range(0, tokens, step):
                end = begin + step
                logits = lax.dot_general(
                    query[begin:end, inside * HD : (inside + 1) * HD],
                    pair[:end, :HD],
                    (((1,), (1,)), ((), ())),
                    preferred_element_type=jnp.float32,
                ) * (1.0 / math.sqrt(HD))
                logits = logits + bias[begin:end, :end]
                expo = jnp.exp(logits - jnp.max(logits, axis=1, keepdims=True))
                probs = (expo / jnp.sum(expo, axis=1, keepdims=True)).astype(jnp.bfloat16)
                attended = jnp.dot(probs, pair[:end, HD:], preferred_element_type=jnp.float32)
                out_ref[begin:end, :] += attended * head_cols
    for one in copies:
        one.wait_send()


def score(half, meansq, gain, w_query, w_keyval, segment, out_head, res_head, heads, kvs):
    owners, parts, rows, width = half.shape
    tokens, depth = owners * rows, parts * width
    count = kvs + heads // 2
    vmem = pl.BlockSpec(memory_space=pltpu.VMEM)
    anyw = pl.BlockSpec(memory_space=pl.ANY)
    cols = gain.shape[0]
    return pl.pallas_call(
        functools.partial(score_kernel, cols, heads, kvs),
        out_shape=jax.ShapeDtypeStruct((tokens, 128), jnp.float32),
        in_specs=[vmem, vmem, vmem, anyw, anyw, vmem, vmem, vmem, vmem],
        out_specs=vmem,
        scratch_shapes=[
            pltpu.VMEM((tokens, depth), jnp.bfloat16),
            pltpu.VMEM((2 * count, depth, 2 * HD), jnp.bfloat16),
            pltpu.VMEM((count, tokens, 2 * HD), jnp.float32),
            pltpu.VMEM((count, tokens, 2 * HD), jnp.float32),
            pltpu.VMEM((count, tokens, 2 * HD), jnp.float32),
            pltpu.VMEM((tokens, tokens), jnp.float32),
            pltpu.SemaphoreType.DMA((2 * count,)),
            pltpu.SemaphoreType.DMA((count,)),
            pltpu.SemaphoreType.DMA((count,)),
        ],
        compiler_params=pltpu.CompilerParams(
            collective_id=2, has_side_effects=True, vmem_limit_bytes=50 * 1024 * 1024
        ),
    )(
        half, meansq, gain, w_query, w_keyval, segment[:, None], segment[None, :],
        out_head.reshape(2, 1, heads * HD), res_head,
    )


def fused_kernel(
    chunks, lengths_any, x_any, gain_any, wq_ref, wkv_ref, head_any, res_any, out_ref,
    lengths_ref, gain_ref, head_ref, res_ref, small_sem, x_ref, placed, sib, comb, yb, own, xb, full, normed, weights, sent, got, mine, keys, values,
    acc, scale, stat, stats, part, held, x_sem, w_sem, sib_send, sib_recv, y_send, y_recv,
    x_send, x_recv, z_send, z_recv, fy_send, fy_recv, fs_send, fs_recv, p_send, p_recv,
    stat_send, stat_recv, held_send, held_recv,
):
    sections, row_count, cols = 4, 2, 4
    count = sections * row_count * cols
    tokens, width = acc.shape[0], x_ref.shape[1]
    high = tokens // chunks
    rows = high // sections
    rolls = lengths_ref.shape[0]
    chunk = 2 * HD
    parts = weights.shape[0] // 2
    sec, row, col = (lax.axis_index(name) for name in ("section", "dp", "mp"))
    core, side = sec % 2, sec // 2
    me = (sec * row_count + row) * cols + col
    rank = jnp.where(row == 0, col, 3 - col)
    sibling = (2 * side + 1 - core, row, col)
    across = 2 * (1 - side) + core
    over_y = (across, row, col)
    over_x = (sec, 1 - row, col)

    def line(target):
        return (sec, row, jnp.where(row == 0, target, 3 - target))

    def half(origin):
        return jnp.where(row == 0, origin, 1 - origin)

    def copy(src, dst, send_sem, recv_sem, device):
        return pltpu.make_async_remote_copy(
            src_ref=src,
            dst_ref=dst,
            send_sem=send_sem,
            recv_sem=recv_sem,
            device_id=device,
            device_id_type=pl.DeviceIdType.MESH,
        )

    load = pltpu.make_async_copy(x_any, x_ref, x_sem)
    load.start()
    small = []
    for index, (src, dst) in enumerate(
        ((lengths_any, lengths_ref), (gain_any, gain_ref), (head_any, head_ref), (res_any, res_ref))
    ):
        small.append(pltpu.make_async_copy(src, dst, small_sem.at[index]))
        small[-1].start()
    kv_first = col * 2
    loads = []
    for turn, where in enumerate((1 - row, row)):
        for index in range(parts):
            if index == 0:
                begin, ref = (kv_first + where) * chunk, wkv_ref
            else:
                begin, ref = where * GROUP * HD + (index - 1) * chunk, wq_ref
            slot = turn * parts + index
            columns = pl.ds(pl.multiple_of(begin, chunk), chunk)
            loads.append(
                pltpu.make_async_copy(ref.at[0, :, columns], weights.at[slot], w_sem.at[slot])
            )
            loads[-1].start()

    barrier = pltpu.get_barrier_semaphore()

    def peer(step):
        return coords((me + step) % count, row_count, cols)

    near = [sibling, over_y, over_x] + [(sec, row, (col + step) % cols) for step in (1, 2, 3)]
    for device in near:
        pl.semaphore_signal(
            barrier, inc=1, device_id=device, device_id_type=pl.DeviceIdType.MESH
        )

    small[0].wait()
    owner = sec * row_count + row
    my_off, my_len, total = 0, 0, 0
    offsets = []
    for index in range(rolls):
        length = lengths_ref[index]
        offsets.append(total)
        total = total + length
        my_off = my_off + jnp.where(index < owner, length, 0)
        my_len = my_len + jnp.where(index == owner, length, 0)

    load.wait()
    limit = x_ref.shape[0]

    def place(begin):
        slots = begin + lax.broadcasted_iota(jnp.int32, (high, limit), 0)
        spots = lax.broadcasted_iota(jnp.int32, (high, limit), 1)
        hit = (slots == my_off + spots) & (spots < my_len)
        rows_here = jnp.dot(
            jnp.where(hit, 1.0, 0.0).astype(jnp.bfloat16), x_ref[...],
            preferred_element_type=jnp.float32,
        )
        return rows_here.astype(jnp.bfloat16).reshape(2, 2, rows, width)

    lines = lax.broadcasted_iota(jnp.int32, (limit, tokens), 1)
    spots = lax.broadcasted_iota(jnp.int32, (limit, tokens), 0)
    hit = (lines == my_off + spots) & (spots < my_len)
    square = jnp.zeros((limit, 128), jnp.float32)
    for group in range(width // 128):
        piece = x_ref[:, group * 128 : (group + 1) * 128].astype(jnp.float32)
        square = square + piece * piece
    moved = jnp.dot(
        jnp.broadcast_to(jnp.sum(jnp.transpose(square), axis=0, keepdims=True), (8, limit)),
        jnp.where(hit, 1.0, 0.0), preferred_element_type=jnp.float32,
        precision=lax.Precision.HIGHEST,
    )
    blocks = tokens // 128
    for block in range(blocks):
        stat[0, block : block + 1] = moved[:1, block * 128 : (block + 1) * 128]
    pl.semaphore_wait(barrier, len(near))

    def to_sib(c):
        return copy(placed.at[c, :, 1 - core], sib.at[c], sib_send.at[c], sib_recv.at[c], sibling)

    def to_y(c):
        return copy(comb.at[c, 1 - side], yb.at[c], y_send.at[c], y_recv.at[c], over_y)

    def to_x(c):
        return copy(own.at[c], xb.at[c], x_send.at[c], x_recv.at[c], over_x)

    def dispatch(c):
        placed[c] = place(c * high)
        to_sib(c).start()

    def reduce_pair(c):
        to_sib(c).wait_recv()
        comb[c] = placed[c, :, core] + sib[c]
        to_y(c).start()

    early = rank <= 1
    mine_half = col % 2

    def z_copy(c, origin, target, slot):
        ref = full.at[c, half(origin), sec]
        return copy(ref, ref, z_send.at[c, slot], z_recv.at[c, origin], line(target))

    def fy_copy(c, origin, group):
        ref = full.at[c, half(origin), group]
        return copy(ref, ref, fy_send.at[c, origin], fy_recv.at[c, origin], over_y)

    def fs_copy(c, which, group):
        ref = full.at[c, :, group]
        return copy(ref, ref, fs_send.at[c, which], fs_recv.at[c, which], sibling)

    def gather_own(c):
        to_y(c).wait_recv()
        own[c] = comb[c, side] + yb[c]

        @pl.when(rank >= 2)
        def _():
            to_x(c).start()

    def land(c):
        @pl.when(early)
        def _():
            to_x(c).wait_recv()
            full[c, mine_half, sec] = own[c] + xb[c]

        @pl.when(rank == 0)
        def _():
            z_copy(c, 0, 1, 0).start()
            fy_copy(c, 0, sec).start()

        @pl.when(rank == 1)
        def _():
            z_copy(c, 1, 2, 0).start()
            z_copy(c, 1, 0, 1).start()
            fy_copy(c, 1, sec).start()

    def pass_on(c, at):
        for origin in (1, 0):
            if at == origin:
                continue
            z_copy(c, origin, origin, 0).wait_recv()
            if at in (1, 2):
                z_copy(c, origin, at + 1, 2 if at == 1 else origin).start()
            fy_copy(c, origin, sec).start()
        fs_copy(c, 0, sec).start()

    def to_both(c):
        for origin in (1, 0):
            fy_copy(c, origin, across).wait_recv()
        fs_copy(c, 1, across).start()

    def everyone(src, dst, send_sem, recv_sem):
        def one(step):
            return copy(src, dst.at[me], send_sem.at[step], recv_sem.at[step], peer(step))

        def send(step, carry):
            one(step).start()
            return carry

        def finish(step, carry):
            one(step).wait()
            return carry

        return (
            lambda: lax.fori_loop(1, count, send, 0),
            lambda: lax.fori_loop(1, count, finish, 0),
        )

    rounds = (sibling, over_y, over_x, near[3 + 1], (sec, row, col + 1 - 2 * (col % 2)))

    def stat_copy(turn):
        return copy(
            stat.at[turn], stats.at[turn], stat_send.at[turn], stat_recv.at[turn], rounds[turn]
        )

    def stat_round(turn):
        if turn:
            stat_copy(turn - 1).wait_recv()
            stat[turn] = stat[turn - 1] + stats[turn - 1]
        stat_copy(turn).start()

    keys[...] = jnp.zeros_like(keys)
    values[...] = jnp.zeros_like(values)

    def ready():
        for one in small[1:]:
            one.wait()
        last = len(rounds) - 1
        stat_copy(last).wait_recv()
        mean = (stat[last] + stats[last]) / (cols * width)
        factor = lax.rsqrt(mean + EPS)
        for block in range(blocks):
            wide = jnp.broadcast_to(factor[block : block + 1], (128, 128))
            scale[block * 128 : (block + 1) * 128] = jnp.transpose(wide)

    def exchange(c):
        return copy(sent.at[c], got.at[c], p_send.at[c], p_recv.at[c], over_x)

    def project(c):
        for which, group in ((0, 2 * side + 1 - core), (1, 2 * (1 - side) + 1 - core)):
            fs_copy(c, which, group).wait_recv()
        here = pl.ds(pl.multiple_of(c * high, high), high)
        factor = scale[here, :][:, :1]

        @pl.when(c == 0)
        def _():
            for one in loads:
                one.wait()

        for part_index in range(2):
            piece = full[c, part_index].reshape(high, width).astype(jnp.float32)
            normed[:, part_index * width : (part_index + 1) * width] = (
                piece * factor * gain_ref[row * 2 + part_index]
            ).astype(jnp.bfloat16)
        for index in range(parts):
            sent[c, index] = jnp.dot(
                normed[...], weights[index], preferred_element_type=jnp.float32
            )
        exchange(c).start()
        for index in range(parts):
            mine[c, index] = jnp.dot(
                normed[...], weights[parts + index], preferred_element_type=jnp.float32
            )

        acc[here] = jnp.zeros((high, 128), jnp.float32)

        @pl.when(early)
        def _():
            piece = full[c, mine_half].reshape(high, width).astype(jnp.float32) * res_ref[...]
            lanes = piece[:, :128]
            for group in range(1, width // 128):
                lanes = lanes + piece[:, group * 128 : (group + 1) * 128]
            acc[here] = lanes

    def attend(c):
        exchange(c).wait_recv()

        @pl.when(2 * c < chunks)
        def _():
            attend_to(c, tokens // 2)

        @pl.when(2 * c >= chunks)
        def _():
            attend_to(c, tokens)

    def attend_to(c, end):
        here = pl.ds(pl.multiple_of(c * high, high), high)
        pair = (mine[c, 0] + got[c, 0]).astype(jnp.bfloat16)
        keys[here] = pair[:, :HD]
        values[here] = pair[:, HD:]
        heads = []
        for index in range(1, parts):
            both = (mine[c, index] + got[c, index]).astype(jnp.bfloat16)
            heads += [both[:, :HD], both[:, HD:]]
        query = jnp.concatenate(heads, axis=0)
        logits = lax.dot_general(
            query, keys[:end], (((1,), (1,)), ((), ())), preferred_element_type=jnp.float32
        ) * (1.0 / math.sqrt(HD))
        slots = c * high + lax.broadcasted_iota(jnp.int32, (high, end), 0)
        spots = lax.broadcasted_iota(jnp.int32, (high, end), 1)
        start = jnp.zeros((high, end), jnp.int32)
        for offset in offsets[1:]:
            start = jnp.where(slots >= offset, offset, start)
        allowed = (spots >= start) & (spots <= slots)
        bias = jnp.where(allowed, 0.0, -jnp.inf)
        logits = logits + jnp.concatenate([bias] * len(heads), axis=0)
        expo = jnp.exp(logits - jnp.max(logits, axis=1, keepdims=True))
        probs = (expo / jnp.sum(expo, axis=1, keepdims=True)).astype(jnp.bfloat16)
        attended = jnp.dot(probs, values[:end], preferred_element_type=jnp.float32)
        lanes = acc[here]
        for head in range(len(heads)):
            lanes = lanes + attended[head * high : (head + 1) * high] * head_ref[
                row, :, head * HD : (head + 1) * HD
            ]
        acc[here] = lanes

    lags = (4, 4, 6, 7)
    first = ((dispatch, 0), (reduce_pair, 1), (gather_own, 2), (land, 3))
    later = ((project, 8), (attend, 10))

    def at_lag(k, lag, stage):
        @pl.when((k >= lag) & (k < chunks + lag))
        def _():
            stage(k - lag)

    def step(k, carry):
        for stage, lag in first:
            at_lag(k, lag, stage)
        for turn in range(len(rounds)):
            @pl.when(k == turn + 1)
            def _():
                stat_round(turn)

        for at in range(cols):
            @pl.when(rank == at)
            def _():
                at_lag(k, lags[at], lambda c: pass_on(c, at))
                at_lag(k, lags[at] + 1, to_both)

        pl.when(k == later[0][1])(ready)
        for stage, lag in later:
            at_lag(k, lag, stage)
        return carry

    lax.fori_loop(0, chunks + later[-1][1], step, 0)

    for block in range(blocks):
        lanes = acc[block * 128 : (block + 1) * 128]
        part[block : block + 1] = jnp.sum(jnp.transpose(lanes), axis=0, keepdims=True)
    send_part, finish_part = everyone(part, held, held_send, held_recv)
    send_part()
    held[me] = part[...]

    def drain(c, carry):
        to_sib(c).wait_send()
        to_y(c).wait_send()

        @pl.when(rank >= 2)
        def _():
            to_x(c).wait_send()

        for origin in range(2):
            fy_copy(c, origin, sec).wait_send()
        fs_copy(c, 0, sec).wait_send()
        fs_copy(c, 1, across).wait_send()
        exchange(c).wait_send()

        @pl.when(rank == 0)
        def _():
            z_copy(c, 0, 1, 0).wait_send()

        @pl.when(rank == 1)
        def _():
            z_copy(c, 1, 2, 0).wait_send()
            z_copy(c, 1, 0, 1).wait_send()
            z_copy(c, 0, 2, 2).wait_send()

        @pl.when(rank == 2)
        def _():
            z_copy(c, 1, 3, 1).wait_send()
            z_copy(c, 0, 3, 0).wait_send()

        return carry

    lax.fori_loop(0, chunks, drain, 0)
    for turn in range(len(rounds)):
        stat_copy(turn).wait_send()
    finish_part()
    spots = lax.broadcasted_iota(jnp.int32, (128, limit), 1)
    totals = []
    for section in range(sections):
        begin = section * row_count * cols
        totals.append(jnp.sum(held[begin : begin + row_count * cols], axis=0))
    result = jnp.zeros((sections, limit), jnp.float32)
    for block in range(blocks):
        slots = block * 128 + lax.broadcasted_iota(jnp.int32, (128, limit), 0)
        hit = (slots == my_off + spots) & (spots < my_len)
        picked = jnp.concatenate([one[block : block + 1] for one in totals], axis=0)
        result = result + jnp.dot(
            picked, jnp.where(hit, 1.0, 0.0), preferred_element_type=jnp.float32,
            precision=lax.Precision.HIGHEST,
        )
    out_ref[...] = result


def fused(rollouts, lengths, gain, w_query, w_keyval, out_head, res_head, chunks):
    limit, width = rollouts.shape[1:]
    depth = w_query.shape[1]
    tokens = lengths.shape[0] * limit // 4
    high = tokens // chunks
    rows = high // 4
    vmem = pl.BlockSpec(memory_space=pltpu.VMEM)
    hbm = pl.BlockSpec(memory_space=pltpu.HBM)
    bf16, f32, dma = jnp.bfloat16, jnp.float32, pltpu.SemaphoreType.DMA
    parts = 3
    sems = [(chunks,)] * 6 + [(chunks, 3)] + [(chunks, 2)] * 5 + [(chunks,)] * 2 + [(5,)] * 2 + [(32,)] * 2
    out = pl.pallas_call(
        functools.partial(fused_kernel, chunks),
        out_shape=jax.ShapeDtypeStruct((4, limit), f32),
        in_specs=[hbm] * 7,
        out_specs=vmem,
        scratch_shapes=[
            pltpu.SMEM(lengths.shape, jnp.int32),
            pltpu.VMEM(gain.shape, f32),
            pltpu.VMEM((2, 1, GROUP * HD), f32),
            pltpu.VMEM(res_head.shape, f32),
            dma((4,)),
            pltpu.VMEM((limit, width), bf16),
            pltpu.VMEM((chunks, 2, 2, rows, width), bf16),
            pltpu.VMEM((chunks, 2, rows, width), bf16),
            pltpu.VMEM((chunks, 2, rows, width), bf16),
            pltpu.VMEM((chunks, rows, width), bf16),
            pltpu.VMEM((chunks, rows, width), bf16),
            pltpu.VMEM((chunks, rows, width), bf16),
            pltpu.VMEM((chunks, 2, 4, rows, width), bf16),
            pltpu.VMEM((high, depth), bf16),
            pltpu.VMEM((2 * parts, depth, 2 * HD), bf16),
            pltpu.VMEM((chunks, parts, high, 2 * HD), f32),
            pltpu.VMEM((chunks, parts, high, 2 * HD), f32),
            pltpu.VMEM((chunks, parts, high, 2 * HD), f32),
            pltpu.VMEM((tokens, HD), bf16),
            pltpu.VMEM((tokens, HD), bf16),
            pltpu.VMEM((tokens, 128), f32),
            pltpu.VMEM((tokens, 128), f32),
            pltpu.VMEM((5, tokens // 128, 128), f32),
            pltpu.VMEM((5, tokens // 128, 128), f32),
            pltpu.VMEM((tokens // 128, 128), f32),
            pltpu.VMEM((32, tokens // 128, 128), f32),
            dma,
            dma((2 * parts,)),
        ]
        + [dma(size) for size in sems],
        compiler_params=pltpu.CompilerParams(
            collective_id=3, has_side_effects=True, vmem_limit_bytes=48 * 1024 * 1024
        ),
    )(
        lengths, rollouts.reshape(limit, width), gain, w_query, w_keyval,
        out_head.reshape(2, 1, GROUP * HD), res_head,
    )
    return out.reshape(4, 1, limit)


def plain(half, meansq, gains, w_query, w_keyval, segment, out_head, res_head):
    owners, _, rows, local_width = half.shape
    tokens = owners * rows
    row_count, cols = lax.axis_size("dp"), lax.axis_size("mp")
    my_row, my_col = lax.axis_index("dp"), lax.axis_index("mp")
    slots = jnp.arange(tokens, dtype=jnp.int32)
    scale_row = lax.rsqrt(meansq[:, None, :, :1] + EPS)
    parts = cols // row_count
    gain = lax.dynamic_slice_in_dim(gains, my_row * parts, parts, 0)
    normed = (half.astype(jnp.float32) * scale_row * gain[None]).astype(jnp.bfloat16)

    heads_here = w_query.shape[2] // HD
    kv_here = max(1, heads_here // GROUP)
    kv_first = my_col * heads_here // GROUP
    w_kv = lax.dynamic_slice_in_dim(w_keyval[0], kv_first * 2 * HD, kv_here * 2 * HD, 1)
    q_part, kv_part = 0.0, 0.0
    for part in range(parts):
        rows = normed[:, part].reshape(tokens, local_width)
        begin = part * local_width
        end = begin + local_width
        q_part += jnp.dot(rows, w_query[0, begin:end], preferred_element_type=jnp.float32)
        kv_part += jnp.dot(rows, w_kv[begin:end], preferred_element_type=jnp.float32)
    heads, kvs = heads_here, kv_here
    summed = lax.psum(jnp.concatenate([q_part, kv_part], axis=1), "dp")
    head_cols = out_head[0]
    weight = (my_row == 0).astype(jnp.float32)
    summed = summed.astype(jnp.bfloat16)
    query = summed[:, : heads * HD].reshape(tokens, kvs, heads // kvs, HD)
    keyval = summed[:, heads * HD :].reshape(tokens, kvs, 2, HD)
    logits = jnp.einsum(
        "qkgd,skd->kgqs", query, keyval[:, :, 0, :], preferred_element_type=jnp.float32
    ) * (1.0 / math.sqrt(HD))
    allowed = (segment[:, None] == segment[None, :]) & (slots[None, :] <= slots[:, None])
    logits = jnp.where(allowed, logits, -jnp.inf)
    expo = jnp.exp(logits - jnp.max(logits, axis=-1, keepdims=True))
    probs = (expo / jnp.sum(expo, axis=-1, keepdims=True)).astype(jnp.bfloat16)
    attended = jnp.einsum(
        "kgqs,skd->qkgd", probs, keyval[:, :, 1, :], preferred_element_type=jnp.float32
    ).reshape(tokens, heads * HD)
    inner = my_col - my_row * parts
    res_in = lax.dynamic_index_in_dim(half, jnp.clip(inner, 0, parts - 1), 1, keepdims=False)
    res_sum = jnp.sum(
        res_in.reshape(tokens, local_width).astype(jnp.float32) * res_head[0][None, :], axis=1
    )
    res_sum = jnp.where((inner >= 0) & (inner < parts), res_sum, 0.0)
    return weight * jnp.sum(attended * head_cols[None, :], axis=1) + res_sum


def body(rollouts, lengths, norm_gain, w_query, w_keyval, out_head, res_head):
    roll_count, max_len, local_width = rollouts.shape
    sections, row_count, cols = (lax.axis_size(name) for name in ("section", "dp", "mp"))
    if (sections, row_count, cols, roll_count) == (4, 2, 4, 1) and w_query.shape[2] == 8 * HD:
        gains = norm_gain[0].reshape(cols, 1, local_width)
        return fused(rollouts, lengths, gains, w_query, w_keyval, out_head, res_head, CHUNKS)
    owner = lax.axis_index(OWN)
    total_rolls = lengths.shape[0]
    tokens = total_rolls * max_len // 4

    ids = jnp.arange(total_rolls, dtype=jnp.int32)
    offsets = jnp.sum(jnp.where(ids[None, :] < ids[:, None], lengths[None, :], 0), axis=1)
    slots = jnp.arange(tokens, dtype=jnp.int32)
    segment = jnp.sum((slots[:, None] >= offsets[None, :]).astype(jnp.int32), axis=1)

    position = jnp.arange(max_len, dtype=jnp.int32)
    mine = owner * roll_count + jnp.arange(roll_count, dtype=jnp.int32)
    my_off = jnp.sum(jnp.where(ids[None, :] == mine[:, None], offsets[None, :], 0), axis=1)
    my_len = jnp.sum(jnp.where(ids[None, :] == mine[:, None], lengths[None, :], 0), axis=1)
    place = (
        (slots[:, None, None] == my_off[None, :, None] + position[None, None, :])
        & (position[None, None, :] < my_len[None, :, None])
    ).astype(jnp.bfloat16)
    placed = jnp.dot(
        place.reshape(tokens, roll_count * max_len),
        rollouts.reshape(roll_count * max_len, local_width),
        preferred_element_type=jnp.float32,
    ).astype(jnp.bfloat16)
    half, meansq = spread(placed, sections, row_count, cols)
    heads_here = w_query.shape[2] // HD
    gains = norm_gain[0].reshape(cols, 1, local_width)
    if row_count == 2 and heads_here % (2 * GROUP) == 0 and tokens % 256 == 0:
        lanes = score(
            half, meansq, gains, w_query, w_keyval, segment, out_head, res_head,
            heads_here // 2, heads_here // 2 // GROUP,
        )
        partial = jnp.sum(lanes, axis=1)
    else:
        partial = plain(
            half, meansq, gains, w_query, w_keyval, segment, out_head, res_head
        )
    home = share(partial, sections, row_count, cols)
    home = jnp.pad(home, ((0, 0), (0, max_len)))
    lines = []
    for local in range(roll_count):
        line = lax.dynamic_slice_in_dim(home, my_off[local], max_len, 1)
        lines.append(jnp.where(position[None, :] < my_len[local], line, 0.0))
    return jnp.stack(lines, axis=1)


def solution(mesh):
    in_specs = (
        P(("section", "dp"), None, "mp"),
        P(),
        P("section", None),
        P("section", "dp", "mp"),
        P("section", "dp", None),
        P("section", "mp"),
        P("section", "mp"),
    )
    out_specs = P(None, ("section", "dp"), None)
    return jax.shard_map(body, mesh=mesh, in_specs=in_specs, out_specs=out_specs, check_vma=False)
```

```python
import functools
import math

import jax
import jax.numpy as jnp
from jax import lax
from jax.experimental import pallas as pl
from jax.experimental.pallas import tpu as pltpu
from jax.sharding import PartitionSpec as P

HD = 128
KV = 8
HEADS = 32
GROUP = HEADS // KV
EPS = 1e-05
CHUNKS = 8
OWN = ("section", "dp")


def coords(index, row_count, cols):
    return (index // (row_count * cols), index // cols % row_count, index % cols)


def share_kernel(sections, row_count, cols, part_ref, out_ref, held, send_sem, recv_sem):
    count = sections * row_count * cols
    me = (lax.axis_index("section") * row_count + lax.axis_index("dp")) * cols
    me = me + lax.axis_index("mp")
    barrier = pltpu.get_barrier_semaphore()

    def peer(step):
        return coords((me + step) % count, row_count, cols)

    def greet(step, carry):
        pl.semaphore_signal(
            barrier, inc=1, device_id=peer(step), device_id_type=pl.DeviceIdType.MESH
        )
        return carry

    lax.fori_loop(1, count, greet, 0)
    pl.semaphore_wait(barrier, count - 1)

    def copy(step):
        return pltpu.make_async_remote_copy(
            src_ref=part_ref,
            dst_ref=held.at[me],
            send_sem=send_sem.at[step],
            recv_sem=recv_sem.at[step],
            device_id=peer(step),
            device_id_type=pl.DeviceIdType.MESH,
        )

    def send(step, carry):
        copy(step).start()
        return carry

    def finish(step, carry):
        copy(step).wait()
        return carry

    lax.fori_loop(1, count, send, 0)
    held[me] = part_ref[...]
    lax.fori_loop(1, count, finish, 0)
    for section in range(sections):
        begin = section * row_count * cols
        out_ref[section] = jnp.sum(held[begin : begin + row_count * cols], axis=0)


def share(partial, sections, row_count, cols):
    rows = partial.shape[0] // 128
    count = sections * row_count * cols
    return pl.pallas_call(
        functools.partial(share_kernel, sections, row_count, cols),
        out_shape=jax.ShapeDtypeStruct((sections, rows, 128), jnp.float32),
        in_specs=[pl.BlockSpec(memory_space=pltpu.VMEM)],
        out_specs=pl.BlockSpec(memory_space=pltpu.VMEM),
        scratch_shapes=[
            pltpu.VMEM((count, rows, 128), jnp.float32),
            pltpu.SemaphoreType.DMA((count,)),
            pltpu.SemaphoreType.DMA((count,)),
        ],
        compiler_params=pltpu.CompilerParams(collective_id=0, has_side_effects=True),
    )(partial.reshape(rows, 128)).reshape(sections, rows * 128)


def spread_kernel(
    sections, row_count, cols, placed_ref, out_ref, stat_ref, sib, comb, got, allm, *sems
):
    pair_send, pair_recv, swap_send, swap_recv, col_send, col_recv = sems[:6]
    half_send, half_recv, stat_send, stat_recv, fwd_send, fwd_recv, fst_send, fst_recv = sems[6:]
    pairs, parts = sections // 2, cols // row_count
    sec, row, col = (lax.axis_index(name) for name in ("section", "dp", "mp"))
    par, pair = sec % 2, sec // 2
    sibling = (2 * pair + 1 - par, row, col)
    count = pairs * row_count

    def target(step):
        return (pair + step // row_count) % pairs, (row + step % row_count) % row_count

    def source(step):
        far = (pair + pairs - step // row_count) % pairs
        return (2 * far + par) * row_count + (row + row_count - step % row_count) % row_count

    def plane(step):
        far, line = target(step)
        return (2 * far + par, line, col)

    def column(step):
        return (sec, row, (col + step) % cols)

    def copy(src, dst, send_sem, recv_sem, device):
        return pltpu.make_async_remote_copy(
            src_ref=src,
            dst_ref=dst,
            send_sem=send_sem,
            recv_sem=recv_sem,
            device_id=device,
            device_id_type=pl.DeviceIdType.MESH,
        )

    barrier = pltpu.get_barrier_semaphore()
    others = [sibling]
    others += [plane(step) for step in range(1, count)]
    others += [column(step) for step in range(1, cols)]
    for device in others:
        pl.semaphore_signal(
            barrier, inc=1, device_id=device, device_id_type=pl.DeviceIdType.MESH
        )
    pl.semaphore_wait(barrier, len(others))

    to_pair = [
        copy(
            placed_ref.at[far, 1 - par], sib.at[far], pair_send.at[far], pair_recv.at[far], sibling
        )
        for far in range(pairs)
    ]
    for one in to_pair:
        one.start()
    for far in range(pairs):
        to_pair[far].wait_recv()
        comb[far] = placed_ref[far, par] + sib[far]

    chunks = 4
    high = allm.shape[1] // chunks
    spans = [pl.ds(chunk * high, high) for chunk in range(chunks)]
    place = pair * row_count + row
    me = sec * row_count + row
    swaps = [[] for _ in spans]
    gathers = [[] for _ in spans]
    halves = [[] for _ in spans]
    stats = [[] for _ in spans]
    forwards = []

    for chunk, span in enumerate(spans):
        for step in range(1, count):
            far, line = target(step)
            slot = chunk * count + step
            swaps[chunk].append(
                copy(
                    comb.at[far, line, span], got.at[place, span],
                    swap_send.at[slot], swap_recv.at[slot], plane(step),
                )
            )
            swaps[chunk][-1].start()
    got[place] = comb[pair, row]

    for chunk, span in enumerate(spans):
        for one in swaps[chunk]:
            one.wait_recv()
        total = got[0, span]
        for index in range(1, count):
            total = total + got[index, span]
        allm[col, span] = total
        for step in range(1, cols):
            slot = chunk * cols + step
            gathers[chunk].append(
                copy(
                    allm.at[col, span], allm.at[col, span],
                    col_send.at[slot], col_recv.at[slot], column(step),
                )
            )
            gathers[chunk][-1].start()

    for chunk, span in enumerate(spans):
        for one in gathers[chunk]:
            one.wait_recv()
        for step in range(1, count):
            far, line = target(step)
            slot = chunk * count + step
            halves[chunk].append(
                copy(
                    allm.at[pl.ds(line * parts, parts), span], out_ref.at[me, :, span],
                    half_send.at[slot], half_recv.at[slot], plane(step),
                )
            )
            halves[chunk][-1].start()
        out_ref[me, :, span] = allm[pl.ds(row * parts, parts), span]
        slot = chunk * count
        forwards.append(
            copy(
                out_ref.at[me, :, span], out_ref.at[me, :, span],
                fwd_send.at[slot], fwd_recv.at[slot], sibling,
            )
        )
        forwards[-1].start()
        square = jnp.zeros((high, 1), jnp.float32)
        for index in range(cols):
            values = allm[index, span].astype(jnp.float32)
            square += jnp.sum(values * values, axis=1, keepdims=True)
        square = square / (cols * allm.shape[2])
        stat_ref[me, span] = jnp.broadcast_to(square, (high, 128))
        for step in range(1, count):
            slot = chunk * count + step
            stats[chunk].append(
                copy(
                    stat_ref.at[me, span], stat_ref.at[me, span],
                    stat_send.at[slot], stat_recv.at[slot], plane(step),
                )
            )
            stats[chunk][-1].start()
        slot = chunk * count
        forwards.append(
            copy(
                stat_ref.at[me, span], stat_ref.at[me, span],
                fst_send.at[slot], fst_recv.at[slot], sibling,
            )
        )
        forwards[-1].start()
    for chunk, span in enumerate(spans):
        for step in range(1, count):
            origin = source(step)
            slot = chunk * count + step
            halves[chunk][step - 1].wait_recv()
            forwards.append(
                copy(
                    out_ref.at[origin, :, span], out_ref.at[origin, :, span],
                    fwd_send.at[slot], fwd_recv.at[slot], sibling,
                )
            )
            forwards[-1].start()
            stats[chunk][step - 1].wait_recv()
            forwards.append(
                copy(
                    stat_ref.at[origin, span], stat_ref.at[origin, span],
                    fst_send.at[slot], fst_recv.at[slot], sibling,
                )
            )
            forwards[-1].start()
    for one in forwards:
        one.wait()
    for one in to_pair + sum(swaps + gathers + halves + stats, []):
        one.wait_send()


def spread(placed, sections, row_count, cols):
    owners = sections * row_count
    rows, width = placed.shape[0] // owners, placed.shape[1]
    pairs, count = sections // 2, sections // 2 * row_count
    parts = cols // row_count
    sizes = [pairs] * 2 + [4 * count] * 2 + [4 * cols] * 2 + [4 * count] * 8
    return pl.pallas_call(
        functools.partial(spread_kernel, sections, row_count, cols),
        out_shape=(
            jax.ShapeDtypeStruct((owners, parts, rows, width), jnp.bfloat16),
            jax.ShapeDtypeStruct((owners, rows, 128), jnp.float32),
        ),
        in_specs=[pl.BlockSpec(memory_space=pltpu.VMEM)],
        out_specs=(
            pl.BlockSpec(memory_space=pltpu.VMEM),
            pl.BlockSpec(memory_space=pltpu.VMEM),
        ),
        scratch_shapes=[
            pltpu.VMEM((pairs, row_count, rows, width), jnp.bfloat16),
            pltpu.VMEM((pairs, row_count, rows, width), jnp.bfloat16),
            pltpu.VMEM((count, rows, width), jnp.bfloat16),
            pltpu.VMEM((cols, rows, width), jnp.bfloat16),
        ]
        + [pltpu.SemaphoreType.DMA((size,)) for size in sizes],
        compiler_params=pltpu.CompilerParams(
            collective_id=1, has_side_effects=True, vmem_limit_bytes=40 * 1024 * 1024
        ),
    )(placed.reshape(pairs, 2, row_count, rows, width))


def score_kernel(
    cols, heads, kvs, half_ref, meansq_ref, gain_ref, wq_ref, wkv_ref, seg_col_ref, seg_row_ref,
    head_ref, res_ref, out_ref, normed, weights, mine, sent, got, bias, w_sem, send_sem, recv_sem
):
    owners, parts, rows, width = half_ref.shape
    tokens = owners * rows
    sec, row, col = (lax.axis_index(name) for name in ("section", "dp", "mp"))
    peer = (sec, 1 - row, col)
    chunk = 2 * HD
    queries = heads * HD // chunk
    count = kvs + queries
    kv_first = col * 2 * heads // GROUP

    barrier = pltpu.get_barrier_semaphore()
    pl.semaphore_signal(barrier, inc=1, device_id=peer, device_id_type=pl.DeviceIdType.MESH)

    loads = []
    for turn, line in enumerate((1 - row, row)):
        for index in range(count):
            if index < kvs:
                begin, ref = (kv_first + line * kvs + index) * chunk, wkv_ref
            else:
                begin, ref = line * heads * HD + (index - kvs) * chunk, wq_ref
            slot = turn * count + index
            columns = pl.ds(pl.multiple_of(begin, chunk), chunk)
            loads.append(
                pltpu.make_async_copy(ref.at[0, :, columns], weights.at[slot], w_sem.at[slot])
            )
            loads[-1].start()

    def norm(owner, carry):
        scale = lax.rsqrt(meansq_ref[owner][:, :1] + EPS)
        spot = pl.ds(pl.multiple_of(owner * rows, rows), rows)
        for part in range(parts):
            values = half_ref[owner, part].astype(jnp.float32)
            normed[spot, part * width : (part + 1) * width] = (
                values * scale * gain_ref[row * parts + part]
            ).astype(jnp.bfloat16)
        return carry

    lax.fori_loop(0, owners, norm, 0)
    pl.semaphore_wait(barrier, 1)

    copies = []
    for index in range(count):
        loads[index].wait()
        sent[index] = jnp.dot(normed[...], weights[index], preferred_element_type=jnp.float32)
        copies.append(
            pltpu.make_async_remote_copy(
                src_ref=sent.at[index],
                dst_ref=got.at[index],
                send_sem=send_sem.at[index],
                recv_sem=recv_sem.at[index],
                device_id=peer,
                device_id_type=pl.DeviceIdType.MESH,
            )
        )
        copies[-1].start()
    for index in range(count):
        loads[count + index].wait()
        mine[index] = jnp.dot(
            normed[...], weights[count + index], preferred_element_type=jnp.float32
        )

    inner = col - row * parts
    held = jnp.where((inner >= 0) & (inner < parts), 1.0, 0.0).astype(jnp.float32)
    inner = jnp.clip(inner, 0, parts - 1)

    def residual(owner, carry):
        values = half_ref[owner, inner].astype(jnp.float32) * res_ref[...]
        lanes = values[:, :128]
        for group in range(1, width // 128):
            lanes = lanes + values[:, group * 128 : (group + 1) * 128]
        out_ref[pl.ds(pl.multiple_of(owner * rows, rows), rows), :] = lanes * held
        return carry

    lax.fori_loop(0, owners, residual, 0)
    ahead = lax.broadcasted_iota(jnp.int32, (tokens, tokens), 0) >= lax.broadcasted_iota(
        jnp.int32, (tokens, tokens), 1
    )
    allowed = (seg_col_ref[...] == seg_row_ref[...]) & ahead
    bias[...] = jnp.where(allowed, 0.0, -jnp.inf)

    keyval = []
    for index in range(kvs):
        copies[index].wait_recv()
        keyval.append((mine[index] + got[index]).astype(jnp.bfloat16))
    step = 256
    for index in range(queries):
        copies[kvs + index].wait_recv()
        query = (mine[kvs + index] + got[kvs + index]).astype(jnp.bfloat16)
        for inside in range(chunk // HD):
            head = index * (chunk // HD) + inside
            pair = keyval[head * kvs // heads]
            head_cols = head_ref[row, :, head * HD : (head + 1) * HD]
            for begin in range(0, tokens, step):
                end = begin + step
                logits = lax.dot_general(
                    query[begin:end, inside * HD : (inside + 1) * HD],
                    pair[:end, :HD],
                    (((1,), (1,)), ((), ())),
                    preferred_element_type=jnp.float32,
                ) * (1.0 / math.sqrt(HD))
                logits = logits + bias[begin:end, :end]
                expo = jnp.exp(logits - jnp.max(logits, axis=1, keepdims=True))
                probs = (expo / jnp.sum(expo, axis=1, keepdims=True)).astype(jnp.bfloat16)
                attended = jnp.dot(probs, pair[:end, HD:], preferred_element_type=jnp.float32)
                out_ref[begin:end, :] += attended * head_cols
    for one in copies:
        one.wait_send()


def score(half, meansq, gain, w_query, w_keyval, segment, out_head, res_head, heads, kvs):
    owners, parts, rows, width = half.shape
    tokens, depth = owners * rows, parts * width
    count = kvs + heads // 2
    vmem = pl.BlockSpec(memory_space=pltpu.VMEM)
    anyw = pl.BlockSpec(memory_space=pl.ANY)
    cols = gain.shape[0]
    return pl.pallas_call(
        functools.partial(score_kernel, cols, heads, kvs),
        out_shape=jax.ShapeDtypeStruct((tokens, 128), jnp.float32),
        in_specs=[vmem, vmem, vmem, anyw, anyw, vmem, vmem, vmem, vmem],
        out_specs=vmem,
        scratch_shapes=[
            pltpu.VMEM((tokens, depth), jnp.bfloat16),
            pltpu.VMEM((2 * count, depth, 2 * HD), jnp.bfloat16),
            pltpu.VMEM((count, tokens, 2 * HD), jnp.float32),
            pltpu.VMEM((count, tokens, 2 * HD), jnp.float32),
            pltpu.VMEM((count, tokens, 2 * HD), jnp.float32),
            pltpu.VMEM((tokens, tokens), jnp.float32),
            pltpu.SemaphoreType.DMA((2 * count,)),
            pltpu.SemaphoreType.DMA((count,)),
            pltpu.SemaphoreType.DMA((count,)),
        ],
        compiler_params=pltpu.CompilerParams(
            collective_id=2, has_side_effects=True, vmem_limit_bytes=50 * 1024 * 1024
        ),
    )(
        half, meansq, gain, w_query, w_keyval, segment[:, None], segment[None, :],
        out_head.reshape(2, 1, heads * HD), res_head,
    )


def fused_kernel(
    chunks, lengths_any, x_any, gain_any, wq_ref, wkv_ref, head_any, res_any, out_ref,
    lengths_ref, gain_ref, head_ref, res_ref, small_sem, x_ref, placed, sib, comb, yb, own, xb, full, normed, weights, sent, got, mine, keys, values,
    acc, scale, stat, stats, part, held, x_sem, w_sem, sib_send, sib_recv, y_send, y_recv,
    x_send, x_recv, z_send, z_recv, fy_send, fy_recv, fs_send, fs_recv, p_send, p_recv,
    stat_send, stat_recv, held_send, held_recv,
):
    sections, row_count, cols = 4, 2, 4
    count = sections * row_count * cols
    tokens, width = acc.shape[0], x_ref.shape[1]
    high = tokens // chunks
    rows = high // sections
    rolls = lengths_ref.shape[0]
    chunk = 2 * HD
    parts = weights.shape[0] // 2
    sec, row, col = (lax.axis_index(name) for name in ("section", "dp", "mp"))
    core, side = sec % 2, sec // 2
    me = (sec * row_count + row) * cols + col
    rank = jnp.where(row == 0, col, 3 - col)
    sibling = (2 * side + 1 - core, row, col)
    across = 2 * (1 - side) + core
    over_y = (across, row, col)
    over_x = (sec, 1 - row, col)

    def line(target):
        return (sec, row, jnp.where(row == 0, target, 3 - target))

    def half(origin):
        return jnp.where(row == 0, origin, 1 - origin)

    def copy(src, dst, send_sem, recv_sem, device):
        return pltpu.make_async_remote_copy(
            src_ref=src,
            dst_ref=dst,
            send_sem=send_sem,
            recv_sem=recv_sem,
            device_id=device,
            device_id_type=pl.DeviceIdType.MESH,
        )

    load = pltpu.make_async_copy(x_any, x_ref, x_sem)
    load.start()
    small = []
    for index, (src, dst) in enumerate(
        ((lengths_any, lengths_ref), (gain_any, gain_ref), (head_any, head_ref), (res_any, res_ref))
    ):
        small.append(pltpu.make_async_copy(src, dst, small_sem.at[index]))
        small[-1].start()
    kv_first = col * 2
    loads = []
    for turn, where in enumerate((1 - row, row)):
        for index in range(parts):
            if index == 0:
                begin, ref = (kv_first + where) * chunk, wkv_ref
            else:
                begin, ref = where * GROUP * HD + (index - 1) * chunk, wq_ref
            slot = turn * parts + index
            columns = pl.ds(pl.multiple_of(begin, chunk), chunk)
            loads.append(
                pltpu.make_async_copy(ref.at[0, :, columns], weights.at[slot], w_sem.at[slot])
            )
            loads[-1].start()

    barrier = pltpu.get_barrier_semaphore()

    def peer(step):
        return coords((me + step) % count, row_count, cols)

    near = [sibling, over_y, over_x] + [(sec, row, (col + step) % cols) for step in (1, 2, 3)]
    for device in near:
        pl.semaphore_signal(
            barrier, inc=1, device_id=device, device_id_type=pl.DeviceIdType.MESH
        )

    small[0].wait()
    owner = sec * row_count + row
    my_off, my_len, total = 0, 0, 0
    offsets = []
    for index in range(rolls):
        length = lengths_ref[index]
        offsets.append(total)
        total = total + length
        my_off = my_off + jnp.where(index < owner, length, 0)
        my_len = my_len + jnp.where(index == owner, length, 0)

    load.wait()
    limit = x_ref.shape[0]

    def place(begin):
        slots = begin + lax.broadcasted_iota(jnp.int32, (high, limit), 0)
        spots = lax.broadcasted_iota(jnp.int32, (high, limit), 1)
        hit = (slots == my_off + spots) & (spots < my_len)
        rows_here = jnp.dot(
            jnp.where(hit, 1.0, 0.0).astype(jnp.bfloat16), x_ref[...],
            preferred_element_type=jnp.float32,
        )
        return rows_here.astype(jnp.bfloat16).reshape(2, 2, rows, width)

    blocks = tokens // 128

    def squares():
        lines = lax.broadcasted_iota(jnp.int32, (limit, tokens), 1)
        spots = lax.broadcasted_iota(jnp.int32, (limit, tokens), 0)
        hit = (lines == my_off + spots) & (spots < my_len)
        square = jnp.zeros((limit, 128), jnp.float32)
        for group in range(width // 128):
            piece = x_ref[:, group * 128 : (group + 1) * 128].astype(jnp.float32)
            square = square + piece * piece
        moved = jnp.dot(
            jnp.broadcast_to(jnp.sum(jnp.transpose(square), axis=0, keepdims=True), (8, limit)),
            jnp.where(hit, 1.0, 0.0), preferred_element_type=jnp.float32,
            precision=lax.Precision.HIGHEST,
        )
        for block in range(blocks):
            stat[0, block : block + 1] = moved[:1, block * 128 : (block + 1) * 128]

    squares()
    placed[0] = place(0)
    pl.semaphore_wait(barrier, len(near))

    def to_sib(c):
        return copy(placed.at[c, :, 1 - core], sib.at[c], sib_send, sib_recv.at[c], sibling)

    def to_y(c):
        return copy(comb.at[c, 1 - side], yb.at[c], y_send, y_recv.at[c], over_y)

    def to_x(c):
        return copy(own.at[c], xb.at[c], x_send, x_recv.at[c], over_x)

    def dispatch(c):
        @pl.when(c > 0)
        def _():
            placed[c] = place(c * high)

        to_sib(c).start()

    def reduce_pair(c):
        to_sib(c).wait_recv()
        comb[c] = placed[c, :, core] + sib[c]
        to_y(c).start()

    early = rank <= 1
    mine_half = col % 2

    def z_copy(c, origin, target):
        ref = full.at[c, half(origin), sec]
        return copy(ref, ref, z_send, z_recv.at[c, origin], line(target))

    def fy_copy(c, origin, group):
        ref = full.at[c, half(origin), group]
        return copy(ref, ref, fy_send, fy_recv.at[c], over_y)

    def fs_copy(c, group):
        ref = full.at[c, :, group]
        return copy(ref, ref, fs_send, fs_recv.at[c], sibling)

    def gather_own(c):
        to_y(c).wait_recv()
        own[c] = comb[c, side] + yb[c]

        @pl.when(rank >= 2)
        def _():
            to_x(c).start()

    def land(c):
        @pl.when(early)
        def _():
            to_x(c).wait_recv()
            full[c, mine_half, sec] = own[c] + xb[c]

        @pl.when(rank == 0)
        def _():
            z_copy(c, 0, 1).start()
            fy_copy(c, 0, sec).start()

        @pl.when(rank == 1)
        def _():
            z_copy(c, 1, 2).start()
            z_copy(c, 1, 0).start()
            fy_copy(c, 1, sec).start()

    def pass_on(c, at):
        for origin in (1, 0):
            if at == origin:
                continue
            z_copy(c, origin, origin).wait_recv()
            if at in (1, 2):
                z_copy(c, origin, at + 1).start()
            fy_copy(c, origin, sec).start()
        fs_copy(c, sec).start()

    def to_both(c):
        both = full.at[c, :, across]
        copy(both, both, fy_send, fy_recv.at[c], over_y).wait_recv()
        fs_copy(c, across).start()

    rounds = (sibling, over_y, over_x, near[3 + 1], (sec, row, col + 1 - 2 * (col % 2)))

    def stat_copy(turn):
        return copy(
            stat.at[turn], stats.at[turn], stat_send.at[turn], stat_recv.at[turn], rounds[turn]
        )

    def stat_round(turn):
        if turn:
            stat_copy(turn - 1).wait_recv()
            stat[turn] = stat[turn - 1] + stats[turn - 1]
        stat_copy(turn).start()

    keys[...] = jnp.zeros_like(keys)
    values[...] = jnp.zeros_like(values)

    def ready():
        for one in small[1:]:
            one.wait()
        last = len(rounds) - 1
        stat_copy(last).wait_recv()
        mean = (stat[last] + stats[last]) / (cols * width)
        factor = lax.rsqrt(mean + EPS)
        for block in range(blocks):
            wide = jnp.broadcast_to(factor[block : block + 1], (128, 128))
            scale[block * 128 : (block + 1) * 128] = jnp.transpose(wide)

    def exchange(c):
        return copy(sent.at[c], got.at[c], p_send, p_recv.at[c], over_x)

    def project(c):
        both = full.at[c, :, pl.ds(0, 2)]
        copy(both, both, fs_send, fs_recv.at[c], sibling).wait_recv()
        here = pl.ds(pl.multiple_of(c * high, high), high)
        factor = scale[here, :][:, :1]

        @pl.when(c == 0)
        def _():
            for one in loads:
                one.wait()

        for part_index in range(2):
            piece = full[c, part_index].reshape(high, width).astype(jnp.float32)
            normed[:, part_index * width : (part_index + 1) * width] = (
                piece * factor * gain_ref[row * 2 + part_index]
            ).astype(jnp.bfloat16)
        for index in range(parts):
            sent[c, index] = jnp.dot(
                normed[...], weights[index], preferred_element_type=jnp.float32
            )
        exchange(c).start()
        for index in range(parts):
            mine[c, index] = jnp.dot(
                normed[...], weights[parts + index], preferred_element_type=jnp.float32
            )

        acc[here] = jnp.zeros((high, 128), jnp.float32)

        @pl.when(early)
        def _():
            piece = full[c, mine_half].reshape(high, width).astype(jnp.float32) * res_ref[...]
            lanes = piece[:, :128]
            for group in range(1, width // 128):
                lanes = lanes + piece[:, group * 128 : (group + 1) * 128]
            acc[here] = lanes

    def attend(c):
        exchange(c).wait_recv()

        @pl.when(2 * c < chunks)
        def _():
            attend_to(c, tokens // 2)

        @pl.when(2 * c >= chunks)
        def _():
            attend_to(c, tokens)

    def attend_to(c, end):
        here = pl.ds(pl.multiple_of(c * high, high), high)
        pair = (mine[c, 0] + got[c, 0]).astype(jnp.bfloat16)
        keys[here] = pair[:, :HD]
        values[here] = pair[:, HD:]
        heads = []
        for index in range(1, parts):
            both = (mine[c, index] + got[c, index]).astype(jnp.bfloat16)
            heads += [both[:, :HD], both[:, HD:]]
        query = jnp.concatenate(heads, axis=0)
        logits = lax.dot_general(
            query, keys[:end], (((1,), (1,)), ((), ())), preferred_element_type=jnp.float32
        ) * (1.0 / math.sqrt(HD))
        slots = c * high + lax.broadcasted_iota(jnp.int32, (high, end), 0)
        spots = lax.broadcasted_iota(jnp.int32, (high, end), 1)
        start = jnp.zeros((high, end), jnp.int32)
        for offset in offsets[1:]:
            start = jnp.where(slots >= offset, offset, start)
        allowed = (spots >= start) & (spots <= slots)
        bias = jnp.where(allowed, 0.0, -jnp.inf)
        logits = logits + jnp.concatenate([bias] * len(heads), axis=0)
        expo = jnp.exp(logits - jnp.max(logits, axis=1, keepdims=True))
        probs = (expo / jnp.sum(expo, axis=1, keepdims=True)).astype(jnp.bfloat16)
        attended = jnp.dot(probs, values[:end], preferred_element_type=jnp.float32)
        lanes = acc[here]
        for head in range(len(heads)):
            lanes = lanes + attended[head * high : (head + 1) * high] * head_ref[
                row, :, head * HD : (head + 1) * HD
            ]
        acc[here] = lanes

    lags = (4, 4, 5, 6)
    first = ((dispatch, 0), (reduce_pair, 1), (gather_own, 2), (land, 3))
    later = ((project, 8), (attend, 10))

    def at_lag(k, lag, stage):
        @pl.when((k >= lag) & (k < chunks + lag))
        def _():
            stage(k - lag)

    def step(k, carry):
        for stage, lag in first:
            at_lag(k, lag, stage)
        for turn in range(len(rounds)):
            @pl.when(k == (1, 2, 3, 4, 6)[turn])
            def _():
                stat_round(turn)

        for at in range(cols):
            @pl.when(rank == at)
            def _():
                at_lag(k, lags[at], lambda c: pass_on(c, at))
                at_lag(k, lags[at] + 1, to_both)

        pl.when(k == later[0][1])(ready)
        for stage, lag in later:
            at_lag(k, lag, stage)
        return carry

    lax.fori_loop(0, chunks + later[-1][1], step, 0)

    for block in range(blocks):
        lanes = acc[block * 128 : (block + 1) * 128]
        part[block : block + 1] = jnp.sum(jnp.transpose(lanes), axis=0, keepdims=True)

    for other in range(1, count):
        copy(part, held.at[me], held_send, held_recv, peer(other)).start()
    held[me] = part[...]

    def sent_all(ref, sem):
        copy(ref, ref, sem, sem, sibling).wait_send()

    sent_all(sib, sib_send)
    sent_all(yb, y_send)
    sent_all(comb, fy_send)
    sent_all(placed, fs_send)
    sent_all(sent, p_send)

    @pl.when(rank >= 2)
    def _():
        sent_all(xb, x_send)

    for at in range(3):
        @pl.when(rank == at)
        def _():
            sent_all(full.at[:, 0, pl.ds(0, (1, 3, 2)[at])], z_send)

    for turn in range(len(rounds)):
        stat_copy(turn).wait_send()
    slots = lax.broadcasted_iota(jnp.int32, (tokens, limit), 0)
    spots = lax.broadcasted_iota(jnp.int32, (tokens, limit), 1)
    hit = (slots == my_off + spots) & (spots < my_len)
    picks = jnp.where(hit, 1.0, 0.0).astype(jnp.bfloat16)
    others = held.at[pl.ds(0, count - 1)]
    copy(others, others, held_send, held_recv, sibling).wait()
    totals = []
    for section in range(sections):
        begin = section * row_count * cols
        totals.append(jnp.sum(held[begin : begin + row_count * cols], axis=0))
    home = jnp.concatenate(
        [
            jnp.concatenate([one[block : block + 1] for one in totals], axis=0)
            for block in range(blocks)
        ],
        axis=1,
    )
    result = jnp.zeros((sections, limit), jnp.float32)
    for _ in range(3):
        piece = home.astype(jnp.bfloat16)
        home = home - piece.astype(jnp.float32)
        result = result + jnp.dot(piece, picks, preferred_element_type=jnp.float32)
    out_ref[...] = result


def fused(rollouts, lengths, gain, w_query, w_keyval, out_head, res_head, chunks):
    limit, width = rollouts.shape[1:]
    depth = w_query.shape[1]
    tokens = lengths.shape[0] * limit // 4
    high = tokens // chunks
    rows = high // 4
    vmem = pl.BlockSpec(memory_space=pltpu.VMEM)
    hbm = pl.BlockSpec(memory_space=pltpu.HBM)
    bf16, f32, dma = jnp.bfloat16, jnp.float32, pltpu.SemaphoreType.DMA
    parts = 3
    one, each = (), (chunks,)
    sems = [one, each] * 3 + [one, (chunks, 2)] + [one, each] * 3 + [(5,)] * 2 + [one] * 2
    out = pl.pallas_call(
        functools.partial(fused_kernel, chunks),
        out_shape=jax.ShapeDtypeStruct((4, limit), f32),
        in_specs=[hbm] * 7,
        out_specs=vmem,
        scratch_shapes=[
            pltpu.SMEM(lengths.shape, jnp.int32),
            pltpu.VMEM(gain.shape, f32),
            pltpu.VMEM((2, 1, GROUP * HD), f32),
            pltpu.VMEM(res_head.shape, f32),
            dma((4,)),
            pltpu.VMEM((limit, width), bf16),
            pltpu.VMEM((chunks, 2, 2, rows, width), bf16),
            pltpu.VMEM((chunks, 2, rows, width), bf16),
            pltpu.VMEM((chunks, 2, rows, width), bf16),
            pltpu.VMEM((chunks, rows, width), bf16),
            pltpu.VMEM((chunks, rows, width), bf16),
            pltpu.VMEM((chunks, rows, width), bf16),
            pltpu.VMEM((chunks, 2, 4, rows, width), bf16),
            pltpu.VMEM((high, depth), bf16),
            pltpu.VMEM((2 * parts, depth, 2 * HD), bf16),
            pltpu.VMEM((chunks, parts, high, 2 * HD), f32),
            pltpu.VMEM((chunks, parts, high, 2 * HD), f32),
            pltpu.VMEM((chunks, parts, high, 2 * HD), f32),
            pltpu.VMEM((tokens, HD), bf16),
            pltpu.VMEM((tokens, HD), bf16),
            pltpu.VMEM((tokens, 128), f32),
            pltpu.VMEM((tokens, 128), f32),
            pltpu.VMEM((5, tokens // 128, 128), f32),
            pltpu.VMEM((5, tokens // 128, 128), f32),
            pltpu.VMEM((tokens // 128, 128), f32),
            pltpu.VMEM((32, tokens // 128, 128), f32),
            dma,
            dma((2 * parts,)),
        ]
        + [dma(size) if size else dma for size in sems],
        compiler_params=pltpu.CompilerParams(
            collective_id=3, has_side_effects=True, vmem_limit_bytes=62 * 1024 * 1024
        ),
    )(
        lengths, rollouts.reshape(limit, width), gain, w_query, w_keyval,
        out_head.reshape(2, 1, GROUP * HD), res_head,
    )
    return out.reshape(4, 1, limit)


def plain(half, meansq, gains, w_query, w_keyval, segment, out_head, res_head):
    owners, _, rows, local_width = half.shape
    tokens = owners * rows
    row_count, cols = lax.axis_size("dp"), lax.axis_size("mp")
    my_row, my_col = lax.axis_index("dp"), lax.axis_index("mp")
    slots = jnp.arange(tokens, dtype=jnp.int32)
    scale_row = lax.rsqrt(meansq[:, None, :, :1] + EPS)
    parts = cols // row_count
    gain = lax.dynamic_slice_in_dim(gains, my_row * parts, parts, 0)
    normed = (half.astype(jnp.float32) * scale_row * gain[None]).astype(jnp.bfloat16)

    heads_here = w_query.shape[2] // HD
    kv_here = max(1, heads_here // GROUP)
    kv_first = my_col * heads_here // GROUP
    w_kv = lax.dynamic_slice_in_dim(w_keyval[0], kv_first * 2 * HD, kv_here * 2 * HD, 1)
    q_part, kv_part = 0.0, 0.0
    for part in range(parts):
        rows = normed[:, part].reshape(tokens, local_width)
        begin = part * local_width
        end = begin + local_width
        q_part += jnp.dot(rows, w_query[0, begin:end], preferred_element_type=jnp.float32)
        kv_part += jnp.dot(rows, w_kv[begin:end], preferred_element_type=jnp.float32)
    heads, kvs = heads_here, kv_here
    summed = lax.psum(jnp.concatenate([q_part, kv_part], axis=1), "dp")
    head_cols = out_head[0]
    weight = (my_row == 0).astype(jnp.float32)
    summed = summed.astype(jnp.bfloat16)
    query = summed[:, : heads * HD].reshape(tokens, kvs, heads // kvs, HD)
    keyval = summed[:, heads * HD :].reshape(tokens, kvs, 2, HD)
    logits = jnp.einsum(
        "qkgd,skd->kgqs", query, keyval[:, :, 0, :], preferred_element_type=jnp.float32
    ) * (1.0 / math.sqrt(HD))
    allowed = (segment[:, None] == segment[None, :]) & (slots[None, :] <= slots[:, None])
    logits = jnp.where(allowed, logits, -jnp.inf)
    expo = jnp.exp(logits - jnp.max(logits, axis=-1, keepdims=True))
    probs = (expo / jnp.sum(expo, axis=-1, keepdims=True)).astype(jnp.bfloat16)
    attended = jnp.einsum(
        "kgqs,skd->qkgd", probs, keyval[:, :, 1, :], preferred_element_type=jnp.float32
    ).reshape(tokens, heads * HD)
    inner = my_col - my_row * parts
    res_in = lax.dynamic_index_in_dim(half, jnp.clip(inner, 0, parts - 1), 1, keepdims=False)
    res_sum = jnp.sum(
        res_in.reshape(tokens, local_width).astype(jnp.float32) * res_head[0][None, :], axis=1
    )
    res_sum = jnp.where((inner >= 0) & (inner < parts), res_sum, 0.0)
    return weight * jnp.sum(attended * head_cols[None, :], axis=1) + res_sum


def body(rollouts, lengths, norm_gain, w_query, w_keyval, out_head, res_head):
    roll_count, max_len, local_width = rollouts.shape
    sections, row_count, cols = (lax.axis_size(name) for name in ("section", "dp", "mp"))
    if (sections, row_count, cols, roll_count) == (4, 2, 4, 1) and w_query.shape[2] == 8 * HD:
        gains = norm_gain[0].reshape(cols, 1, local_width)
        return fused(rollouts, lengths, gains, w_query, w_keyval, out_head, res_head, CHUNKS)
    owner = lax.axis_index(OWN)
    total_rolls = lengths.shape[0]
    tokens = total_rolls * max_len // 4

    ids = jnp.arange(total_rolls, dtype=jnp.int32)
    offsets = jnp.sum(jnp.where(ids[None, :] < ids[:, None], lengths[None, :], 0), axis=1)
    slots = jnp.arange(tokens, dtype=jnp.int32)
    segment = jnp.sum((slots[:, None] >= offsets[None, :]).astype(jnp.int32), axis=1)

    position = jnp.arange(max_len, dtype=jnp.int32)
    mine = owner * roll_count + jnp.arange(roll_count, dtype=jnp.int32)
    my_off = jnp.sum(jnp.where(ids[None, :] == mine[:, None], offsets[None, :], 0), axis=1)
    my_len = jnp.sum(jnp.where(ids[None, :] == mine[:, None], lengths[None, :], 0), axis=1)
    place = (
        (slots[:, None, None] == my_off[None, :, None] + position[None, None, :])
        & (position[None, None, :] < my_len[None, :, None])
    ).astype(jnp.bfloat16)
    placed = jnp.dot(
        place.reshape(tokens, roll_count * max_len),
        rollouts.reshape(roll_count * max_len, local_width),
        preferred_element_type=jnp.float32,
    ).astype(jnp.bfloat16)
    half, meansq = spread(placed, sections, row_count, cols)
    heads_here = w_query.shape[2] // HD
    gains = norm_gain[0].reshape(cols, 1, local_width)
    if row_count == 2 and heads_here % (2 * GROUP) == 0 and tokens % 256 == 0:
        lanes = score(
            half, meansq, gains, w_query, w_keyval, segment, out_head, res_head,
            heads_here // 2, heads_here // 2 // GROUP,
        )
        partial = jnp.sum(lanes, axis=1)
    else:
        partial = plain(
            half, meansq, gains, w_query, w_keyval, segment, out_head, res_head
        )
    home = share(partial, sections, row_count, cols)
    home = jnp.pad(home, ((0, 0), (0, max_len)))
    lines = []
    for local in range(roll_count):
        line = lax.dynamic_slice_in_dim(home, my_off[local], max_len, 1)
        lines.append(jnp.where(position[None, :] < my_len[local], line, 0.0))
    return jnp.stack(lines, axis=1)


def solution(mesh):
    in_specs = (
        P(("section", "dp"), None, "mp"),
        P(),
        P("section", None),
        P("section", "dp", "mp"),
        P("section", "dp", None),
        P("section", "mp"),
        P("section", "mp"),
    )
    out_specs = P(None, ("section", "dp"), None)
    return jax.shard_map(body, mesh=mesh, in_specs=in_specs, out_specs=out_specs, check_vma=False)
```

```python
import functools
import math

import jax
import jax.numpy as jnp
from jax import lax
from jax.experimental import pallas as pl
from jax.experimental.pallas import tpu as pltpu
from jax.sharding import PartitionSpec as P

HD = 128
KV = 8
HEADS = 32
GROUP = HEADS // KV
EPS = 1e-05
CHUNKS = 8
OWN = ("section", "dp")


def coords(index, row_count, cols):
    return (index // (row_count * cols), index // cols % row_count, index % cols)


def share_kernel(sections, row_count, cols, part_ref, out_ref, held, send_sem, recv_sem):
    count = sections * row_count * cols
    me = (lax.axis_index("section") * row_count + lax.axis_index("dp")) * cols
    me = me + lax.axis_index("mp")
    barrier = pltpu.get_barrier_semaphore()

    def peer(step):
        return coords((me + step) % count, row_count, cols)

    def greet(step, carry):
        pl.semaphore_signal(
            barrier, inc=1, device_id=peer(step), device_id_type=pl.DeviceIdType.MESH
        )
        return carry

    lax.fori_loop(1, count, greet, 0)
    pl.semaphore_wait(barrier, count - 1)

    def copy(step):
        return pltpu.make_async_remote_copy(
            src_ref=part_ref,
            dst_ref=held.at[me],
            send_sem=send_sem.at[step],
            recv_sem=recv_sem.at[step],
            device_id=peer(step),
            device_id_type=pl.DeviceIdType.MESH,
        )

    def send(step, carry):
        copy(step).start()
        return carry

    def finish(step, carry):
        copy(step).wait()
        return carry

    lax.fori_loop(1, count, send, 0)
    held[me] = part_ref[...]
    lax.fori_loop(1, count, finish, 0)
    for section in range(sections):
        begin = section * row_count * cols
        out_ref[section] = jnp.sum(held[begin : begin + row_count * cols], axis=0)


def share(partial, sections, row_count, cols):
    rows = partial.shape[0] // 128
    count = sections * row_count * cols
    return pl.pallas_call(
        functools.partial(share_kernel, sections, row_count, cols),
        out_shape=jax.ShapeDtypeStruct((sections, rows, 128), jnp.float32),
        in_specs=[pl.BlockSpec(memory_space=pltpu.VMEM)],
        out_specs=pl.BlockSpec(memory_space=pltpu.VMEM),
        scratch_shapes=[
            pltpu.VMEM((count, rows, 128), jnp.float32),
            pltpu.SemaphoreType.DMA((count,)),
            pltpu.SemaphoreType.DMA((count,)),
        ],
        compiler_params=pltpu.CompilerParams(collective_id=0, has_side_effects=True),
    )(partial.reshape(rows, 128)).reshape(sections, rows * 128)


def spread_kernel(
    sections, row_count, cols, placed_ref, out_ref, stat_ref, sib, comb, got, allm, *sems
):
    pair_send, pair_recv, swap_send, swap_recv, col_send, col_recv = sems[:6]
    half_send, half_recv, stat_send, stat_recv, fwd_send, fwd_recv, fst_send, fst_recv = sems[6:]
    pairs, parts = sections // 2, cols // row_count
    sec, row, col = (lax.axis_index(name) for name in ("section", "dp", "mp"))
    par, pair = sec % 2, sec // 2
    sibling = (2 * pair + 1 - par, row, col)
    count = pairs * row_count

    def target(step):
        return (pair + step // row_count) % pairs, (row + step % row_count) % row_count

    def source(step):
        far = (pair + pairs - step // row_count) % pairs
        return (2 * far + par) * row_count + (row + row_count - step % row_count) % row_count

    def plane(step):
        far, line = target(step)
        return (2 * far + par, line, col)

    def column(step):
        return (sec, row, (col + step) % cols)

    def copy(src, dst, send_sem, recv_sem, device):
        return pltpu.make_async_remote_copy(
            src_ref=src,
            dst_ref=dst,
            send_sem=send_sem,
            recv_sem=recv_sem,
            device_id=device,
            device_id_type=pl.DeviceIdType.MESH,
        )

    barrier = pltpu.get_barrier_semaphore()
    others = [sibling]
    others += [plane(step) for step in range(1, count)]
    others += [column(step) for step in range(1, cols)]
    for device in others:
        pl.semaphore_signal(
            barrier, inc=1, device_id=device, device_id_type=pl.DeviceIdType.MESH
        )
    pl.semaphore_wait(barrier, len(others))

    to_pair = [
        copy(
            placed_ref.at[far, 1 - par], sib.at[far], pair_send.at[far], pair_recv.at[far], sibling
        )
        for far in range(pairs)
    ]
    for one in to_pair:
        one.start()
    for far in range(pairs):
        to_pair[far].wait_recv()
        comb[far] = placed_ref[far, par] + sib[far]

    chunks = 4
    high = allm.shape[1] // chunks
    spans = [pl.ds(chunk * high, high) for chunk in range(chunks)]
    place = pair * row_count + row
    me = sec * row_count + row
    swaps = [[] for _ in spans]
    gathers = [[] for _ in spans]
    halves = [[] for _ in spans]
    stats = [[] for _ in spans]
    forwards = []

    for chunk, span in enumerate(spans):
        for step in range(1, count):
            far, line = target(step)
            slot = chunk * count + step
            swaps[chunk].append(
                copy(
                    comb.at[far, line, span], got.at[place, span],
                    swap_send.at[slot], swap_recv.at[slot], plane(step),
                )
            )
            swaps[chunk][-1].start()
    got[place] = comb[pair, row]

    for chunk, span in enumerate(spans):
        for one in swaps[chunk]:
            one.wait_recv()
        total = got[0, span]
        for index in range(1, count):
            total = total + got[index, span]
        allm[col, span] = total
        for step in range(1, cols):
            slot = chunk * cols + step
            gathers[chunk].append(
                copy(
                    allm.at[col, span], allm.at[col, span],
                    col_send.at[slot], col_recv.at[slot], column(step),
                )
            )
            gathers[chunk][-1].start()

    for chunk, span in enumerate(spans):
        for one in gathers[chunk]:
            one.wait_recv()
        for step in range(1, count):
            far, line = target(step)
            slot = chunk * count + step
            halves[chunk].append(
                copy(
                    allm.at[pl.ds(line * parts, parts), span], out_ref.at[me, :, span],
                    half_send.at[slot], half_recv.at[slot], plane(step),
                )
            )
            halves[chunk][-1].start()
        out_ref[me, :, span] = allm[pl.ds(row * parts, parts), span]
        slot = chunk * count
        forwards.append(
            copy(
                out_ref.at[me, :, span], out_ref.at[me, :, span],
                fwd_send.at[slot], fwd_recv.at[slot], sibling,
            )
        )
        forwards[-1].start()
        square = jnp.zeros((high, 1), jnp.float32)
        for index in range(cols):
            values = allm[index, span].astype(jnp.float32)
            square += jnp.sum(values * values, axis=1, keepdims=True)
        square = square / (cols * allm.shape[2])
        stat_ref[me, span] = jnp.broadcast_to(square, (high, 128))
        for step in range(1, count):
            slot = chunk * count + step
            stats[chunk].append(
                copy(
                    stat_ref.at[me, span], stat_ref.at[me, span],
                    stat_send.at[slot], stat_recv.at[slot], plane(step),
                )
            )
            stats[chunk][-1].start()
        slot = chunk * count
        forwards.append(
            copy(
                stat_ref.at[me, span], stat_ref.at[me, span],
                fst_send.at[slot], fst_recv.at[slot], sibling,
            )
        )
        forwards[-1].start()
    for chunk, span in enumerate(spans):
        for step in range(1, count):
            origin = source(step)
            slot = chunk * count + step
            halves[chunk][step - 1].wait_recv()
            forwards.append(
                copy(
                    out_ref.at[origin, :, span], out_ref.at[origin, :, span],
                    fwd_send.at[slot], fwd_recv.at[slot], sibling,
                )
            )
            forwards[-1].start()
            stats[chunk][step - 1].wait_recv()
            forwards.append(
                copy(
                    stat_ref.at[origin, span], stat_ref.at[origin, span],
                    fst_send.at[slot], fst_recv.at[slot], sibling,
                )
            )
            forwards[-1].start()
    for one in forwards:
        one.wait()
    for one in to_pair + sum(swaps + gathers + halves + stats, []):
        one.wait_send()


def spread(placed, sections, row_count, cols):
    owners = sections * row_count
    rows, width = placed.shape[0] // owners, placed.shape[1]
    pairs, count = sections // 2, sections // 2 * row_count
    parts = cols // row_count
    sizes = [pairs] * 2 + [4 * count] * 2 + [4 * cols] * 2 + [4 * count] * 8
    return pl.pallas_call(
        functools.partial(spread_kernel, sections, row_count, cols),
        out_shape=(
            jax.ShapeDtypeStruct((owners, parts, rows, width), jnp.bfloat16),
            jax.ShapeDtypeStruct((owners, rows, 128), jnp.float32),
        ),
        in_specs=[pl.BlockSpec(memory_space=pltpu.VMEM)],
        out_specs=(
            pl.BlockSpec(memory_space=pltpu.VMEM),
            pl.BlockSpec(memory_space=pltpu.VMEM),
        ),
        scratch_shapes=[
            pltpu.VMEM((pairs, row_count, rows, width), jnp.bfloat16),
            pltpu.VMEM((pairs, row_count, rows, width), jnp.bfloat16),
            pltpu.VMEM((count, rows, width), jnp.bfloat16),
            pltpu.VMEM((cols, rows, width), jnp.bfloat16),
        ]
        + [pltpu.SemaphoreType.DMA((size,)) for size in sizes],
        compiler_params=pltpu.CompilerParams(
            collective_id=1, has_side_effects=True, vmem_limit_bytes=40 * 1024 * 1024
        ),
    )(placed.reshape(pairs, 2, row_count, rows, width))


def score_kernel(
    cols, heads, kvs, half_ref, meansq_ref, gain_ref, wq_ref, wkv_ref, seg_col_ref, seg_row_ref,
    head_ref, res_ref, out_ref, normed, weights, mine, sent, got, bias, w_sem, send_sem, recv_sem
):
    owners, parts, rows, width = half_ref.shape
    tokens = owners * rows
    sec, row, col = (lax.axis_index(name) for name in ("section", "dp", "mp"))
    peer = (sec, 1 - row, col)
    chunk = 2 * HD
    queries = heads * HD // chunk
    count = kvs + queries
    kv_first = col * 2 * heads // GROUP

    barrier = pltpu.get_barrier_semaphore()
    pl.semaphore_signal(barrier, inc=1, device_id=peer, device_id_type=pl.DeviceIdType.MESH)

    loads = []
    for turn, line in enumerate((1 - row, row)):
        for index in range(count):
            if index < kvs:
                begin, ref = (kv_first + line * kvs + index) * chunk, wkv_ref
            else:
                begin, ref = line * heads * HD + (index - kvs) * chunk, wq_ref
            slot = turn * count + index
            columns = pl.ds(pl.multiple_of(begin, chunk), chunk)
            loads.append(
                pltpu.make_async_copy(ref.at[0, :, columns], weights.at[slot], w_sem.at[slot])
            )
            loads[-1].start()

    def norm(owner, carry):
        scale = lax.rsqrt(meansq_ref[owner][:, :1] + EPS)
        spot = pl.ds(pl.multiple_of(owner * rows, rows), rows)
        for part in range(parts):
            values = half_ref[owner, part].astype(jnp.float32)
            normed[spot, part * width : (part + 1) * width] = (
                values * scale * gain_ref[row * parts + part]
            ).astype(jnp.bfloat16)
        return carry

    lax.fori_loop(0, owners, norm, 0)
    pl.semaphore_wait(barrier, 1)

    copies = []
    for index in range(count):
        loads[index].wait()
        sent[index] = jnp.dot(normed[...], weights[index], preferred_element_type=jnp.float32)
        copies.append(
            pltpu.make_async_remote_copy(
                src_ref=sent.at[index],
                dst_ref=got.at[index],
                send_sem=send_sem.at[index],
                recv_sem=recv_sem.at[index],
                device_id=peer,
                device_id_type=pl.DeviceIdType.MESH,
            )
        )
        copies[-1].start()
    for index in range(count):
        loads[count + index].wait()
        mine[index] = jnp.dot(
            normed[...], weights[count + index], preferred_element_type=jnp.float32
        )

    inner = col - row * parts
    held = jnp.where((inner >= 0) & (inner < parts), 1.0, 0.0).astype(jnp.float32)
    inner = jnp.clip(inner, 0, parts - 1)

    def residual(owner, carry):
        values = half_ref[owner, inner].astype(jnp.float32) * res_ref[...]
        lanes = values[:, :128]
        for group in range(1, width // 128):
            lanes = lanes + values[:, group * 128 : (group + 1) * 128]
        out_ref[pl.ds(pl.multiple_of(owner * rows, rows), rows), :] = lanes * held
        return carry

    lax.fori_loop(0, owners, residual, 0)
    ahead = lax.broadcasted_iota(jnp.int32, (tokens, tokens), 0) >= lax.broadcasted_iota(
        jnp.int32, (tokens, tokens), 1
    )
    allowed = (seg_col_ref[...] == seg_row_ref[...]) & ahead
    bias[...] = jnp.where(allowed, 0.0, -jnp.inf)

    keyval = []
    for index in range(kvs):
        copies[index].wait_recv()
        keyval.append((mine[index] + got[index]).astype(jnp.bfloat16))
    step = 256
    for index in range(queries):
        copies[kvs + index].wait_recv()
        query = (mine[kvs + index] + got[kvs + index]).astype(jnp.bfloat16)
        for inside in range(chunk // HD):
            head = index * (chunk // HD) + inside
            pair = keyval[head * kvs // heads]
            head_cols = head_ref[row, :, head * HD : (head + 1) * HD]
            for begin in range(0, tokens, step):
                end = begin + step
                logits = lax.dot_general(
                    query[begin:end, inside * HD : (inside + 1) * HD],
                    pair[:end, :HD],
                    (((1,), (1,)), ((), ())),
                    preferred_element_type=jnp.float32,
                ) * (1.0 / math.sqrt(HD))
                logits = logits + bias[begin:end, :end]
                expo = jnp.exp(logits - jnp.max(logits, axis=1, keepdims=True))
                probs = (expo / jnp.sum(expo, axis=1, keepdims=True)).astype(jnp.bfloat16)
                attended = jnp.dot(probs, pair[:end, HD:], preferred_element_type=jnp.float32)
                out_ref[begin:end, :] += attended * head_cols
    for one in copies:
        one.wait_send()


def score(half, meansq, gain, w_query, w_keyval, segment, out_head, res_head, heads, kvs):
    owners, parts, rows, width = half.shape
    tokens, depth = owners * rows, parts * width
    count = kvs + heads // 2
    vmem = pl.BlockSpec(memory_space=pltpu.VMEM)
    anyw = pl.BlockSpec(memory_space=pl.ANY)
    cols = gain.shape[0]
    return pl.pallas_call(
        functools.partial(score_kernel, cols, heads, kvs),
        out_shape=jax.ShapeDtypeStruct((tokens, 128), jnp.float32),
        in_specs=[vmem, vmem, vmem, anyw, anyw, vmem, vmem, vmem, vmem],
        out_specs=vmem,
        scratch_shapes=[
            pltpu.VMEM((tokens, depth), jnp.bfloat16),
            pltpu.VMEM((2 * count, depth, 2 * HD), jnp.bfloat16),
            pltpu.VMEM((count, tokens, 2 * HD), jnp.float32),
            pltpu.VMEM((count, tokens, 2 * HD), jnp.float32),
            pltpu.VMEM((count, tokens, 2 * HD), jnp.float32),
            pltpu.VMEM((tokens, tokens), jnp.float32),
            pltpu.SemaphoreType.DMA((2 * count,)),
            pltpu.SemaphoreType.DMA((count,)),
            pltpu.SemaphoreType.DMA((count,)),
        ],
        compiler_params=pltpu.CompilerParams(
            collective_id=2, has_side_effects=True, vmem_limit_bytes=50 * 1024 * 1024
        ),
    )(
        half, meansq, gain, w_query, w_keyval, segment[:, None], segment[None, :],
        out_head.reshape(2, 1, heads * HD), res_head,
    )


def fused_kernel(
    chunks, lengths_any, x_any, gain_any, wq_ref, wkv_ref, head_any, res_any, out_ref,
    lengths_ref, gain_ref, head_ref, res_ref, small_sem, x_ref, placed, sib, comb, yb, own, xb, full, normed, weights, sent, got, mine, keys, values,
    acc, scale, stat, stats, part, held, x_sem, w_sem, sib_send, sib_recv, y_send, y_recv,
    x_send, x_recv, z_send, z_recv, fy_send, fy_recv, fs_send, fs_recv, p_send, p_recv,
    stat_send, stat_recv, held_send, held_recv,
):
    sections, row_count, cols = 4, 2, 4
    count = sections * row_count * cols
    tokens, width = acc.shape[0], x_ref.shape[1]
    high = tokens // chunks
    rows = high // sections
    rolls = lengths_ref.shape[0]
    chunk = 2 * HD
    parts = weights.shape[0] // 2
    sec, row, col = (lax.axis_index(name) for name in ("section", "dp", "mp"))
    core, side = sec % 2, sec // 2
    me = (sec * row_count + row) * cols + col
    rank = jnp.where(row == 0, col, 3 - col)
    sibling = (2 * side + 1 - core, row, col)
    across = 2 * (1 - side) + core
    over_y = (across, row, col)
    over_x = (sec, 1 - row, col)

    def line(target):
        return (sec, row, jnp.where(row == 0, target, 3 - target))

    def half(origin):
        return jnp.where(row == 0, origin, 1 - origin)

    def copy(src, dst, send_sem, recv_sem, device):
        return pltpu.make_async_remote_copy(
            src_ref=src,
            dst_ref=dst,
            send_sem=send_sem,
            recv_sem=recv_sem,
            device_id=device,
            device_id_type=pl.DeviceIdType.MESH,
        )

    load = pltpu.make_async_copy(x_any, x_ref, x_sem)
    load.start()
    small = []
    for index, (src, dst) in enumerate(
        ((lengths_any, lengths_ref), (gain_any, gain_ref), (head_any, head_ref), (res_any, res_ref))
    ):
        small.append(pltpu.make_async_copy(src, dst, small_sem.at[index]))
        small[-1].start()
    kv_first = col * 2
    loads = []
    for turn, where in enumerate((1 - row, row)):
        for index in range(parts):
            if index == 0:
                begin, ref = (kv_first + where) * chunk, wkv_ref
            else:
                begin, ref = where * GROUP * HD + (index - 1) * chunk, wq_ref
            slot = turn * parts + index
            columns = pl.ds(pl.multiple_of(begin, chunk), chunk)
            loads.append(
                pltpu.make_async_copy(ref.at[0, :, columns], weights.at[slot], w_sem.at[slot])
            )

    barrier = pltpu.get_barrier_semaphore()

    def peer(step):
        return coords((me + step) % count, row_count, cols)

    near = [sibling, over_y, over_x] + [(sec, row, (col + step) % cols) for step in (1, 2, 3)]
    for device in near:
        pl.semaphore_signal(
            barrier, inc=1, device_id=device, device_id_type=pl.DeviceIdType.MESH
        )

    small[0].wait()
    owner = sec * row_count + row
    my_off, my_len, total = 0, 0, 0
    offsets = []
    for index in range(rolls):
        length = lengths_ref[index]
        offsets.append(total)
        total = total + length
        my_off = my_off + jnp.where(index < owner, length, 0)
        my_len = my_len + jnp.where(index == owner, length, 0)

    load.wait()
    limit = x_ref.shape[0]

    def place(begin):
        slots = begin + lax.broadcasted_iota(jnp.int32, (high, limit), 0)
        spots = lax.broadcasted_iota(jnp.int32, (high, limit), 1)
        hit = (slots == my_off + spots) & (spots < my_len)
        rows_here = jnp.dot(
            jnp.where(hit, 1.0, 0.0).astype(jnp.bfloat16), x_ref[...],
            preferred_element_type=jnp.float32,
        )
        return rows_here.astype(jnp.bfloat16).reshape(2, 2, rows, width)

    blocks = tokens // 128

    def squares():
        lines = lax.broadcasted_iota(jnp.int32, (limit, tokens), 1)
        spots = lax.broadcasted_iota(jnp.int32, (limit, tokens), 0)
        hit = (lines == my_off + spots) & (spots < my_len)
        square = jnp.zeros((limit, 128), jnp.float32)
        for group in range(width // 128):
            piece = x_ref[:, group * 128 : (group + 1) * 128].astype(jnp.float32)
            square = square + piece * piece
        moved = jnp.dot(
            jnp.broadcast_to(jnp.sum(jnp.transpose(square), axis=0, keepdims=True), (8, limit)),
            jnp.where(hit, 1.0, 0.0), preferred_element_type=jnp.float32,
            precision=lax.Precision.HIGHEST,
        )
        for block in range(blocks):
            stat[0, block : block + 1] = moved[:1, block * 128 : (block + 1) * 128]

    placed[0] = place(0)
    pl.semaphore_wait(barrier, len(near))

    def to_sib(c):
        return copy(placed.at[c, :, 1 - core], sib.at[c], sib_send, sib_recv.at[c], sibling)

    def to_y(c):
        return copy(comb.at[c, 1 - side], yb.at[c], y_send, y_recv.at[c], over_y)

    def to_x(c):
        return copy(own.at[c], xb.at[c], x_send, x_recv.at[c], over_x)

    def dispatch(c):
        @pl.when(c > 0)
        def _():
            placed[c] = place(c * high)

        to_sib(c).start()

    def reduce_pair(c):
        to_sib(c).wait_recv()
        comb[c] = placed[c, :, core] + sib[c]
        to_y(c).start()

    early = rank <= 1
    mine_half = col % 2

    def z_copy(c, origin, target):
        ref = full.at[c, half(origin), sec]
        return copy(ref, ref, z_send, z_recv.at[c, origin], line(target))

    def fy_copy(c, origin, group):
        ref = full.at[c, half(origin), group]
        return copy(ref, ref, fy_send, fy_recv.at[c], over_y)

    def fs_copy(c, group):
        ref = full.at[c, :, group]
        return copy(ref, ref, fs_send, fs_recv.at[c], sibling)

    def gather_own(c):
        to_y(c).wait_recv()
        own[c] = comb[c, side] + yb[c]

        @pl.when(rank >= 2)
        def _():
            to_x(c).start()

    def land(c):
        @pl.when(early)
        def _():
            to_x(c).wait_recv()
            full[c, mine_half, sec] = own[c] + xb[c]

        @pl.when(rank == 0)
        def _():
            z_copy(c, 0, 1).start()
            fy_copy(c, 0, sec).start()

        @pl.when(rank == 1)
        def _():
            z_copy(c, 1, 2).start()
            z_copy(c, 1, 0).start()
            fy_copy(c, 1, sec).start()

    def pass_on(c, at):
        for origin in (1, 0):
            if at == origin:
                continue
            z_copy(c, origin, origin).wait_recv()
            if at in (1, 2):
                z_copy(c, origin, at + 1).start()
            fy_copy(c, origin, sec).start()
        fs_copy(c, sec).start()

    def to_both(c):
        both = full.at[c, :, across]
        copy(both, both, fy_send, fy_recv.at[c], over_y).wait_recv()
        fs_copy(c, across).start()

    rounds = (sibling, over_y, over_x, near[3 + 1], (sec, row, col + 1 - 2 * (col % 2)))

    def stat_copy(turn):
        return copy(
            stat.at[turn], stats.at[turn], stat_send.at[turn], stat_recv.at[turn], rounds[turn]
        )

    def stat_round(turn):
        if turn:
            stat_copy(turn - 1).wait_recv()
            stat[turn] = stat[turn - 1] + stats[turn - 1]
        else:
            squares()
        stat_copy(turn).start()

    keys[...] = jnp.zeros_like(keys)
    values[...] = jnp.zeros_like(values)

    def ready():
        for one in small[1:]:
            one.wait()
        last = len(rounds) - 1
        stat_copy(last).wait_recv()
        mean = (stat[last] + stats[last]) / (cols * width)
        factor = lax.rsqrt(mean + EPS)
        for block in range(blocks):
            wide = jnp.broadcast_to(factor[block : block + 1], (128, 128))
            scale[block * 128 : (block + 1) * 128] = jnp.transpose(wide)

    def exchange(c):
        return copy(sent.at[c], got.at[c], p_send, p_recv.at[c], over_x)

    def project(c):
        both = full.at[c, :, pl.ds(0, 2)]
        copy(both, both, fs_send, fs_recv.at[c], sibling).wait_recv()
        here = pl.ds(pl.multiple_of(c * high, high), high)
        factor = scale[here, :][:, :1]

        @pl.when(c == 0)
        def _():
            for one in loads:
                one.wait()

        for part_index in range(2):
            piece = full[c, part_index].reshape(high, width).astype(jnp.float32)
            normed[:, part_index * width : (part_index + 1) * width] = (
                piece * factor * gain_ref[row * 2 + part_index]
            ).astype(jnp.bfloat16)
        for index in range(parts):
            sent[c, index] = jnp.dot(
                normed[...], weights[index], preferred_element_type=jnp.float32
            )
        exchange(c).start()
        for index in range(parts):
            mine[c, index] = jnp.dot(
                normed[...], weights[parts + index], preferred_element_type=jnp.float32
            )

        acc[here] = jnp.zeros((high, 128), jnp.float32)

        @pl.when(early)
        def _():
            piece = full[c, mine_half].reshape(high, width).astype(jnp.float32) * res_ref[...]
            lanes = piece[:, :128]
            for group in range(1, width // 128):
                lanes = lanes + piece[:, group * 128 : (group + 1) * 128]
            acc[here] = lanes

    def attend(c):
        exchange(c).wait_recv()

        @pl.when(2 * c < chunks)
        def _():
            attend_to(c, tokens // 2)

        @pl.when(2 * c >= chunks)
        def _():
            attend_to(c, tokens)

    def attend_to(c, end):
        here = pl.ds(pl.multiple_of(c * high, high), high)
        pair = (mine[c, 0] + got[c, 0]).astype(jnp.bfloat16)
        keys[here] = pair[:, :HD]
        values[here] = pair[:, HD:]
        heads = []
        for index in range(1, parts):
            both = (mine[c, index] + got[c, index]).astype(jnp.bfloat16)
            heads += [both[:, :HD], both[:, HD:]]
        query = jnp.concatenate(heads, axis=0)
        logits = lax.dot_general(
            query, keys[:end], (((1,), (1,)), ((), ())), preferred_element_type=jnp.float32
        ) * (1.0 / math.sqrt(HD))
        slots = c * high + lax.broadcasted_iota(jnp.int32, (high, end), 0)
        spots = lax.broadcasted_iota(jnp.int32, (high, end), 1)
        start = jnp.zeros((high, end), jnp.int32)
        for offset in offsets[1:]:
            start = jnp.where(slots >= offset, offset, start)
        allowed = (spots >= start) & (spots <= slots)
        bias = jnp.where(allowed, 0.0, -jnp.inf)
        logits = logits + jnp.concatenate([bias] * len(heads), axis=0)
        expo = jnp.exp(logits - jnp.max(logits, axis=1, keepdims=True))
        probs = (expo / jnp.sum(expo, axis=1, keepdims=True)).astype(jnp.bfloat16)
        attended = jnp.dot(probs, values[:end], preferred_element_type=jnp.float32)
        lanes = acc[here]
        for head in range(len(heads)):
            lanes = lanes + attended[head * high : (head + 1) * high] * head_ref[
                row, :, head * HD : (head + 1) * HD
            ]
        acc[here] = lanes

    lags = (4, 4, 5, 6)
    first = ((dispatch, 0), (reduce_pair, 1), (gather_own, 2), (land, 3))
    later = ((project, 8), (attend, 10))

    def at_lag(k, lag, stage):
        @pl.when((k >= lag) & (k < chunks + lag))
        def _():
            stage(k - lag)

    def publish(begin, end):
        for block in range(begin, end):
            lanes = acc[block * 128 : (block + 1) * 128]
            part[block : block + 1] = jnp.sum(jnp.transpose(lanes), axis=0, keepdims=True)
        span = pl.ds(begin, end - begin)
        for other in range(1, count):
            copy(part.at[span], held.at[me, span], held_send, held_recv, peer(other)).start()

    def step(k, carry):
        for stage, lag in first:
            at_lag(k, lag, stage)
        for turn in range(len(rounds)):
            @pl.when(k == (3, 4, 5, 6, 7)[turn])
            def _():
                stat_round(turn)

        @pl.when(k == 1)
        def _():
            for one in loads:
                one.start()

        for at in range(cols):
            @pl.when(rank == at)
            def _():
                at_lag(k, lags[at], lambda c: pass_on(c, at))
                at_lag(k, lags[at] + 1, to_both)

        pl.when(k == later[0][1])(ready)
        pl.when(k == later[1][1] + chunks - chunks // blocks)(lambda: publish(0, blocks - 1))
        for stage, lag in later:
            at_lag(k, lag, stage)
        return carry

    lax.fori_loop(0, chunks + later[-1][1], step, 0)

    publish(blocks - 1, blocks)
    held[me] = part[...]

    def sent_all(ref, sem):
        copy(ref, ref, sem, sem, sibling).wait_send()

    sent_all(sib, sib_send)
    sent_all(yb, y_send)
    sent_all(comb, fy_send)
    sent_all(placed, fs_send)
    sent_all(sent, p_send)

    @pl.when(rank >= 2)
    def _():
        sent_all(xb, x_send)

    for at in range(3):
        @pl.when(rank == at)
        def _():
            sent_all(full.at[:, 0, pl.ds(0, (1, 3, 2)[at])], z_send)

    for turn in range(len(rounds)):
        stat_copy(turn).wait_send()
    slots = lax.broadcasted_iota(jnp.int32, (tokens, limit), 0)
    spots = lax.broadcasted_iota(jnp.int32, (tokens, limit), 1)
    hit = (slots == my_off + spots) & (spots < my_len)
    picks = jnp.where(hit, 1.0, 0.0).astype(jnp.bfloat16)
    others = held.at[pl.ds(0, count - 1)]
    copy(others, others, held_send, held_recv, sibling).wait()
    totals = []
    for section in range(sections):
        begin = section * row_count * cols
        totals.append(jnp.sum(held[begin : begin + row_count * cols], axis=0))
    home = jnp.concatenate(
        [
            jnp.concatenate([one[block : block + 1] for one in totals], axis=0)
            for block in range(blocks)
        ],
        axis=1,
    )
    result = jnp.zeros((sections, limit), jnp.float32)
    for _ in range(3):
        piece = home.astype(jnp.bfloat16)
        home = home - piece.astype(jnp.float32)
        result = result + jnp.dot(piece, picks, preferred_element_type=jnp.float32)
    out_ref[...] = result


def fused(rollouts, lengths, gain, w_query, w_keyval, out_head, res_head, chunks):
    limit, width = rollouts.shape[1:]
    depth = w_query.shape[1]
    tokens = lengths.shape[0] * limit // 4
    high = tokens // chunks
    rows = high // 4
    vmem = pl.BlockSpec(memory_space=pltpu.VMEM)
    hbm = pl.BlockSpec(memory_space=pltpu.HBM)
    bf16, f32, dma = jnp.bfloat16, jnp.float32, pltpu.SemaphoreType.DMA
    parts = 3
    one, each = (), (chunks,)
    sems = [one, each] * 3 + [one, (chunks, 2)] + [one, each] * 3 + [(5,)] * 2 + [one] * 2
    out = pl.pallas_call(
        functools.partial(fused_kernel, chunks),
        out_shape=jax.ShapeDtypeStruct((4, limit), f32),
        in_specs=[hbm] * 7,
        out_specs=vmem,
        scratch_shapes=[
            pltpu.SMEM(lengths.shape, jnp.int32),
            pltpu.VMEM(gain.shape, f32),
            pltpu.VMEM((2, 1, GROUP * HD), f32),
            pltpu.VMEM(res_head.shape, f32),
            dma((4,)),
            pltpu.VMEM((limit, width), bf16),
            pltpu.VMEM((chunks, 2, 2, rows, width), bf16),
            pltpu.VMEM((chunks, 2, rows, width), bf16),
            pltpu.VMEM((chunks, 2, rows, width), bf16),
            pltpu.VMEM((chunks, rows, width), bf16),
            pltpu.VMEM((chunks, rows, width), bf16),
            pltpu.VMEM((chunks, rows, width), bf16),
            pltpu.VMEM((chunks, 2, 4, rows, width), bf16),
            pltpu.VMEM((high, depth), bf16),
            pltpu.VMEM((2 * parts, depth, 2 * HD), bf16),
            pltpu.VMEM((chunks, parts, high, 2 * HD), f32),
            pltpu.VMEM((chunks, parts, high, 2 * HD), f32),
            pltpu.VMEM((chunks, parts, high, 2 * HD), f32),
            pltpu.VMEM((tokens, HD), bf16),
            pltpu.VMEM((tokens, HD), bf16),
            pltpu.VMEM((tokens, 128), f32),
            pltpu.VMEM((tokens, 128), f32),
            pltpu.VMEM((5, tokens // 128, 128), f32),
            pltpu.VMEM((5, tokens // 128, 128), f32),
            pltpu.VMEM((tokens // 128, 128), f32),
            pltpu.VMEM((32, tokens // 128, 128), f32),
            dma,
            dma((2 * parts,)),
        ]
        + [dma(size) if size else dma for size in sems],
        compiler_params=pltpu.CompilerParams(
            collective_id=3, has_side_effects=True, vmem_limit_bytes=62 * 1024 * 1024
        ),
    )(
        lengths, rollouts.reshape(limit, width), gain, w_query, w_keyval,
        out_head.reshape(2, 1, GROUP * HD), res_head,
    )
    return out.reshape(4, 1, limit)


def plain(half, meansq, gains, w_query, w_keyval, segment, out_head, res_head):
    owners, _, rows, local_width = half.shape
    tokens = owners * rows
    row_count, cols = lax.axis_size("dp"), lax.axis_size("mp")
    my_row, my_col = lax.axis_index("dp"), lax.axis_index("mp")
    slots = jnp.arange(tokens, dtype=jnp.int32)
    scale_row = lax.rsqrt(meansq[:, None, :, :1] + EPS)
    parts = cols // row_count
    gain = lax.dynamic_slice_in_dim(gains, my_row * parts, parts, 0)
    normed = (half.astype(jnp.float32) * scale_row * gain[None]).astype(jnp.bfloat16)

    heads_here = w_query.shape[2] // HD
    kv_here = max(1, heads_here // GROUP)
    kv_first = my_col * heads_here // GROUP
    w_kv = lax.dynamic_slice_in_dim(w_keyval[0], kv_first * 2 * HD, kv_here * 2 * HD, 1)
    q_part, kv_part = 0.0, 0.0
    for part in range(parts):
        rows = normed[:, part].reshape(tokens, local_width)
        begin = part * local_width
        end = begin + local_width
        q_part += jnp.dot(rows, w_query[0, begin:end], preferred_element_type=jnp.float32)
        kv_part += jnp.dot(rows, w_kv[begin:end], preferred_element_type=jnp.float32)
    heads, kvs = heads_here, kv_here
    summed = lax.psum(jnp.concatenate([q_part, kv_part], axis=1), "dp")
    head_cols = out_head[0]
    weight = (my_row == 0).astype(jnp.float32)
    summed = summed.astype(jnp.bfloat16)
    query = summed[:, : heads * HD].reshape(tokens, kvs, heads // kvs, HD)
    keyval = summed[:, heads * HD :].reshape(tokens, kvs, 2, HD)
    logits = jnp.einsum(
        "qkgd,skd->kgqs", query, keyval[:, :, 0, :], preferred_element_type=jnp.float32
    ) * (1.0 / math.sqrt(HD))
    allowed = (segment[:, None] == segment[None, :]) & (slots[None, :] <= slots[:, None])
    logits = jnp.where(allowed, logits, -jnp.inf)
    expo = jnp.exp(logits - jnp.max(logits, axis=-1, keepdims=True))
    probs = (expo / jnp.sum(expo, axis=-1, keepdims=True)).astype(jnp.bfloat16)
    attended = jnp.einsum(
        "kgqs,skd->qkgd", probs, keyval[:, :, 1, :], preferred_element_type=jnp.float32
    ).reshape(tokens, heads * HD)
    inner = my_col - my_row * parts
    res_in = lax.dynamic_index_in_dim(half, jnp.clip(inner, 0, parts - 1), 1, keepdims=False)
    res_sum = jnp.sum(
        res_in.reshape(tokens, local_width).astype(jnp.float32) * res_head[0][None, :], axis=1
    )
    res_sum = jnp.where((inner >= 0) & (inner < parts), res_sum, 0.0)
    return weight * jnp.sum(attended * head_cols[None, :], axis=1) + res_sum


def body(rollouts, lengths, norm_gain, w_query, w_keyval, out_head, res_head):
    roll_count, max_len, local_width = rollouts.shape
    sections, row_count, cols = (lax.axis_size(name) for name in ("section", "dp", "mp"))
    if (sections, row_count, cols, roll_count) == (4, 2, 4, 1) and w_query.shape[2] == 8 * HD:
        gains = norm_gain[0].reshape(cols, 1, local_width)
        return fused(rollouts, lengths, gains, w_query, w_keyval, out_head, res_head, CHUNKS)
    owner = lax.axis_index(OWN)
    total_rolls = lengths.shape[0]
    tokens = total_rolls * max_len // 4

    ids = jnp.arange(total_rolls, dtype=jnp.int32)
    offsets = jnp.sum(jnp.where(ids[None, :] < ids[:, None], lengths[None, :], 0), axis=1)
    slots = jnp.arange(tokens, dtype=jnp.int32)
    segment = jnp.sum((slots[:, None] >= offsets[None, :]).astype(jnp.int32), axis=1)

    position = jnp.arange(max_len, dtype=jnp.int32)
    mine = owner * roll_count + jnp.arange(roll_count, dtype=jnp.int32)
    my_off = jnp.sum(jnp.where(ids[None, :] == mine[:, None], offsets[None, :], 0), axis=1)
    my_len = jnp.sum(jnp.where(ids[None, :] == mine[:, None], lengths[None, :], 0), axis=1)
    place = (
        (slots[:, None, None] == my_off[None, :, None] + position[None, None, :])
        & (position[None, None, :] < my_len[None, :, None])
    ).astype(jnp.bfloat16)
    placed = jnp.dot(
        place.reshape(tokens, roll_count * max_len),
        rollouts.reshape(roll_count * max_len, local_width),
        preferred_element_type=jnp.float32,
    ).astype(jnp.bfloat16)
    half, meansq = spread(placed, sections, row_count, cols)
    heads_here = w_query.shape[2] // HD
    gains = norm_gain[0].reshape(cols, 1, local_width)
    if row_count == 2 and heads_here % (2 * GROUP) == 0 and tokens % 256 == 0:
        lanes = score(
            half, meansq, gains, w_query, w_keyval, segment, out_head, res_head,
            heads_here // 2, heads_here // 2 // GROUP,
        )
        partial = jnp.sum(lanes, axis=1)
    else:
        partial = plain(
            half, meansq, gains, w_query, w_keyval, segment, out_head, res_head
        )
    home = share(partial, sections, row_count, cols)
    home = jnp.pad(home, ((0, 0), (0, max_len)))
    lines = []
    for local in range(roll_count):
        line = lax.dynamic_slice_in_dim(home, my_off[local], max_len, 1)
        lines.append(jnp.where(position[None, :] < my_len[local], line, 0.0))
    return jnp.stack(lines, axis=1)


def solution(mesh):
    in_specs = (
        P(("section", "dp"), None, "mp"),
        P(),
        P("section", None),
        P("section", "dp", "mp"),
        P("section", "dp", None),
        P("section", "mp"),
        P("section", "mp"),
    )
    out_specs = P(None, ("section", "dp"), None)
    return jax.shard_map(body, mesh=mesh, in_specs=in_specs, out_specs=out_specs, check_vma=False)
```

```python
import functools
import math

import jax
import jax.numpy as jnp
from jax import lax
from jax.experimental import pallas as pl
from jax.experimental.pallas import tpu as pltpu
from jax.sharding import PartitionSpec as P

HD = 128
KV = 8
HEADS = 32
GROUP = HEADS // KV
EPS = 1e-05
CHUNKS = 8
OWN = ("section", "dp")


def coords(index, row_count, cols):
    return (index // (row_count * cols), index // cols % row_count, index % cols)


def share_kernel(sections, row_count, cols, part_ref, out_ref, held, send_sem, recv_sem):
    count = sections * row_count * cols
    me = (lax.axis_index("section") * row_count + lax.axis_index("dp")) * cols
    me = me + lax.axis_index("mp")
    barrier = pltpu.get_barrier_semaphore()

    def peer(step):
        return coords((me + step) % count, row_count, cols)

    def greet(step, carry):
        pl.semaphore_signal(
            barrier, inc=1, device_id=peer(step), device_id_type=pl.DeviceIdType.MESH
        )
        return carry

    lax.fori_loop(1, count, greet, 0)
    pl.semaphore_wait(barrier, count - 1)

    def copy(step):
        return pltpu.make_async_remote_copy(
            src_ref=part_ref,
            dst_ref=held.at[me],
            send_sem=send_sem.at[step],
            recv_sem=recv_sem.at[step],
            device_id=peer(step),
            device_id_type=pl.DeviceIdType.MESH,
        )

    def send(step, carry):
        copy(step).start()
        return carry

    def finish(step, carry):
        copy(step).wait()
        return carry

    lax.fori_loop(1, count, send, 0)
    held[me] = part_ref[...]
    lax.fori_loop(1, count, finish, 0)
    for section in range(sections):
        begin = section * row_count * cols
        out_ref[section] = jnp.sum(held[begin : begin + row_count * cols], axis=0)


def share(partial, sections, row_count, cols):
    rows = partial.shape[0] // 128
    count = sections * row_count * cols
    return pl.pallas_call(
        functools.partial(share_kernel, sections, row_count, cols),
        out_shape=jax.ShapeDtypeStruct((sections, rows, 128), jnp.float32),
        in_specs=[pl.BlockSpec(memory_space=pltpu.VMEM)],
        out_specs=pl.BlockSpec(memory_space=pltpu.VMEM),
        scratch_shapes=[
            pltpu.VMEM((count, rows, 128), jnp.float32),
            pltpu.SemaphoreType.DMA((count,)),
            pltpu.SemaphoreType.DMA((count,)),
        ],
        compiler_params=pltpu.CompilerParams(collective_id=0, has_side_effects=True),
    )(partial.reshape(rows, 128)).reshape(sections, rows * 128)


def spread_kernel(
    sections, row_count, cols, placed_ref, out_ref, stat_ref, sib, comb, got, allm, *sems
):
    pair_send, pair_recv, swap_send, swap_recv, col_send, col_recv = sems[:6]
    half_send, half_recv, stat_send, stat_recv, fwd_send, fwd_recv, fst_send, fst_recv = sems[6:]
    pairs, parts = sections // 2, cols // row_count
    sec, row, col = (lax.axis_index(name) for name in ("section", "dp", "mp"))
    par, pair = sec % 2, sec // 2
    sibling = (2 * pair + 1 - par, row, col)
    count = pairs * row_count

    def target(step):
        return (pair + step // row_count) % pairs, (row + step % row_count) % row_count

    def source(step):
        far = (pair + pairs - step // row_count) % pairs
        return (2 * far + par) * row_count + (row + row_count - step % row_count) % row_count

    def plane(step):
        far, line = target(step)
        return (2 * far + par, line, col)

    def column(step):
        return (sec, row, (col + step) % cols)

    def copy(src, dst, send_sem, recv_sem, device):
        return pltpu.make_async_remote_copy(
            src_ref=src,
            dst_ref=dst,
            send_sem=send_sem,
            recv_sem=recv_sem,
            device_id=device,
            device_id_type=pl.DeviceIdType.MESH,
        )

    barrier = pltpu.get_barrier_semaphore()
    others = [sibling]
    others += [plane(step) for step in range(1, count)]
    others += [column(step) for step in range(1, cols)]
    for device in others:
        pl.semaphore_signal(
            barrier, inc=1, device_id=device, device_id_type=pl.DeviceIdType.MESH
        )
    pl.semaphore_wait(barrier, len(others))

    to_pair = [
        copy(
            placed_ref.at[far, 1 - par], sib.at[far], pair_send.at[far], pair_recv.at[far], sibling
        )
        for far in range(pairs)
    ]
    for one in to_pair:
        one.start()
    for far in range(pairs):
        to_pair[far].wait_recv()
        comb[far] = placed_ref[far, par] + sib[far]

    chunks = 4
    high = allm.shape[1] // chunks
    spans = [pl.ds(chunk * high, high) for chunk in range(chunks)]
    place = pair * row_count + row
    me = sec * row_count + row
    swaps = [[] for _ in spans]
    gathers = [[] for _ in spans]
    halves = [[] for _ in spans]
    stats = [[] for _ in spans]
    forwards = []

    for chunk, span in enumerate(spans):
        for step in range(1, count):
            far, line = target(step)
            slot = chunk * count + step
            swaps[chunk].append(
                copy(
                    comb.at[far, line, span], got.at[place, span],
                    swap_send.at[slot], swap_recv.at[slot], plane(step),
                )
            )
            swaps[chunk][-1].start()
    got[place] = comb[pair, row]

    for chunk, span in enumerate(spans):
        for one in swaps[chunk]:
            one.wait_recv()
        total = got[0, span]
        for index in range(1, count):
            total = total + got[index, span]
        allm[col, span] = total
        for step in range(1, cols):
            slot = chunk * cols + step
            gathers[chunk].append(
                copy(
                    allm.at[col, span], allm.at[col, span],
                    col_send.at[slot], col_recv.at[slot], column(step),
                )
            )
            gathers[chunk][-1].start()

    for chunk, span in enumerate(spans):
        for one in gathers[chunk]:
            one.wait_recv()
        for step in range(1, count):
            far, line = target(step)
            slot = chunk * count + step
            halves[chunk].append(
                copy(
                    allm.at[pl.ds(line * parts, parts), span], out_ref.at[me, :, span],
                    half_send.at[slot], half_recv.at[slot], plane(step),
                )
            )
            halves[chunk][-1].start()
        out_ref[me, :, span] = allm[pl.ds(row * parts, parts), span]
        slot = chunk * count
        forwards.append(
            copy(
                out_ref.at[me, :, span], out_ref.at[me, :, span],
                fwd_send.at[slot], fwd_recv.at[slot], sibling,
            )
        )
        forwards[-1].start()
        square = jnp.zeros((high, 1), jnp.float32)
        for index in range(cols):
            values = allm[index, span].astype(jnp.float32)
            square += jnp.sum(values * values, axis=1, keepdims=True)
        square = square / (cols * allm.shape[2])
        stat_ref[me, span] = jnp.broadcast_to(square, (high, 128))
        for step in range(1, count):
            slot = chunk * count + step
            stats[chunk].append(
                copy(
                    stat_ref.at[me, span], stat_ref.at[me, span],
                    stat_send.at[slot], stat_recv.at[slot], plane(step),
                )
            )
            stats[chunk][-1].start()
        slot = chunk * count
        forwards.append(
            copy(
                stat_ref.at[me, span], stat_ref.at[me, span],
                fst_send.at[slot], fst_recv.at[slot], sibling,
            )
        )
        forwards[-1].start()
    for chunk, span in enumerate(spans):
        for step in range(1, count):
            origin = source(step)
            slot = chunk * count + step
            halves[chunk][step - 1].wait_recv()
            forwards.append(
                copy(
                    out_ref.at[origin, :, span], out_ref.at[origin, :, span],
                    fwd_send.at[slot], fwd_recv.at[slot], sibling,
                )
            )
            forwards[-1].start()
            stats[chunk][step - 1].wait_recv()
            forwards.append(
                copy(
                    stat_ref.at[origin, span], stat_ref.at[origin, span],
                    fst_send.at[slot], fst_recv.at[slot], sibling,
                )
            )
            forwards[-1].start()
    for one in forwards:
        one.wait()
    for one in to_pair + sum(swaps + gathers + halves + stats, []):
        one.wait_send()


def spread(placed, sections, row_count, cols):
    owners = sections * row_count
    rows, width = placed.shape[0] // owners, placed.shape[1]
    pairs, count = sections // 2, sections // 2 * row_count
    parts = cols // row_count
    sizes = [pairs] * 2 + [4 * count] * 2 + [4 * cols] * 2 + [4 * count] * 8
    return pl.pallas_call(
        functools.partial(spread_kernel, sections, row_count, cols),
        out_shape=(
            jax.ShapeDtypeStruct((owners, parts, rows, width), jnp.bfloat16),
            jax.ShapeDtypeStruct((owners, rows, 128), jnp.float32),
        ),
        in_specs=[pl.BlockSpec(memory_space=pltpu.VMEM)],
        out_specs=(
            pl.BlockSpec(memory_space=pltpu.VMEM),
            pl.BlockSpec(memory_space=pltpu.VMEM),
        ),
        scratch_shapes=[
            pltpu.VMEM((pairs, row_count, rows, width), jnp.bfloat16),
            pltpu.VMEM((pairs, row_count, rows, width), jnp.bfloat16),
            pltpu.VMEM((count, rows, width), jnp.bfloat16),
            pltpu.VMEM((cols, rows, width), jnp.bfloat16),
        ]
        + [pltpu.SemaphoreType.DMA((size,)) for size in sizes],
        compiler_params=pltpu.CompilerParams(
            collective_id=1, has_side_effects=True, vmem_limit_bytes=40 * 1024 * 1024
        ),
    )(placed.reshape(pairs, 2, row_count, rows, width))


def score_kernel(
    cols, heads, kvs, half_ref, meansq_ref, gain_ref, wq_ref, wkv_ref, seg_col_ref, seg_row_ref,
    head_ref, res_ref, out_ref, normed, weights, mine, sent, got, bias, w_sem, send_sem, recv_sem
):
    owners, parts, rows, width = half_ref.shape
    tokens = owners * rows
    sec, row, col = (lax.axis_index(name) for name in ("section", "dp", "mp"))
    peer = (sec, 1 - row, col)
    chunk = 2 * HD
    queries = heads * HD // chunk
    count = kvs + queries
    kv_first = col * 2 * heads // GROUP

    barrier = pltpu.get_barrier_semaphore()
    pl.semaphore_signal(barrier, inc=1, device_id=peer, device_id_type=pl.DeviceIdType.MESH)

    loads = []
    for turn, line in enumerate((1 - row, row)):
        for index in range(count):
            if index < kvs:
                begin, ref = (kv_first + line * kvs + index) * chunk, wkv_ref
            else:
                begin, ref = line * heads * HD + (index - kvs) * chunk, wq_ref
            slot = turn * count + index
            columns = pl.ds(pl.multiple_of(begin, chunk), chunk)
            loads.append(
                pltpu.make_async_copy(ref.at[0, :, columns], weights.at[slot], w_sem.at[slot])
            )
            loads[-1].start()

    def norm(owner, carry):
        scale = lax.rsqrt(meansq_ref[owner][:, :1] + EPS)
        spot = pl.ds(pl.multiple_of(owner * rows, rows), rows)
        for part in range(parts):
            values = half_ref[owner, part].astype(jnp.float32)
            normed[spot, part * width : (part + 1) * width] = (
                values * scale * gain_ref[row * parts + part]
            ).astype(jnp.bfloat16)
        return carry

    lax.fori_loop(0, owners, norm, 0)
    pl.semaphore_wait(barrier, 1)

    copies = []
    for index in range(count):
        loads[index].wait()
        sent[index] = jnp.dot(normed[...], weights[index], preferred_element_type=jnp.float32)
        copies.append(
            pltpu.make_async_remote_copy(
                src_ref=sent.at[index],
                dst_ref=got.at[index],
                send_sem=send_sem.at[index],
                recv_sem=recv_sem.at[index],
                device_id=peer,
                device_id_type=pl.DeviceIdType.MESH,
            )
        )
        copies[-1].start()
    for index in range(count):
        loads[count + index].wait()
        mine[index] = jnp.dot(
            normed[...], weights[count + index], preferred_element_type=jnp.float32
        )

    inner = col - row * parts
    held = jnp.where((inner >= 0) & (inner < parts), 1.0, 0.0).astype(jnp.float32)
    inner = jnp.clip(inner, 0, parts - 1)

    def residual(owner, carry):
        values = half_ref[owner, inner].astype(jnp.float32) * res_ref[...]
        lanes = values[:, :128]
        for group in range(1, width // 128):
            lanes = lanes + values[:, group * 128 : (group + 1) * 128]
        out_ref[pl.ds(pl.multiple_of(owner * rows, rows), rows), :] = lanes * held
        return carry

    lax.fori_loop(0, owners, residual, 0)
    ahead = lax.broadcasted_iota(jnp.int32, (tokens, tokens), 0) >= lax.broadcasted_iota(
        jnp.int32, (tokens, tokens), 1
    )
    allowed = (seg_col_ref[...] == seg_row_ref[...]) & ahead
    bias[...] = jnp.where(allowed, 0.0, -jnp.inf)

    keyval = []
    for index in range(kvs):
        copies[index].wait_recv()
        keyval.append((mine[index] + got[index]).astype(jnp.bfloat16))
    step = 256
    for index in range(queries):
        copies[kvs + index].wait_recv()
        query = (mine[kvs + index] + got[kvs + index]).astype(jnp.bfloat16)
        for inside in range(chunk // HD):
            head = index * (chunk // HD) + inside
            pair = keyval[head * kvs // heads]
            head_cols = head_ref[row, :, head * HD : (head + 1) * HD]
            for begin in range(0, tokens, step):
                end = begin + step
                logits = lax.dot_general(
                    query[begin:end, inside * HD : (inside + 1) * HD],
                    pair[:end, :HD],
                    (((1,), (1,)), ((), ())),
                    preferred_element_type=jnp.float32,
                ) * (1.0 / math.sqrt(HD))
                logits = logits + bias[begin:end, :end]
                expo = jnp.exp(logits - jnp.max(logits, axis=1, keepdims=True))
                probs = (expo / jnp.sum(expo, axis=1, keepdims=True)).astype(jnp.bfloat16)
                attended = jnp.dot(probs, pair[:end, HD:], preferred_element_type=jnp.float32)
                out_ref[begin:end, :] += attended * head_cols
    for one in copies:
        one.wait_send()


def score(half, meansq, gain, w_query, w_keyval, segment, out_head, res_head, heads, kvs):
    owners, parts, rows, width = half.shape
    tokens, depth = owners * rows, parts * width
    count = kvs + heads // 2
    vmem = pl.BlockSpec(memory_space=pltpu.VMEM)
    anyw = pl.BlockSpec(memory_space=pl.ANY)
    cols = gain.shape[0]
    return pl.pallas_call(
        functools.partial(score_kernel, cols, heads, kvs),
        out_shape=jax.ShapeDtypeStruct((tokens, 128), jnp.float32),
        in_specs=[vmem, vmem, vmem, anyw, anyw, vmem, vmem, vmem, vmem],
        out_specs=vmem,
        scratch_shapes=[
            pltpu.VMEM((tokens, depth), jnp.bfloat16),
            pltpu.VMEM((2 * count, depth, 2 * HD), jnp.bfloat16),
            pltpu.VMEM((count, tokens, 2 * HD), jnp.float32),
            pltpu.VMEM((count, tokens, 2 * HD), jnp.float32),
            pltpu.VMEM((count, tokens, 2 * HD), jnp.float32),
            pltpu.VMEM((tokens, tokens), jnp.float32),
            pltpu.SemaphoreType.DMA((2 * count,)),
            pltpu.SemaphoreType.DMA((count,)),
            pltpu.SemaphoreType.DMA((count,)),
        ],
        compiler_params=pltpu.CompilerParams(
            collective_id=2, has_side_effects=True, vmem_limit_bytes=50 * 1024 * 1024
        ),
    )(
        half, meansq, gain, w_query, w_keyval, segment[:, None], segment[None, :],
        out_head.reshape(2, 1, heads * HD), res_head,
    )


def fused_kernel(
    chunks, lengths_any, x_any, gain_any, wq_ref, wkv_ref, head_any, res_any, out_ref,
    lengths_ref, gain_ref, head_ref, res_ref, small_sem, x_ref, placed, sib, comb, yb, own, xb, full, normed, weights, sent, got, mine, keys, values,
    acc, scale, stat, stats, part, held, x_sem, w_sem, sib_send, sib_recv, y_send, y_recv,
    x_send, x_recv, z_send, z_recv, fy_send, fy_recv, fs_send, fs_recv, p_send, p_recv,
    stat_send, stat_recv, held_send, held_recv,
):
    sections, row_count, cols = 4, 2, 4
    count = sections * row_count * cols
    tokens, width = acc.shape[0], x_ref.shape[1]
    high = tokens // chunks
    rows = high // sections
    rolls = lengths_ref.shape[0]
    chunk = 2 * HD
    parts = weights.shape[0] // 2
    sec, row, col = (lax.axis_index(name) for name in ("section", "dp", "mp"))
    core, side = sec % 2, sec // 2
    me = (sec * row_count + row) * cols + col
    rank = jnp.where(row == 0, col, 3 - col)
    sibling = (2 * side + 1 - core, row, col)
    across = 2 * (1 - side) + core
    over_y = (across, row, col)
    over_x = (sec, 1 - row, col)

    def line(target):
        return (sec, row, jnp.where(row == 0, target, 3 - target))

    def half(origin):
        return jnp.where(row == 0, origin, 1 - origin)

    def copy(src, dst, send_sem, recv_sem, device):
        return pltpu.make_async_remote_copy(
            src_ref=src,
            dst_ref=dst,
            send_sem=send_sem,
            recv_sem=recv_sem,
            device_id=device,
            device_id_type=pl.DeviceIdType.MESH,
        )

    load = pltpu.make_async_copy(x_any, x_ref, x_sem)
    small = []
    for index, (src, dst) in enumerate(
        ((lengths_any, lengths_ref), (gain_any, gain_ref), (head_any, head_ref), (res_any, res_ref))
    ):
        small.append(pltpu.make_async_copy(src, dst, small_sem.at[index]))

    small[0].start()
    load.start()
    kv_first = col * 2
    loads = []
    for turn, where in enumerate((1 - row, row)):
        for index in range(parts):
            if index == 0:
                begin, ref = (kv_first + where) * chunk, wkv_ref
            else:
                begin, ref = where * GROUP * HD + (index - 1) * chunk, wq_ref
            slot = turn * parts + index
            columns = pl.ds(pl.multiple_of(begin, chunk), chunk)
            loads.append(
                pltpu.make_async_copy(ref.at[0, :, columns], weights.at[slot], w_sem.at[slot])
            )

    barrier = pltpu.get_barrier_semaphore()

    def peer(step):
        return coords((me + step) % count, row_count, cols)

    near = [sibling, over_y, over_x] + [(sec, row, (col + step) % cols) for step in (1, 2, 3)]
    for device in near:
        pl.semaphore_signal(
            barrier, inc=1, device_id=device, device_id_type=pl.DeviceIdType.MESH
        )

    small[0].wait()
    owner = sec * row_count + row
    my_off, my_len, total = 0, 0, 0
    offsets = []
    for index in range(rolls):
        length = lengths_ref[index]
        offsets.append(total)
        total = total + length
        my_off = my_off + jnp.where(index < owner, length, 0)
        my_len = my_len + jnp.where(index == owner, length, 0)

    load.wait()
    limit = x_ref.shape[0]

    def place(begin):
        slots = begin + lax.broadcasted_iota(jnp.int32, (high, limit), 0)
        spots = lax.broadcasted_iota(jnp.int32, (high, limit), 1)
        hit = (slots == my_off + spots) & (spots < my_len)
        rows_here = jnp.dot(
            jnp.where(hit, 1.0, 0.0).astype(jnp.bfloat16), x_ref[...],
            preferred_element_type=jnp.float32,
        )
        return rows_here.astype(jnp.bfloat16).reshape(2, 2, rows, width)

    blocks = tokens // 128

    def squares():
        lines = lax.broadcasted_iota(jnp.int32, (limit, tokens), 1)
        spots = lax.broadcasted_iota(jnp.int32, (limit, tokens), 0)
        hit = (lines == my_off + spots) & (spots < my_len)
        square = jnp.zeros((limit, 128), jnp.float32)
        for group in range(width // 128):
            piece = x_ref[:, group * 128 : (group + 1) * 128].astype(jnp.float32)
            square = square + piece * piece
        moved = jnp.dot(
            jnp.broadcast_to(jnp.sum(jnp.transpose(square), axis=0, keepdims=True), (8, limit)),
            jnp.where(hit, 1.0, 0.0), preferred_element_type=jnp.float32,
            precision=lax.Precision.HIGHEST,
        )
        for block in range(blocks):
            stat[0, block : block + 1] = moved[:1, block * 128 : (block + 1) * 128]

    placed[0] = place(0)
    pl.semaphore_wait(barrier, len(near))

    def to_sib(c):
        return copy(placed.at[c, :, 1 - core], sib.at[c], sib_send, sib_recv.at[c], sibling)

    def to_y(c):
        return copy(comb.at[c, 1 - side], yb.at[c], y_send, y_recv.at[c], over_y)

    def to_x(c):
        return copy(own.at[c], xb.at[c], x_send, x_recv.at[c], over_x)

    def dispatch(c):
        @pl.when(c > 0)
        def _():
            placed[c] = place(c * high)

        to_sib(c).start()

    def reduce_pair(c):
        to_sib(c).wait_recv()
        comb[c] = placed[c, :, core] + sib[c]
        to_y(c).start()

    early = rank <= 1
    mine_half = col % 2

    def z_copy(c, origin, target):
        ref = full.at[c, half(origin), sec]
        return copy(ref, ref, z_send, z_recv.at[c, origin], line(target))

    def fy_copy(c, origin, group):
        ref = full.at[c, half(origin), group]
        return copy(ref, ref, fy_send, fy_recv.at[c], over_y)

    def fs_copy(c, group):
        ref = full.at[c, :, group]
        return copy(ref, ref, fs_send, fs_recv.at[c], sibling)

    def gather_own(c):
        to_y(c).wait_recv()
        own[c] = comb[c, side] + yb[c]

        @pl.when(rank >= 2)
        def _():
            to_x(c).start()

    def land(c):
        @pl.when(early)
        def _():
            to_x(c).wait_recv()
            full[c, mine_half, sec] = own[c] + xb[c]

        @pl.when(rank == 0)
        def _():
            z_copy(c, 0, 1).start()
            fy_copy(c, 0, sec).start()

        @pl.when(rank == 1)
        def _():
            z_copy(c, 1, 2).start()
            z_copy(c, 1, 0).start()
            fy_copy(c, 1, sec).start()

    def pass_on(c, at):
        for origin in (1, 0):
            if at == origin:
                continue
            z_copy(c, origin, origin).wait_recv()
            if at in (1, 2):
                z_copy(c, origin, at + 1).start()
            fy_copy(c, origin, sec).start()
        fs_copy(c, sec).start()

    def to_both(c):
        both = full.at[c, :, across]
        copy(both, both, fy_send, fy_recv.at[c], over_y).wait_recv()
        fs_copy(c, across).start()

    rounds = (sibling, over_y, over_x, near[3 + 1], (sec, row, col + 1 - 2 * (col % 2)))

    def stat_copy(turn):
        return copy(
            stat.at[turn], stats.at[turn], stat_send.at[turn], stat_recv.at[turn], rounds[turn]
        )

    def stat_round(turn):
        if turn:
            stat_copy(turn - 1).wait_recv()
            stat[turn] = stat[turn - 1] + stats[turn - 1]
        else:
            squares()
        stat_copy(turn).start()

    keys[...] = jnp.zeros_like(keys)
    values[...] = jnp.zeros_like(values)

    def ready():
        for one in small[1:]:
            one.wait()
        last = len(rounds) - 1
        stat_copy(last).wait_recv()
        mean = (stat[last] + stats[last]) / (cols * width)
        factor = lax.rsqrt(mean + EPS)
        for block in range(blocks):
            wide = jnp.broadcast_to(factor[block : block + 1], (128, 128))
            scale[block * 128 : (block + 1) * 128] = jnp.transpose(wide)

    def exchange(c):
        return copy(sent.at[c], got.at[c], p_send, p_recv.at[c], over_x)

    def project(c):
        both = full.at[c, :, pl.ds(0, 2)]
        copy(both, both, fs_send, fs_recv.at[c], sibling).wait_recv()
        here = pl.ds(pl.multiple_of(c * high, high), high)
        factor = scale[here, :][:, :1]

        @pl.when(c == 0)
        def _():
            for one in loads:
                one.wait()

        for part_index in range(2):
            piece = full[c, part_index].reshape(high, width).astype(jnp.float32)
            normed[:, part_index * width : (part_index + 1) * width] = (
                piece * factor * gain_ref[row * 2 + part_index]
            ).astype(jnp.bfloat16)
        for index in range(parts):
            sent[c, index] = jnp.dot(
                normed[...], weights[index], preferred_element_type=jnp.float32
            )
        exchange(c).start()
        for index in range(parts):
            mine[c, index] = jnp.dot(
                normed[...], weights[parts + index], preferred_element_type=jnp.float32
            )

        acc[here] = jnp.zeros((high, 128), jnp.float32)

        @pl.when(early)
        def _():
            piece = full[c, mine_half].reshape(high, width).astype(jnp.float32) * res_ref[...]
            lanes = piece[:, :128]
            for group in range(1, width // 128):
                lanes = lanes + piece[:, group * 128 : (group + 1) * 128]
            acc[here] = lanes

    def attend(c):
        exchange(c).wait_recv()

        @pl.when(2 * c < chunks)
        def _():
            attend_to(c, tokens // 2)

        @pl.when(2 * c >= chunks)
        def _():
            attend_to(c, tokens)

    def attend_to(c, end):
        here = pl.ds(pl.multiple_of(c * high, high), high)
        pair = (mine[c, 0] + got[c, 0]).astype(jnp.bfloat16)
        keys[here] = pair[:, :HD]
        values[here] = pair[:, HD:]
        heads = []
        for index in range(1, parts):
            both = (mine[c, index] + got[c, index]).astype(jnp.bfloat16)
            heads += [both[:, :HD], both[:, HD:]]
        query = jnp.concatenate(heads, axis=0)
        logits = lax.dot_general(
            query, keys[:end], (((1,), (1,)), ((), ())), preferred_element_type=jnp.float32
        ) * (1.0 / math.sqrt(HD))
        slots = c * high + lax.broadcasted_iota(jnp.int32, (high, end), 0)
        spots = lax.broadcasted_iota(jnp.int32, (high, end), 1)
        start = jnp.zeros((high, end), jnp.int32)
        for offset in offsets[1:]:
            start = jnp.where(slots >= offset, offset, start)
        allowed = (spots >= start) & (spots <= slots)
        bias = jnp.where(allowed, 0.0, -jnp.inf)
        logits = logits + jnp.concatenate([bias] * len(heads), axis=0)
        expo = jnp.exp(logits - jnp.max(logits, axis=1, keepdims=True))
        probs = (expo / jnp.sum(expo, axis=1, keepdims=True)).astype(jnp.bfloat16)
        attended = jnp.dot(probs, values[:end], preferred_element_type=jnp.float32)
        lanes = acc[here]
        for head in range(len(heads)):
            lanes = lanes + attended[head * high : (head + 1) * high] * head_ref[
                row, :, head * HD : (head + 1) * HD
            ]
        acc[here] = lanes

    lags = (4, 4, 5, 6)
    first = ((dispatch, 0), (reduce_pair, 1), (gather_own, 2), (land, 3))
    later = ((project, 8), (attend, 10))

    def at_lag(k, lag, stage):
        @pl.when((k >= lag) & (k < chunks + lag))
        def _():
            stage(k - lag)

    def publish(begin, end):
        for block in range(begin, end):
            lanes = acc[block * 128 : (block + 1) * 128]
            part[block : block + 1] = jnp.sum(jnp.transpose(lanes), axis=0, keepdims=True)
        span = pl.ds(begin, end - begin)
        for other in range(1, count):
            copy(part.at[span], held.at[me, span], held_send, held_recv, peer(other)).start()

    def step(k, carry):
        for stage, lag in first:
            at_lag(k, lag, stage)
        for turn in range(len(rounds)):
            @pl.when(k == (3, 4, 5, 6, 7)[turn])
            def _():
                stat_round(turn)

        @pl.when(k == 1)
        def _():
            for one in small[1:] + loads:
                one.start()

        for at in range(cols):
            @pl.when(rank == at)
            def _():
                at_lag(k, lags[at], lambda c: pass_on(c, at))
                at_lag(k, lags[at] + 1, to_both)

        pl.when(k == later[0][1])(ready)
        pl.when(k == later[1][1] + chunks - chunks // blocks)(lambda: publish(0, blocks - 1))
        for stage, lag in later:
            at_lag(k, lag, stage)
        return carry

    lax.fori_loop(0, chunks + later[-1][1], step, 0)

    publish(blocks - 1, blocks)
    held[me] = part[...]

    def sent_all(ref, sem):
        copy(ref, ref, sem, sem, sibling).wait_send()

    sent_all(sib, sib_send)
    sent_all(yb, y_send)
    sent_all(comb, fy_send)
    sent_all(placed, fs_send)
    sent_all(sent, p_send)

    @pl.when(rank >= 2)
    def _():
        sent_all(xb, x_send)

    for at in range(3):
        @pl.when(rank == at)
        def _():
            sent_all(full.at[:, 0, pl.ds(0, (1, 3, 2)[at])], z_send)

    for turn in range(len(rounds)):
        stat_copy(turn).wait_send()
    slots = lax.broadcasted_iota(jnp.int32, (tokens, limit), 0)
    spots = lax.broadcasted_iota(jnp.int32, (tokens, limit), 1)
    hit = (slots == my_off + spots) & (spots < my_len)
    picks = jnp.where(hit, 1.0, 0.0).astype(jnp.bfloat16)
    others = held.at[pl.ds(0, count - 1)]
    copy(others, others, held_send, held_recv, sibling).wait()
    totals = []
    for section in range(sections):
        begin = section * row_count * cols
        totals.append(jnp.sum(held[begin : begin + row_count * cols], axis=0))
    home = jnp.concatenate(
        [
            jnp.concatenate([one[block : block + 1] for one in totals], axis=0)
            for block in range(blocks)
        ],
        axis=1,
    )
    result = jnp.zeros((sections, limit), jnp.float32)
    for _ in range(3):
        piece = home.astype(jnp.bfloat16)
        home = home - piece.astype(jnp.float32)
        result = result + jnp.dot(piece, picks, preferred_element_type=jnp.float32)
    out_ref[...] = result


def fused(rollouts, lengths, gain, w_query, w_keyval, out_head, res_head, chunks):
    limit, width = rollouts.shape[1:]
    depth = w_query.shape[1]
    tokens = lengths.shape[0] * limit // 4
    high = tokens // chunks
    rows = high // 4
    vmem = pl.BlockSpec(memory_space=pltpu.VMEM)
    hbm = pl.BlockSpec(memory_space=pltpu.HBM)
    bf16, f32, dma = jnp.bfloat16, jnp.float32, pltpu.SemaphoreType.DMA
    parts = 3
    one, each = (), (chunks,)
    sems = [one, each] * 3 + [one, (chunks, 2)] + [one, each] * 3 + [(5,)] * 2 + [one] * 2
    out = pl.pallas_call(
        functools.partial(fused_kernel, chunks),
        out_shape=jax.ShapeDtypeStruct((4, limit), f32),
        in_specs=[hbm] * 7,
        out_specs=vmem,
        scratch_shapes=[
            pltpu.SMEM(lengths.shape, jnp.int32),
            pltpu.VMEM(gain.shape, f32),
            pltpu.VMEM((2, 1, GROUP * HD), f32),
            pltpu.VMEM(res_head.shape, f32),
            dma((4,)),
            pltpu.VMEM((limit, width), bf16),
            pltpu.VMEM((chunks, 2, 2, rows, width), bf16),
            pltpu.VMEM((chunks, 2, rows, width), bf16),
            pltpu.VMEM((chunks, 2, rows, width), bf16),
            pltpu.VMEM((chunks, rows, width), bf16),
            pltpu.VMEM((chunks, rows, width), bf16),
            pltpu.VMEM((chunks, rows, width), bf16),
            pltpu.VMEM((chunks, 2, 4, rows, width), bf16),
            pltpu.VMEM((high, depth), bf16),
            pltpu.VMEM((2 * parts, depth, 2 * HD), bf16),
            pltpu.VMEM((chunks, parts, high, 2 * HD), f32),
            pltpu.VMEM((chunks, parts, high, 2 * HD), f32),
            pltpu.VMEM((chunks, parts, high, 2 * HD), f32),
            pltpu.VMEM((tokens, HD), bf16),
            pltpu.VMEM((tokens, HD), bf16),
            pltpu.VMEM((tokens, 128), f32),
            pltpu.VMEM((tokens, 128), f32),
            pltpu.VMEM((5, tokens // 128, 128), f32),
            pltpu.VMEM((5, tokens // 128, 128), f32),
            pltpu.VMEM((tokens // 128, 128), f32),
            pltpu.VMEM((32, tokens // 128, 128), f32),
            dma,
            dma((2 * parts,)),
        ]
        + [dma(size) if size else dma for size in sems],
        compiler_params=pltpu.CompilerParams(
            collective_id=3, has_side_effects=True, vmem_limit_bytes=62 * 1024 * 1024
        ),
    )(
        lengths, rollouts.reshape(limit, width), gain, w_query, w_keyval,
        out_head.reshape(2, 1, GROUP * HD), res_head,
    )
    return out.reshape(4, 1, limit)


def plain(half, meansq, gains, w_query, w_keyval, segment, out_head, res_head):
    owners, _, rows, local_width = half.shape
    tokens = owners * rows
    row_count, cols = lax.axis_size("dp"), lax.axis_size("mp")
    my_row, my_col = lax.axis_index("dp"), lax.axis_index("mp")
    slots = jnp.arange(tokens, dtype=jnp.int32)
    scale_row = lax.rsqrt(meansq[:, None, :, :1] + EPS)
    parts = cols // row_count
    gain = lax.dynamic_slice_in_dim(gains, my_row * parts, parts, 0)
    normed = (half.astype(jnp.float32) * scale_row * gain[None]).astype(jnp.bfloat16)

    heads_here = w_query.shape[2] // HD
    kv_here = max(1, heads_here // GROUP)
    kv_first = my_col * heads_here // GROUP
    w_kv = lax.dynamic_slice_in_dim(w_keyval[0], kv_first * 2 * HD, kv_here * 2 * HD, 1)
    q_part, kv_part = 0.0, 0.0
    for part in range(parts):
        rows = normed[:, part].reshape(tokens, local_width)
        begin = part * local_width
        end = begin + local_width
        q_part += jnp.dot(rows, w_query[0, begin:end], preferred_element_type=jnp.float32)
        kv_part += jnp.dot(rows, w_kv[begin:end], preferred_element_type=jnp.float32)
    heads, kvs = heads_here, kv_here
    summed = lax.psum(jnp.concatenate([q_part, kv_part], axis=1), "dp")
    head_cols = out_head[0]
    weight = (my_row == 0).astype(jnp.float32)
    summed = summed.astype(jnp.bfloat16)
    query = summed[:, : heads * HD].reshape(tokens, kvs, heads // kvs, HD)
    keyval = summed[:, heads * HD :].reshape(tokens, kvs, 2, HD)
    logits = jnp.einsum(
        "qkgd,skd->kgqs", query, keyval[:, :, 0, :], preferred_element_type=jnp.float32
    ) * (1.0 / math.sqrt(HD))
    allowed = (segment[:, None] == segment[None, :]) & (slots[None, :] <= slots[:, None])
    logits = jnp.where(allowed, logits, -jnp.inf)
    expo = jnp.exp(logits - jnp.max(logits, axis=-1, keepdims=True))
    probs = (expo / jnp.sum(expo, axis=-1, keepdims=True)).astype(jnp.bfloat16)
    attended = jnp.einsum(
        "kgqs,skd->qkgd", probs, keyval[:, :, 1, :], preferred_element_type=jnp.float32
    ).reshape(tokens, heads * HD)
    inner = my_col - my_row * parts
    res_in = lax.dynamic_index_in_dim(half, jnp.clip(inner, 0, parts - 1), 1, keepdims=False)
    res_sum = jnp.sum(
        res_in.reshape(tokens, local_width).astype(jnp.float32) * res_head[0][None, :], axis=1
    )
    res_sum = jnp.where((inner >= 0) & (inner < parts), res_sum, 0.0)
    return weight * jnp.sum(attended * head_cols[None, :], axis=1) + res_sum


def body(rollouts, lengths, norm_gain, w_query, w_keyval, out_head, res_head):
    roll_count, max_len, local_width = rollouts.shape
    sections, row_count, cols = (lax.axis_size(name) for name in ("section", "dp", "mp"))
    if (sections, row_count, cols, roll_count) == (4, 2, 4, 1) and w_query.shape[2] == 8 * HD:
        gains = norm_gain[0].reshape(cols, 1, local_width)
        return fused(rollouts, lengths, gains, w_query, w_keyval, out_head, res_head, CHUNKS)
    owner = lax.axis_index(OWN)
    total_rolls = lengths.shape[0]
    tokens = total_rolls * max_len // 4

    ids = jnp.arange(total_rolls, dtype=jnp.int32)
    offsets = jnp.sum(jnp.where(ids[None, :] < ids[:, None], lengths[None, :], 0), axis=1)
    slots = jnp.arange(tokens, dtype=jnp.int32)
    segment = jnp.sum((slots[:, None] >= offsets[None, :]).astype(jnp.int32), axis=1)

    position = jnp.arange(max_len, dtype=jnp.int32)
    mine = owner * roll_count + jnp.arange(roll_count, dtype=jnp.int32)
    my_off = jnp.sum(jnp.where(ids[None, :] == mine[:, None], offsets[None, :], 0), axis=1)
    my_len = jnp.sum(jnp.where(ids[None, :] == mine[:, None], lengths[None, :], 0), axis=1)
    place = (
        (slots[:, None, None] == my_off[None, :, None] + position[None, None, :])
        & (position[None, None, :] < my_len[None, :, None])
    ).astype(jnp.bfloat16)
    placed = jnp.dot(
        place.reshape(tokens, roll_count * max_len),
        rollouts.reshape(roll_count * max_len, local_width),
        preferred_element_type=jnp.float32,
    ).astype(jnp.bfloat16)
    half, meansq = spread(placed, sections, row_count, cols)
    heads_here = w_query.shape[2] // HD
    gains = norm_gain[0].reshape(cols, 1, local_width)
    if row_count == 2 and heads_here % (2 * GROUP) == 0 and tokens % 256 == 0:
        lanes = score(
            half, meansq, gains, w_query, w_keyval, segment, out_head, res_head,
            heads_here // 2, heads_here // 2 // GROUP,
        )
        partial = jnp.sum(lanes, axis=1)
    else:
        partial = plain(
            half, meansq, gains, w_query, w_keyval, segment, out_head, res_head
        )
    home = share(partial, sections, row_count, cols)
    home = jnp.pad(home, ((0, 0), (0, max_len)))
    lines = []
    for local in range(roll_count):
        line = lax.dynamic_slice_in_dim(home, my_off[local], max_len, 1)
        lines.append(jnp.where(position[None, :] < my_len[local], line, 0.0))
    return jnp.stack(lines, axis=1)


def solution(mesh):
    in_specs = (
        P(("section", "dp"), None, "mp"),
        P(),
        P("section", None),
        P("section", "dp", "mp"),
        P("section", "dp", None),
        P("section", "mp"),
        P("section", "mp"),
    )
    out_specs = P(None, ("section", "dp"), None)
    return jax.shard_map(body, mesh=mesh, in_specs=in_specs, out_specs=out_specs, check_vma=False)
```
